32 devices in a mesh: dp: 2 (over x), expert: 16 (over z, y, core).
Axes of the slice: x: 2, y: 2, z: 4, core: 2. Of those that a mesh axis runs over, the one named last changes fastest.
Arguments:
- query_nope: bfloat16 [16, 128, 2048], P('expert', None, 'dp'), may hold values from -6 to 6
- query_rope: bfloat16 [16, 128, 1024], P('expert', None, 'dp'), may hold values from -8 to 8
- latent_new: bfloat16 [16, 128, 512], P('expert'), may hold values from -6 to 6
- key_rope: bfloat16 [16, 128, 64], P('expert'), may hold values from -8 to 8
- latent_pages: bfloat16 [16, 8, 64, 512], P('expert', 'dp'), may hold values from -6 to 6
- rope_pages: bfloat16 [16, 8, 4096], P('expert', 'dp'), may hold values from -6 to 6
- page_table: int32 [16, 8], P('expert'), may hold values from 0 to 7, each once within a row
- prefix_lengths: int32 [16], P('expert'), may hold values from 0 to 512, as said below
- residual: bfloat16 [16, 128, 2048], P('expert'), may hold values from -60 to 60
- key_up: bfloat16 [16, 128, 512], P('dp'), may hold values from -0.5 to 0.5
- value_up: bfloat16 [16, 512, 128], P('dp'), may hold values from -0.25 to 0.25
- out_weight: bfloat16 [2048, 2048], P('dp'), may hold values from -0.125 to 0.125
- norm_gain: float32 [2048], replicated, may hold values from 0.1 to 1.9
- expert_in: bfloat16 [16, 1408, 2, 2048], P('expert', 'dp'), may hold values from -0.125 to 0.125
- expert_down: bfloat16 [16, 1408, 2048], P('expert', 'dp'), may hold values from -0.15625 to 0.15625
- expert_ids: int32 [16, 128, 6], P('expert'), may hold values from 0 to 15, all different within a row; in each aligned block of 64 rows (0 to 63, 64 to 127, ..., all dimensions but the last counted through in order) at most 48 rows name the same one
- expert_weights: float32 [16, 128, 6], P('expert'), may hold values from 0.05 to 0.4
Outputs:
- layer_out: bfloat16 [16, 128, 2048], P('expert', 'dp')
- expert_mix: bfloat16 [16, 128, 2048], P('expert', 'dp')
The draws below stay inside these ranges and needn't reach their ends.
Inputs may be any that keep to these rules, and one draw needn't show every extreme that they name: `prefix_lengths`: some request's prefix fills all of its 8 page slots. `page_table`: each row names every page slot of its request once; entry j holds positions j * 64 to (j + 1) * 64 - 1. `expert_ids`: each row names 6 distinct experts; in each aligned block of 64 rows of a request (blocks along the first two dimensions taken together) no expert is named more than 48 times, and that many is reached.
All inputs are finite; a program needn't handle non-finite values.
Results may differ from the reference program's by a relative error of at most 0.019.
Values may be sent and summed in bfloat16 or wider, within the bound.
A program may use at most 128 MiB of HBM per device.

```python
import math
import jax
import jax.numpy as jnp
import numpy as np
from jax import lax

D = 2048
H = 16
HD = 128
RD = 64
LAT = 512
FFE = 1408
TOP = 6
PAGE = 64
T_COL = 128
EXPERTS = 16
REQS = 16
PAGES = 8
HSPLIT = 2
QROWS = 64
CAPQ = 48


def rope_pair(key):
    base_k = jnp.clip(jax.random.normal(jax.random.fold_in(key, 11), (REQS, T_COL, RD), jnp.float32), -6.0, 6.0)
    base_q = jnp.clip(jax.random.normal(jax.random.fold_in(key, 12), (REQS, T_COL, H * RD), jnp.float32), -6.0, 6.0)
    return (base_q, base_k)


def draw_query_rope(key, part):
    return rope_pair(key)[0].astype(jnp.bfloat16)


def draw_key_rope(key, part):
    return rope_pair(key)[1].astype(jnp.bfloat16)


def draw_residual(key, part):
    low = math.log(0.3)
    high = math.log(3.0)
    row_scale = jnp.exp(jax.random.uniform(jax.random.fold_in(key, 31), (REQS, T_COL, 1), jnp.float32, low, high))
    col_scale = jnp.exp(jax.random.uniform(jax.random.fold_in(key, 32), (1, 1, D), jnp.float32, low, high))
    base = jnp.clip(jax.random.normal(jax.random.fold_in(key, 33), (REQS, T_COL, D), jnp.float32), -5.0, 5.0)
    return (base * row_scale * col_scale).astype(jnp.bfloat16)


def draw_prefix_lengths(key, part):
    lengths = jax.random.randint(jax.random.fold_in(key, 21), (REQS,), 0, PAGES * PAGE + 1)
    full = jax.random.randint(jax.random.fold_in(key, 22), (), 0, REQS)
    return jnp.where(jnp.arange(REQS) == full, PAGES * PAGE, lengths).astype(jnp.int32)


def block_levels(key, extent, split, low, high):
    loudness = 1.0
    for dim, shards_of in split:
        draws = jax.random.uniform(jax.random.fold_in(jax.random.fold_in(key, 6), dim), (shards_of,), jnp.float32, low / len(split), high / len(split))
        loudness = loudness * jnp.repeat(jnp.exp(draws), extent[dim] // shards_of).reshape((-1,) + (1,) * (len(extent) - 1 - dim))
    return loudness


def deal_out(stream_key, own, number, rows, count, top, most, slope):
    sequence = jax.random.permutation(stream_key, count)
    crowded, usual = load_shares(count, rows * top, most, slope, True), load_shares(count, rows * top, most, slope, False)
    places = jnp.arange(count)

    def named(tallies, rotation):
        used = int((tallies > 0).sum())
        fixed = max(1, used // 4)
        moved = fixed + (places - fixed + rotation * (used - fixed)) % max(1, count - fixed)
        return jnp.zeros((count,), jnp.int32).at[sequence[jnp.where(places < fixed, places, moved)]].set(jnp.asarray(tallies, jnp.int32))

    tallies = jnp.where(number % 4 == 0, named(crowded, number // 4), named(usual, number - number // 4 - 1))
    mixed = jax.random.permutation(jax.random.fold_in(own, 3), count)
    giver, taker = mixed[0:count // 2 * 2:2], mixed[1:count // 2 * 2:2]
    room = jnp.minimum(tallies[giver] - 1, most - tallies[taker]) // 2
    room = jnp.where((giver == sequence[0]) | (taker == sequence[0]) | (tallies[taker] == 0), 0, jnp.maximum(room, 0))
    moved = jax.random.randint(jax.random.fold_in(own, 4), (count // 2,), 0, 1 << 20) % (room + 1)
    tallies = tallies.at[giver].add(-moved).at[taker].add(moved)
    members = jnp.searchsorted(jnp.cumsum(tallies), jnp.arange(rows * top), side="right").astype(jnp.int32)
    grid = members.reshape(top, rows).T
    grid = grid[jax.random.permutation(jax.random.fold_in(own, 1), rows)]
    rotation = jax.random.randint(jax.random.fold_in(own, 2), (rows, 1), 0, top)
    return jnp.take_along_axis(grid, (jnp.arange(top)[None, :] + rotation) % top, axis=1)


def load_shares(count, total, bound, slope, full):
    loads = [(1 << 20) // math.isqrt(grade ** slope) + 1 for grade in range(1, count + 1)]
    largest = bound if full else min(bound, max(-(-total // count), total * loads[0] // sum(loads)))
    least = 1 if total - largest >= count - 1 else 0
    counts, surplus = [largest] + [least] * (count - 1), total - largest - least * (count - 1)
    while surplus > 0:
        free = [i for i in range(1, count) if counts[i] < largest] or [i for i in range(1, count) if counts[i] < bound]
        whole, budget = sum([loads[i] for i in free]), surplus
        for i in free:
            addition = min(bound - counts[i], max(1, budget * loads[i] // whole), surplus)
            counts[i] = counts[i] + addition
            surplus = surplus - addition
    return np.array(counts)


def scatter_about(key, dims, spread, bound, pieces=(), held_as=jnp.bfloat16):
    array = jax.random.normal(key, dims, jnp.float32) * spread
    if len(pieces) > 0:
        array = block_levels(key, dims, pieces, -0.22, 0.18) * array
    return jnp.clip(array, min=-bound, max=bound).astype(held_as)


def setup_inputs(seed: int = 0) -> dict:
    streams_of = jax.random.split(jax.random.key(seed), 18)
    query_nope = scatter_about(streams_of[0], (REQS, T_COL, H * HD), 1.0, 6.0, ((0, 16), (2, 2)))
    query_rope = draw_query_rope(jax.random.fold_in(streams_of[17], 71), 0)
    latent_new = scatter_about(streams_of[2], (REQS, T_COL, LAT), 1.0, 6.0, ((0, 16),))
    key_rope = draw_key_rope(jax.random.fold_in(streams_of[17], 71), 0)
    latent_pages = scatter_about(streams_of[4], (REQS, PAGES, PAGE, LAT), 1.0, 6.0, ((0, 16), (1, 2)))
    rope_pages = scatter_about(streams_of[5], (REQS, PAGES, PAGE * RD), 1.0, 6.0, ((0, 16), (1, 2)))
    page_table = jax.vmap(lambda own: jax.random.permutation(own, PAGES))(jax.random.split(streams_of[6], REQS)).reshape((REQS, PAGES)).astype(jnp.int32)
    prefix_lengths = draw_prefix_lengths(jax.random.fold_in(streams_of[17], 71), 0)
    residual = draw_residual(jax.random.fold_in(streams_of[17], 71), 0)
    key_up = scatter_about(streams_of[9], (H, HD, LAT), HD ** -0.5, 0.5, ((0, 2),))
    value_up = scatter_about(streams_of[10], (H, LAT, HD), LAT ** -0.5, 0.25, ((0, 2),))
    out_weight = scatter_about(streams_of[11], (H * HD, D), (H * HD) ** -0.5, 0.125, ((0, 2),))
    norm_gain = jnp.clip(1.0 + 0.18 * jax.random.normal(streams_of[12], (D,), jnp.float32), 0.1, 1.9)
    expert_in = scatter_about(streams_of[13], (EXPERTS, FFE, 2, D), D ** -0.5, 0.125, ((0, 16), (1, 2)))
    expert_down = scatter_about(streams_of[14], (EXPERTS, FFE, D), FFE ** -0.5, 0.15625, ((0, 16), (1, 2)))
    expert_ids_keys = jax.random.split(jax.random.fold_in(streams_of[15], 1), REQS * T_COL // QROWS)
    expert_ids_turns = jax.random.permutation(jax.random.fold_in(streams_of[15], 3), REQS * T_COL // QROWS)
    expert_ids = jax.vmap(lambda own, number: deal_out(jax.random.fold_in(streams_of[15], 2), own, number, QROWS, EXPERTS, TOP, CAPQ, 2))(expert_ids_keys, expert_ids_turns).reshape((REQS, T_COL, TOP))
    expert_weights = jnp.clip(0.05 + 0.35 * jax.random.uniform(streams_of[16], (REQS, T_COL, TOP), jnp.float32) ** block_levels(streams_of[16], (REQS, T_COL, TOP), ((0, 16),), -0.2, 0.2), 0.05, 0.4)
    return {"query_nope": query_nope, "query_rope": query_rope, "latent_new": latent_new, "key_rope": key_rope, "latent_pages": latent_pages, "rope_pages": rope_pages, "page_table": page_table, "prefix_lengths": prefix_lengths, "residual": residual, "key_up": key_up, "value_up": value_up, "out_weight": out_weight, "norm_gain": norm_gain, "expert_in": expert_in, "expert_down": expert_down, "expert_ids": expert_ids, "expert_weights": expert_weights}


EPS = 1e-06
NEG = -1e+30

def rounded(value):
    return lax.optimization_barrier(value.astype(jnp.bfloat16)).astype(jnp.float32)

def reference(query_nope, query_rope, latent_new, key_rope, latent_pages, rope_pages, page_table, prefix_lengths, residual, key_up, value_up, out_weight, norm_gain, expert_in, expert_down, expert_ids, expert_weights):
    scale = 1.0 / (HD + RD) ** 0.5
    key_up_f = key_up.astype(jnp.float32)
    value_up_f = value_up.astype(jnp.float32)

    def attend(items):
        nope_rows, rope_rows, latent_rows, krope_rows, page_lat, page_rope, table, length, resid_rows = items
        heads_nope = nope_rows.reshape(T_COL, H, HD).astype(jnp.float32)
        query_lat = rounded(jnp.einsum('thd,hdc->thc', heads_nope, key_up_f))
        ordered_lat = page_lat[table].reshape(PAGES * PAGE, LAT)
        ordered_rope = page_rope[table].reshape(PAGES * PAGE, RD)
        keys_lat = jnp.concatenate([ordered_lat, latent_rows], axis=0).astype(jnp.float32)
        keys_rope = jnp.concatenate([ordered_rope, krope_rows], axis=0).astype(jnp.float32)
        heads_rope = rope_rows.reshape(T_COL, H, RD).astype(jnp.float32)
        scores = (jnp.einsum('thc,kc->thk', query_lat, keys_lat) + jnp.einsum('thr,kr->thk', heads_rope, keys_rope)) * scale
        prefix_ok = jnp.arange(PAGES * PAGE) < length
        causal = jnp.arange(T_COL)[None, :] <= jnp.arange(T_COL)[:, None]
        allowed = jnp.concatenate([jnp.broadcast_to(prefix_ok[None, :], (T_COL, PAGES * PAGE)), causal], axis=1)[:, None, :]
        masked = jnp.where(allowed, scores, NEG)
        peak = lax.optimization_barrier(jnp.max(masked, axis=-1, keepdims=True))
        expo = jnp.where(allowed, jnp.exp(masked - peak), 0.0)
        total = lax.optimization_barrier(jnp.sum(expo, axis=-1, keepdims=True))
        probs = rounded(expo)
        attn_latent = rounded(jnp.einsum('thk,kc->thc', probs, keys_lat) / total)
        heads_out = jnp.einsum('thc,hcd->thd', attn_latent, value_up_f).astype(jnp.bfloat16)
        attn = jnp.dot(heads_out.reshape(T_COL, H * HD), out_weight, preferred_element_type=jnp.float32)
        return resid_rows.astype(jnp.float32) + attn
    hidden = lax.map(attend, (query_nope, query_rope, latent_new, key_rope, latent_pages, rope_pages, page_table, prefix_lengths, residual))
    rows = REQS * T_COL
    flat_hidden = hidden.reshape(rows, D)
    power = lax.optimization_barrier(jnp.mean(flat_hidden * flat_hidden, axis=-1, keepdims=True))
    normed = (flat_hidden * lax.rsqrt(power + EPS) * norm_gain).astype(jnp.bfloat16)
    flat_ids = expert_ids.reshape(rows * TOP)
    flat_gates = expert_weights.reshape(rows * TOP)
    onehot = (flat_ids[:, None] == jnp.arange(EXPERTS)[None, :]).astype(jnp.int32)
    before = jnp.cumsum(onehot, axis=0) - onehot
    rank = lax.optimization_barrier(jnp.sum(before * onehot, axis=1)).astype(jnp.int32)
    capacity = REQS * HSPLIT * CAPQ
    group_width = FFE // HSPLIT
    source_row = (jnp.arange(rows * TOP) // TOP).astype(jnp.int32)

    def add_expert(mixture, expert):
        chosen = flat_ids == expert
        slot = jnp.where(chosen, rank, capacity).astype(jnp.int32)
        row_of = jnp.zeros((capacity,), jnp.int32).at[slot].set(source_row, mode='drop')
        gate_of = jnp.zeros((capacity,), jnp.float32).at[slot].set(flat_gates, mode='drop')
        picked = normed[row_of]
        rows_in = expert_in[expert]
        rows_down = expert_down[expert]
        result = jnp.zeros((capacity, D), jnp.float32)
        for group in range(HSPLIT):
            lower = group * group_width
            upper = lower + group_width
            gate_act = jnp.dot(picked, rows_in[lower:upper, 0, :].T, preferred_element_type=jnp.float32)
            up_act = jnp.dot(picked, rows_in[lower:upper, 1, :].T, preferred_element_type=jnp.float32)
            units = (jax.nn.silu(gate_act) * up_act).astype(jnp.bfloat16)
            part = jnp.dot(units, rows_down[lower:upper], preferred_element_type=jnp.float32).astype(jnp.bfloat16)
            result = result + part.astype(jnp.float32)
        mixture = mixture.at[row_of].add(result * gate_of[:, None])
        return (mixture, None)
    mixture, unused = lax.scan(add_expert, jnp.zeros((rows, D), jnp.float32), jnp.arange(EXPERTS))
    layer_out = (flat_hidden + mixture).astype(jnp.bfloat16).reshape(REQS, T_COL, D)
    expert_mix = mixture.astype(jnp.bfloat16).reshape(REQS, T_COL, D)
    return (layer_out, expert_mix)
```

```python
import functools

import jax
import jax.numpy as jnp
from jax import lax
from jax.experimental import pallas as pl
from jax.experimental.pallas import tpu as pltpu
from jax.sharding import PartitionSpec as P

HD = 128
RD = 64
LAT = 512
TOP = 6
PAGE = 64


EPS = 1e-06
NEG = -1e30


def norm_rows(hidden, norm_gain):
    power = jnp.mean(hidden * hidden, axis=-1, keepdims=True)
    return (hidden * lax.rsqrt(power + EPS) * norm_gain).astype(jnp.bfloat16)


def expert_apply(tokens, gate, expert_in, expert_down):
    flat = tokens.reshape(-1, tokens.shape[-1])
    dims = (((1,), (1,)), ((), ()))
    gate_act = lax.dot_general(
        flat, expert_in[0, :, 0, :], dims, preferred_element_type=jnp.float32
    )
    up_act = lax.dot_general(flat, expert_in[0, :, 1, :], dims, preferred_element_type=jnp.float32)
    units = (jax.nn.silu(gate_act) * up_act).astype(jnp.bfloat16)
    part = jnp.dot(units, expert_down[0], preferred_element_type=jnp.float32)
    return (part * gate).astype(jnp.bfloat16)


def moe_kernel(
    sent_ref,
    w_in_ref,
    w_down_ref,
    out_ref,
    tok,
    w_in,
    w_down,
    units,
    gate,
    part,
    core_in,
    acc,
    diag_x,
    diag_y,
    from_x,
    from_y,
    z_send,
    z_up,
    z_down,
    w_sems,
    g_sends,
    g_recvs,
    sends,
    recvs,
):
    x = lax.axis_index("dp")
    e = lax.axis_index("expert")
    z, y, c = e // 4, (e // 2) % 2, e % 2
    rows, model = out_ref.shape
    half = rows // 2
    width = w_down_ref.shape[0]
    high = z // 2
    low_z = z + high * (3 - 2 * z)
    mid = low_z == 1

    def flip(f):
        return f + high * (3 - 2 * f)

    planes = [z, flip(1 - low_z), flip(3 + 0 * z), flip(2 + 0 * z)]
    other_core = {"expert": e + 1 - 2 * c}
    other_y = {"expert": e + 2 - 4 * y}
    other_x = {"dp": 1 - x}
    above, below = {"expert": e + 4}, {"expert": e - 4}
    first, second = pl.ds(0, half), pl.ds(half, half)

    def remote(src, dst, send, recv, to):
        return pltpu.make_async_remote_copy(
            src_ref=src,
            dst_ref=dst,
            send_sem=send,
            recv_sem=recv,
            device_id=to,
            device_id_type=pl.DeviceIdType.MESH,
        )

    def same(ref, kind, p, to):
        return remote(ref, ref, g_sends.at[kind, p], g_recvs.at[kind, p], to)

    def g_up(p):
        return same(tok.at[p, y, c, x], 0, p, above)

    def g_down(p):
        return same(tok.at[p, y, c, x], 1, p, below)

    def g_x(p, i):
        return same(tok.at[p, y, c, i], 2, p, other_x)

    def g_y(p, j):
        return same(tok.at[p, j, c, x], 3, p, other_y)

    def g_diag_x(p, j):
        return same(tok.at[p, j, c, x, first], 4, p, other_x)

    def g_diag_y(p, i):
        return same(tok.at[p, y, c, i, second], 5, p, other_y)

    def g_core_kind(p, kind, cc):
        j, i = (y, y, 1 - y, 1 - y)[kind], (x, 1 - x, x, 1 - x)[kind]
        return same(tok.at[p, j, cc, i], 6 + kind, p, other_core)

    def own_line(p):
        g_x(p, x).start()
        g_y(p, y).start()
        g_core_kind(p, 0, c).start()

    def along_z(p):
        @pl.when(p < z)
        def _():
            g_up(p).wait_recv()

            @pl.when(z < 3)
            def _():
                g_up(p).start()

        @pl.when(p > z)
        def _():
            g_down(p).wait_recv()

            @pl.when(z > 0)
            def _():
                g_down(p).start()

    def beside(p):
        g_x(p, 1 - x).wait_recv()
        g_diag_y(p, 1 - x).start()
        g_core_kind(p, 1, c).start()
        g_y(p, 1 - y).wait_recv()
        g_diag_x(p, 1 - y).start()
        g_core_kind(p, 2, c).start()

    def across(p):
        same(tok.at[p, 1 - y, c, 1 - x, first], 4, p, other_x).wait_recv()
        same(tok.at[p, 1 - y, c, 1 - x, second], 5, p, other_y).wait_recv()
        g_core_kind(p, 3, c).start()

    def whole(p):
        for kind in range(4):
            g_core_kind(p, kind, 1 - c).wait_recv()

    def tokens(p):
        return tok[p, :, :, :, :, pl.ds(0, model)].reshape(8 * rows, model)

    def hidden(p, lo, n):
        dims = (((1,), (1,)), ((), ()))
        values = tokens(p)
        gate_act = lax.dot_general(
            values, w_in[0, pl.ds(lo, n)], dims, preferred_element_type=jnp.float32
        )
        up_act = lax.dot_general(
            values, w_in[1, pl.ds(lo, n)], dims, preferred_element_type=jnp.float32
        )
        units[:, pl.ds(lo, n)] = (gate_act / (1.0 + jnp.exp(-gate_act)) * up_act).astype(
            units.dtype
        )

    def gates(p):
        extra = tok.shape[5] - model
        lanes = lax.broadcasted_iota(jnp.int32, (8 * rows, extra), 1)
        named = (lanes == e) | (lanes == e + lax.axis_size("expert"))
        values = tok[p, :, :, :, :, pl.ds(model, extra)].reshape(8 * rows, extra)
        gate[...] = jnp.sum(
            jnp.where(named, values.astype(jnp.float32), 0.0), axis=1, keepdims=True
        )

    def project(p, lo, n):
        value = jnp.dot(units[...], w_down[:, pl.ds(lo, n)], preferred_element_type=jnp.float32)
        part[p, :, :, :, :, pl.ds(lo, n)] = (
            (value * gate[...]).astype(part.dtype).reshape(2, 2, 2, rows, n)
        )

    def compute(p, between):
        steps = [functools.partial(hidden, p, lo, min(256, width - lo)) for lo in range(0, width, 256)]
        steps += [functools.partial(gates, p)]
        steps += [functools.partial(project, p, lo, 256) for lo in range(0, model, 256)]
        for number, step in enumerate(steps):
            step()
            for act in between.get(number, ()):
                act()

    def copy(src, dst, kind, k, to):
        return remote(src, dst, sends.at[kind, k], recvs.at[kind, k], to)

    def core_copy(k):
        return copy(part.at[planes[k], :, 1 - c], core_in.at[k], 0, k, other_core)

    def diag_y_copy(k):
        return copy(acc.at[k, 1 - y, 1 - x, first], diag_y.at[k], 1, k, other_y)

    def diag_x_copy(k):
        return copy(acc.at[k, 1 - y, 1 - x, second], diag_x.at[k], 2, k, other_x)

    def x_copy(k):
        return copy(acc.at[k, y, 1 - x], from_x.at[k], 3, k, other_x)

    def y_copy(k):
        return copy(acc.at[k, 1 - y, x], from_y.at[k], 4, k, other_y)

    def up_copy(g):
        return copy(z_send.at[g], z_up.at[g], 5, g, above)

    def down_copy(g):
        return copy(z_send.at[g], z_down.at[g], 6, g, below)

    def wide(value):
        return value.astype(jnp.float32)

    def stage_a(k):
        core_copy(k).wait_recv()
        for j in (0, 1):
            for i in (0, 1):
                acc[k, j, i] = (wide(part[planes[k], j, c, i]) + wide(core_in[k, j, i])).astype(
                    acc.dtype
                )
        diag_y_copy(k).start()
        diag_x_copy(k).start()

    def stage_b(k):
        diag_y_copy(k).wait_recv()
        acc[k, y, 1 - x, first] = (wide(acc[k, y, 1 - x, first]) + wide(diag_y[k])).astype(acc.dtype)
        x_copy(k).start()
        diag_x_copy(k).wait_recv()
        acc[k, 1 - y, x, second] = (wide(acc[k, 1 - y, x, second]) + wide(diag_x[k])).astype(
            acc.dtype
        )
        y_copy(k).start()

    def stage_c(k, g, last=False):
        x_copy(k).wait_recv()
        y_copy(k).wait_recv()
        out_ref[...] = wide(acc[k, y, x]) + wide(from_x[k]) + wide(from_y[k])

        @pl.when((g >= z) & (z > 0))
        def _():
            up_copy(g).wait_recv()
            out_ref[...] += wide(z_up[g])

        @pl.when((g <= z) & (z < 3))
        def _():
            down_copy(g).wait_recv()
            out_ref[...] += wide(z_down[g])

        if not last:
            z_send[g] = out_ref[...].astype(z_send.dtype)

            @pl.when(g > z)
            def _():
                up_copy(g).start()

            @pl.when(g < z)
            def _():
                down_copy(g).start()

    load_in = pltpu.make_async_copy(w_in_ref, w_in, w_sems.at[0])
    load_down = pltpu.make_async_copy(w_down_ref, w_down, w_sems.at[1])
    barrier = pltpu.get_barrier_semaphore()
    for to in (other_core, other_x, other_y):
        pl.semaphore_signal(barrier, inc=1, device_id=to, device_id_type=pl.DeviceIdType.MESH)

    @pl.when(z > 0)
    def _():
        pl.semaphore_signal(barrier, inc=1, device_id=below, device_id_type=pl.DeviceIdType.MESH)

    @pl.when(z < 3)
    def _():
        pl.semaphore_signal(barrier, inc=1, device_id=above, device_id_type=pl.DeviceIdType.MESH)

    load_in.start()
    load_down.start()
    tok[z, y, c, x] = sent_ref[...]
    pl.semaphore_wait(barrier, 4 + ((z + 1) // 2) % 2)

    @pl.when(z < 3)
    def _():
        g_up(z).start()

    @pl.when(z > 0)
    def _():
        g_down(z).start()

    own_line(z)
    along_z(planes[1])
    own_line(planes[1])

    @pl.when(mid)
    def _():
        along_z(planes[3])

    beside(planes[0])
    across(planes[0])
    load_in.wait()
    load_down.wait()
    whole(planes[0])

    def far_mid():
        @pl.when(mid)
        def _():
            along_z(planes[2])

    def far_end():
        @pl.when(low_z == 0)
        def _():
            along_z(planes[3])
            along_z(planes[2])

    def do(f, *args):
        return functools.partial(f, *args)

    def start_core(k):
        core_copy(k).start()

    compute(planes[0], {1: [far_mid], 3: [do(beside, planes[1])]})
    far_end()
    own_line(planes[2])
    own_line(planes[3])
    across(planes[1])
    whole(planes[1])
    compute(planes[1], {3: [do(beside, planes[2])]})
    start_core(1)
    across(planes[2])
    whole(planes[2])
    compute(planes[2], {0: [do(stage_a, 1)], 3: [do(beside, planes[3])], 10: [do(stage_b, 1)]})
    start_core(2)
    across(planes[3])
    whole(planes[3])
    compute(planes[3], {0: [do(stage_a, 2)], 10: [do(stage_b, 2)]})
    start_core(3)
    start_core(0)
    early = jnp.where(mid, 2, 1)
    late = 3 - early
    stage_a(3)
    stage_c(early, jnp.where(mid, planes[2], planes[1]))
    stage_a(0)
    stage_b(3)
    stage_c(late, jnp.where(mid, planes[1], planes[2]))
    stage_b(0)
    stage_c(3, planes[3])
    stage_c(0, planes[0], True)

    for k in range(4):
        p = planes[k]
        for made in (core_copy, diag_y_copy, diag_x_copy, x_copy, y_copy):
            made(k).wait_send()
        g_x(p, x).wait_send()
        g_y(p, y).wait_send()
        g_diag_y(p, 1 - x).wait_send()
        g_diag_x(p, 1 - y).wait_send()
        for kind in range(4):
            g_core_kind(p, kind, c).wait_send()

        @pl.when((p <= z) & (z < 3))
        def _():
            g_up(p).wait_send()

        @pl.when((p >= z) & (z > 0))
        def _():
            g_down(p).wait_send()

        if k > 0:

            @pl.when(p > z)
            def _():
                up_copy(p).wait_send()

            @pl.when(p < z)
            def _():
                down_copy(p).wait_send()


def mixture_kernel(sent, w_in, w_down):
    rows, full = sent.shape
    width, model = w_down.shape
    kind = sent.dtype
    line = pltpu.VMEM((4, rows, model), kind)
    halves = pltpu.VMEM((4, rows // 2, model), kind)
    return pl.pallas_call(
        moe_kernel,
        out_shape=jax.ShapeDtypeStruct((rows, model), jnp.float32),
        in_specs=[
            pl.BlockSpec(memory_space=pltpu.VMEM),
            pl.BlockSpec(memory_space=pl.ANY),
            pl.BlockSpec(memory_space=pl.ANY),
        ],
        out_specs=pl.BlockSpec(memory_space=pltpu.VMEM),
        scratch_shapes=[
            pltpu.VMEM((4, 2, 2, 2, rows, full), kind),
            pltpu.VMEM((2, width, model), kind),
            pltpu.VMEM((width, model), kind),
            pltpu.VMEM((8 * rows, width), kind),
            pltpu.VMEM((8 * rows, 1), jnp.float32),
            pltpu.VMEM((4, 2, 2, 2, rows, model), kind),
            pltpu.VMEM((4, 2, 2, rows, model), kind),
            pltpu.VMEM((4, 2, 2, rows, model), kind),
            halves,
            halves,
            line,
            line,
            line,
            line,
            line,
            pltpu.SemaphoreType.DMA((2,)),
            pltpu.SemaphoreType.DMA((10, 4)),
            pltpu.SemaphoreType.DMA((10, 4)),
            pltpu.SemaphoreType.DMA((7, 4)),
            pltpu.SemaphoreType.DMA((7, 4)),
        ],
        compiler_params=pltpu.CompilerParams(
            collective_id=0, has_side_effects=True, vmem_limit_bytes=58 * 2**20
        ),
    )(sent, w_in, w_down)


def per_device(
    query_nope,
    query_rope,
    latent_new,
    key_rope,
    latent_pages,
    rope_pages,
    page_table,
    prefix_lengths,
    residual,
    key_up,
    value_up,
    out_weight,
    norm_gain,
    expert_in,
    expert_down,
    expert_ids,
    expert_weights,
):
    groups = lax.axis_size("dp")
    experts_all = lax.axis_size("expert") * expert_in.shape[0]
    tokens_col = query_nope.shape[1]
    block_rows = tokens_col // groups
    heads_here = key_up.shape[0]
    pages_lat, pages_rope = (
        lax.all_gather(latent_pages[0], "dp", axis=0, tiled=True),
        lax.all_gather(rope_pages[0], "dp", axis=0, tiled=True),
    )
    page_count = pages_lat.shape[0]
    table = page_table[0]
    inverse = jnp.sum(
        jnp.where(
            table[:, None] == jnp.arange(page_count)[None, :], jnp.arange(page_count)[:, None], 0
        ),
        axis=0,
    )
    positions = (inverse[:, None] * PAGE + jnp.arange(PAGE)[None, :]).reshape(-1)
    prefix_ok = positions < prefix_lengths[0]
    keys_lat = jnp.concatenate([pages_lat.reshape(-1, LAT), latent_new[0]], axis=0)
    keys_rope = jnp.concatenate([pages_rope.reshape(-1, RD), key_rope[0]], axis=0)
    heads_nope = query_nope[0].reshape(tokens_col, heads_here, HD)
    query_lat = jnp.einsum(
        "thd,hdc->thc", heads_nope, key_up, preferred_element_type=jnp.float32
    ).astype(jnp.bfloat16)
    heads_rope = query_rope[0].reshape(tokens_col, heads_here, RD)
    scale = 1.0 / (HD + RD) ** 0.5
    scores = (
        jnp.einsum("thc,kc->thk", query_lat, keys_lat, preferred_element_type=jnp.float32)
        + jnp.einsum("thr,kr->thk", heads_rope, keys_rope, preferred_element_type=jnp.float32)
    ) * scale
    causal = jnp.arange(tokens_col)[None, :] <= jnp.arange(tokens_col)[:, None]
    allowed = jnp.concatenate(
        [jnp.broadcast_to(prefix_ok[None, :], (tokens_col, prefix_ok.shape[0])), causal], axis=1
    )[:, None, :]
    masked = jnp.where(allowed, scores, NEG)
    peak = jnp.max(masked, axis=-1, keepdims=True)
    expo = jnp.where(allowed, jnp.exp(masked - peak), 0.0)
    total = jnp.sum(expo, axis=-1, keepdims=True)
    probs = expo.astype(jnp.bfloat16)
    attn_latent = (
        jnp.einsum("thk,kc->thc", probs, keys_lat, preferred_element_type=jnp.float32) / total
    ).astype(jnp.bfloat16)
    heads_out = jnp.einsum(
        "thc,hcd->thd", attn_latent, value_up, preferred_element_type=jnp.float32
    ).astype(jnp.bfloat16)
    partial_out = jnp.dot(
        heads_out.reshape(tokens_col, heads_here * HD),
        out_weight,
        preferred_element_type=jnp.float32,
    )
    attended = lax.psum_scatter(
        partial_out.astype(jnp.bfloat16), "dp", scatter_dimension=0, tiled=True
    ).astype(jnp.float32)
    start = lax.axis_index("dp") * block_rows
    hidden_mine = (
        lax.dynamic_slice_in_dim(residual[0], start, block_rows, 0).astype(jnp.float32) + attended
    )
    normed = norm_rows(hidden_mine, norm_gain)
    ids_mine = lax.dynamic_slice_in_dim(expert_ids[0], start, block_rows, 0)
    weights_mine = lax.dynamic_slice_in_dim(expert_weights[0], start, block_rows, 0)
    gates = jnp.sum(
        jnp.where(
            ids_mine[:, :, None] == jnp.arange(experts_all)[None, None, :],
            weights_mine[:, :, None],
            0.0,
        ),
        axis=1,
    )
    gates_high = gates.astype(jnp.bfloat16)
    gates_low = (gates - gates_high.astype(jnp.float32)).astype(jnp.bfloat16)
    model = normed.shape[1]
    extra = -(-2 * experts_all // 128) * 128
    fill = jnp.zeros((block_rows, extra - 2 * experts_all), jnp.bfloat16)
    sent = jnp.concatenate([normed, gates_high, gates_low, fill], axis=1)
    if groups == 2 and lax.axis_size("expert") == 16:
        mixture = mixture_kernel(sent, jnp.transpose(expert_in[0], (1, 0, 2)), expert_down[0])
    else:
        gathered = lax.all_gather(sent, ("expert", "dp"), axis=0, tiled=True)
        everyone = gathered[:, :model]
        mine = lax.axis_index("expert")
        named = (jnp.arange(extra) == mine) | (jnp.arange(extra) == mine + experts_all)
        gate = jnp.sum(
            jnp.where(named[None, :], gathered[:, model:].astype(jnp.float32), 0.0),
            axis=1,
            keepdims=True,
        )
        part = expert_apply(everyone, gate, expert_in, expert_down)
        mixture = lax.psum_scatter(
            part, ("expert", "dp"), scatter_dimension=0, tiled=True
        ).astype(jnp.float32)
    layer_out = (hidden_mine + mixture).astype(jnp.bfloat16)[None]
    return (layer_out, mixture.astype(jnp.bfloat16)[None])


def solution(mesh):
    return jax.shard_map(
        per_device,
        mesh=mesh,
        in_specs=(
            P("expert", None, "dp"),
            P("expert", None, "dp"),
            P("expert", None, None),
            P("expert", None, None),
            P("expert", "dp", None, None),
            P("expert", "dp", None),
            P("expert", None),
            P("expert"),
            P("expert", None, None),
            P("dp", None, None),
            P("dp", None, None),
            P("dp", None),
            P(),
            P("expert", "dp", None, None),
            P("expert", "dp", None),
            P("expert", None, None),
            P("expert", None, None),
        ),
        out_specs=(P("expert", "dp", None), P("expert", "dp", None)),
        check_vma=False,
    )
```

```python
import functools

import jax
import jax.numpy as jnp
from jax import lax
from jax.experimental import pallas as pl
from jax.experimental.pallas import tpu as pltpu
from jax.sharding import PartitionSpec as P

HD = 128
RD = 64
LAT = 512
TOP = 6
PAGE = 64


EPS = 1e-06
NEG = -1e30


def norm_rows(hidden, norm_gain):
    power = jnp.mean(hidden * hidden, axis=-1, keepdims=True)
    return (hidden * lax.rsqrt(power + EPS) * norm_gain).astype(jnp.bfloat16)


def expert_apply(tokens, gate, expert_in, expert_down):
    flat = tokens.reshape(-1, tokens.shape[-1])
    dims = (((1,), (1,)), ((), ()))
    gate_act = lax.dot_general(
        flat, expert_in[0, :, 0, :], dims, preferred_element_type=jnp.float32
    )
    up_act = lax.dot_general(flat, expert_in[0, :, 1, :], dims, preferred_element_type=jnp.float32)
    units = (jax.nn.silu(gate_act) * up_act).astype(jnp.bfloat16)
    part = jnp.dot(units, expert_down[0], preferred_element_type=jnp.float32)
    return (part * gate).astype(jnp.bfloat16)


def moe_kernel(
    sent_ref,
    w_in_ref,
    w_down_ref,
    out_ref,
    tok,
    raw,
    w_in,
    w_down,
    units,
    gate,
    part,
    core_in,
    acc,
    diag_x,
    diag_y,
    from_x,
    from_y,
    z_send,
    z_up,
    z_down,
    relay,
    w_sems,
    g_sends,
    g_recvs,
    sends,
    recvs,
):
    x = lax.axis_index("dp")
    e = lax.axis_index("expert")
    z, y, c = e // 4, (e // 2) % 2, e % 2
    rows, model = out_ref.shape
    half = rows // 2
    width = w_down_ref.shape[0]
    high = z // 2
    low_z = z + high * (3 - 2 * z)
    mid = low_z == 1

    def flip(f):
        return f + high * (3 - 2 * f)

    planes = [z, flip(1 - low_z), flip(3 + 0 * z), flip(2 + 0 * z)]
    other_core = {"expert": e + 1 - 2 * c}
    other_y = {"expert": e + 2 - 4 * y}
    other_x = {"dp": 1 - x}
    above, below = {"expert": e + 4}, {"expert": e - 4}
    pair, middle = {"expert": e + 4 - 8 * (z % 2)}, {"expert": e + 4 * (3 - 2 * z)}
    halves = first, second = pl.ds(0, half), pl.ds(half, half)

    def remote(src, dst, send, recv, to):
        return pltpu.make_async_remote_copy(
            src_ref=src,
            dst_ref=dst,
            send_sem=send,
            recv_sem=recv,
            device_id=to,
            device_id_type=pl.DeviceIdType.MESH,
        )

    def same(ref, kind, p, to):
        return remote(ref, ref, g_sends.at[kind, p], g_recvs.at[kind, p], to)

    def g_up(p, h):
        return same(tok.at[p, y, c, x, halves[h]], h, p, above)

    def g_down(p, h):
        return same(tok.at[p, y, c, x, halves[h]], 2 + h, p, below)

    def g_x(p, i, h):
        return same(tok.at[p, y, c, i, halves[h]], 4 + h, p, other_x)

    def g_y(p, j, h):
        return same(tok.at[p, j, c, x, halves[h]], 6 + h, p, other_y)

    def g_diag_x(p, j):
        return same(tok.at[p, j, c, x, first], 8, p, other_x)

    def g_diag_y(p, i):
        return same(tok.at[p, y, c, i, second], 9, p, other_y)

    def g_core(p, kind, cc):
        j, i = (y, y, 1 - y, 1 - y)[kind], (x, 1 - x, x, 1 - x)[kind]
        return same(tok.at[p, j, cc, i], 10 + kind, p, other_core)

    def own_line(p):
        g_x(p, x, 1).start()
        g_y(p, y, 0).start()
        g_x(p, x, 0).start()
        g_y(p, y, 1).start()
        g_core(p, 0, c).start()

    def along_z(p, h):
        @pl.when(p < z)
        def _():
            g_up(p, h).wait_recv()

            @pl.when(z < 3)
            def _():
                g_up(p, h).start()

        @pl.when(p > z)
        def _():
            g_down(p, h).wait_recv()

            @pl.when(z > 0)
            def _():
                g_down(p, h).start()

    def beside_send(p):
        g_x(p, 1 - x, 1).wait_recv()
        g_diag_y(p, 1 - x).start()
        g_y(p, 1 - y, 0).wait_recv()
        g_diag_x(p, 1 - y).start()

    def beside_rest(p, diag=True):
        if not diag:
            g_x(p, 1 - x, 1).wait_recv()
            g_y(p, 1 - y, 0).wait_recv()
        g_x(p, 1 - x, 0).wait_recv()
        g_core(p, 1, c).start()
        g_y(p, 1 - y, 1).wait_recv()
        g_core(p, 2, c).start()

    def across(p):
        same(tok.at[p, 1 - y, c, 1 - x, first], 8, p, other_x).wait_recv()
        same(tok.at[p, 1 - y, c, 1 - x, second], 9, p, other_y).wait_recv()
        g_core(p, 3, c).start()

    def diag_up(p):
        return same(tok.at[p, 1 - y, c, 1 - x], 14, p, above)

    def diag_down(p):
        return same(tok.at[p, 1 - y, c, 1 - x], 15, p, below)

    def diag_out():
        @pl.when(z < 3)
        def _():
            diag_up(z).start()

        @pl.when(z > 0)
        def _():
            diag_down(z).start()

    def diag_in(p, forward):
        @pl.when(p < z)
        def _():
            diag_up(p).wait_recv()
            if forward:

                @pl.when(mid)
                def _():
                    diag_up(p).start()

        @pl.when(p > z)
        def _():
            diag_down(p).wait_recv()
            if forward:

                @pl.when(mid)
                def _():
                    diag_down(p).start()

        g_core(p, 3, c).start()

    def whole(p):
        for kind in range(4):
            g_core(p, kind, 1 - c).wait_recv()

    def tokens(p):
        return tok[p, :, :, :, :, pl.ds(0, model)].reshape(8 * rows, model)

    def hidden(p, lo, n):
        dims = (((1,), (1,)), ((), ()))
        values = tokens(p)
        gate_act = lax.dot_general(
            values, w_in[0, pl.ds(lo, n)], dims, preferred_element_type=jnp.float32
        )
        up_act = lax.dot_general(
            values, w_in[1, pl.ds(lo, n)], dims, preferred_element_type=jnp.float32
        )
        units[:, pl.ds(lo, n)] = (gate_act / (1.0 + jnp.exp(-gate_act)) * up_act).astype(
            units.dtype
        )

    def gates(p):
        extra = tok.shape[5] - model
        lanes = lax.broadcasted_iota(jnp.int32, (8 * rows, extra), 1)
        named = (lanes == e) | (lanes == e + lax.axis_size("expert"))
        values = tok[p, :, :, :, :, pl.ds(model, extra)].reshape(8 * rows, extra)
        gate[...] = jnp.sum(
            jnp.where(named, values.astype(jnp.float32), 0.0), axis=1, keepdims=True
        )

    def project(p, lo, n):
        value = jnp.dot(units[...], w_down[:, pl.ds(lo, n)], preferred_element_type=jnp.float32)
        part[p, :, :, :, :, pl.ds(lo, n)] = (
            (value * gate[...]).astype(part.dtype).reshape(2, 2, 2, rows, n)
        )

    def compute(p, between):
        steps = [functools.partial(hidden, p, lo, min(256, width - lo)) for lo in range(0, width, 256)]
        steps += [functools.partial(gates, p)]
        steps += [functools.partial(project, p, lo, 256) for lo in range(0, model, 256)]
        for number, step in enumerate(steps):
            step()
            for act in between.get(number, ()):
                act()

    def copy(src, dst, kind, k, to):
        return remote(src, dst, sends.at[kind, k], recvs.at[kind, k], to)

    def core_copy(k):
        return copy(part.at[planes[k], :, 1 - c], core_in.at[k], 0, k, other_core)

    def diag_y_copy(k):
        return copy(acc.at[k, 1 - y, 1 - x, first], diag_y.at[k], 1, k, other_y)

    def diag_x_copy(k):
        return copy(acc.at[k, 1 - y, 1 - x, second], diag_x.at[k], 2, k, other_x)

    def x_copy(k, h):
        return copy(acc.at[k, y, 1 - x, halves[h]], from_x.at[k, halves[h]], 3 + h, k, other_x)

    def y_copy(k, h):
        return copy(acc.at[k, 1 - y, x, halves[h]], from_y.at[k, halves[h]], 5 + h, k, other_y)

    def up_copy(g, h):
        return copy(z_send.at[g, halves[h]], z_up.at[g, halves[h]], 7 + h, g, above)

    def down_copy(g, h):
        return copy(z_send.at[g, halves[h]], z_down.at[g, halves[h]], 9 + h, g, below)

    def wide(value):
        return value.astype(jnp.float32)

    def relay_copy(k, slot, to):
        return copy(acc.at[k, 1 - y, 1 - x], relay.at[slot], 11, slot, to)

    def add_relay(k, slot):
        relay_copy(k, slot, pair).wait_recv()
        acc[k, 1 - y, 1 - x] = (wide(acc[k, 1 - y, 1 - x]) + wide(relay[slot])).astype(acc.dtype)

    def stage_a(k):
        core_copy(k).wait_recv()
        for j in (0, 1):
            for i in (0, 1):
                acc[k, j, i] = (wide(part[planes[k], j, c, i]) + wide(core_in[k, j, i])).astype(
                    acc.dtype
                )
        x_copy(k, 1).start()
        y_copy(k, 0).start()
        if k % 2 == 1:
            x_copy(k, 0).start()
            y_copy(k, 1).start()
        if k == 0:
            add_relay(0, 0)

            @pl.when(mid)
            def _():
                add_relay(0, 2)

        if k == 1:
            relay_copy(1, 0, pair).start()
        if k == 3:

            @pl.when(mid)
            def _():
                add_relay(3, 1)
                relay_copy(3, 2, middle).start()

            @pl.when(low_z == 0)
            def _():
                relay_copy(3, 1, pair).start()

        if k % 2 == 0:
            diag_y_copy(k).start()
            diag_x_copy(k).start()

    def stage_b(k):
        diag_y_copy(k).wait_recv()
        acc[k, y, 1 - x, first] = (wide(acc[k, y, 1 - x, first]) + wide(diag_y[k])).astype(acc.dtype)
        x_copy(k, 0).start()
        diag_x_copy(k).wait_recv()
        acc[k, 1 - y, x, second] = (wide(acc[k, 1 - y, x, second]) + wide(diag_x[k])).astype(
            acc.dtype
        )
        y_copy(k, 1).start()

    def stage_c(k, g, last=False):
        for h in (0, 1):
            at = halves[h]
            x_copy(k, h).wait_recv()
            y_copy(k, h).wait_recv()
            out_ref[at] = wide(acc[k, y, x, at]) + wide(from_x[k, at]) + wide(from_y[k, at])

            @pl.when((g >= z) & (z > 0))
            def _():
                up_copy(g, h).wait_recv()
                out_ref[at] += wide(z_up[g, at])

            @pl.when((g <= z) & (z < 3))
            def _():
                down_copy(g, h).wait_recv()
                out_ref[at] += wide(z_down[g, at])

            if not last:
                z_send[g, at] = out_ref[at].astype(z_send.dtype)

                @pl.when(g > z)
                def _():
                    up_copy(g, h).start()

                @pl.when(g < z)
                def _():
                    down_copy(g, h).start()

    load_in = pltpu.make_async_copy(w_in_ref, raw, w_sems.at[0])

    def untangle(lo, n):
        for at in range(lo, lo + n, 64):
            pairs = raw[pl.ds(at, 64)].reshape(128, model)
            row = lax.broadcasted_iota(jnp.int32, (128, 128), 0)
            column = lax.broadcasted_iota(jnp.int32, (128, 128), 1)
            order = jnp.where(column == 2 * (row % 64) + row // 64, 1.0, 0.0).astype(raw.dtype)
            sorted_rows = jnp.dot(order, pairs, preferred_element_type=jnp.float32).astype(raw.dtype)
            w_in[0, pl.ds(at, 64)] = sorted_rows[:64]
            w_in[1, pl.ds(at, 64)] = sorted_rows[64:]

    load_down = pltpu.make_async_copy(w_down_ref, w_down, w_sems.at[1])
    barrier = pltpu.get_barrier_semaphore()
    for to in (other_core, other_x, other_y):
        pl.semaphore_signal(barrier, inc=1, device_id=to, device_id_type=pl.DeviceIdType.MESH)

    @pl.when(z > 0)
    def _():
        pl.semaphore_signal(barrier, inc=1, device_id=below, device_id_type=pl.DeviceIdType.MESH)

    @pl.when(z < 3)
    def _():
        pl.semaphore_signal(barrier, inc=1, device_id=above, device_id_type=pl.DeviceIdType.MESH)

    load_in.start()
    load_down.start()
    tok[z, y, c, x] = sent_ref[...]
    pl.semaphore_wait(barrier, 4 + ((z + 1) // 2) % 2)

    for h in (0, 1):

        @pl.when(z < 3)
        def _():
            g_up(z, h).start()

        @pl.when(z > 0)
        def _():
            g_down(z, h).start()

    def do(f, *args):
        return functools.partial(f, *args)

    def at_mid(*acts):
        @pl.when(mid)
        def _():
            for act in acts:
                act()

    def at_end(*acts):
        @pl.when(low_z == 0)
        def _():
            for act in acts:
                act()

    def start_core(k):
        core_copy(k).start()

    own_line(z)
    load_in.wait()
    untangle(0, 256)
    along_z(planes[1], 0)
    at_mid(do(along_z, planes[3], 0))
    beside_send(planes[0])
    along_z(planes[1], 1)
    at_mid(do(along_z, planes[3], 1))
    own_line(planes[1])
    beside_rest(planes[0])
    untangle(256, 256)
    at_mid(do(along_z, planes[2], 0), do(along_z, planes[2], 1))
    at_end(do(along_z, planes[3], 0), do(along_z, planes[3], 1))
    across(planes[0])
    diag_out()
    own_line(planes[3])
    untangle(512, 192)
    load_down.wait()
    whole(planes[0])
    far = do(at_end, do(along_z, planes[2], 0), do(along_z, planes[2], 1))
    compute(
        planes[0],
        {
            2: [far, do(own_line, planes[2])],
            6: [do(beside_rest, planes[1], False)],
        },
    )
    diag_in(planes[1], False)
    whole(planes[1])
    compute(
        planes[1],
        {
            0: [do(diag_in, planes[3], True)],
            1: [do(beside_rest, planes[3], False)],
            6: [do(beside_send, planes[2])],
            11: [do(beside_rest, planes[2])],
        },
    )
    start_core(1)
    across(planes[2])
    whole(planes[2])
    compute(planes[2], {0: [do(stage_a, 1)]})
    start_core(2)
    whole(planes[3])
    compute(
        planes[3],
        {
            0: [do(stage_a, 2)],
            4: [do(at_end, do(stage_c, 1, planes[1]))],
            8: [do(stage_b, 2)],
        },
    )
    start_core(3)
    start_core(0)
    stage_a(3)
    stage_c(2, planes[2])
    stage_a(0)
    at_mid(do(stage_c, 1, planes[1]))
    stage_b(0)
    stage_c(3, planes[3])
    stage_c(0, planes[0], True)

    for k in range(4):
        p = planes[k]
        core_copy(k).wait_send()
        if k % 2 == 0:
            diag_y_copy(k).wait_send()
            diag_x_copy(k).wait_send()
            g_diag_y(p, 1 - x).wait_send()
            g_diag_x(p, 1 - y).wait_send()
        for kind in range(4):
            g_core(p, kind, c).wait_send()
        if k == 0:

            @pl.when(z < 3)
            def _():
                diag_up(p).wait_send()

            @pl.when(z > 0)
            def _():
                diag_down(p).wait_send()

        if k == 1:
            relay_copy(1, 0, pair).wait_send()
        if k == 3:

            @pl.when(mid & (p < z))
            def _():
                diag_up(p).wait_send()

            @pl.when(mid & (p > z))
            def _():
                diag_down(p).wait_send()

            @pl.when(mid)
            def _():
                relay_copy(3, 2, middle).wait_send()

            @pl.when(low_z == 0)
            def _():
                relay_copy(3, 1, pair).wait_send()

        for h in (0, 1):
            x_copy(k, h).wait_send()
            y_copy(k, h).wait_send()
            g_x(p, x, h).wait_send()
            g_y(p, y, h).wait_send()

            @pl.when((p <= z) & (z < 3))
            def _():
                g_up(p, h).wait_send()

            @pl.when((p >= z) & (z > 0))
            def _():
                g_down(p, h).wait_send()

            if k > 0:

                @pl.when(p > z)
                def _():
                    up_copy(p, h).wait_send()

                @pl.when(p < z)
                def _():
                    down_copy(p, h).wait_send()


def mixture_kernel(sent, w_in, w_down):
    rows, full = sent.shape
    width, model = w_down.shape
    kind = sent.dtype
    line = pltpu.VMEM((4, rows, model), kind)
    halves = pltpu.VMEM((4, rows // 2, model), kind)
    return pl.pallas_call(
        moe_kernel,
        out_shape=jax.ShapeDtypeStruct((rows, model), jnp.float32),
        in_specs=[
            pl.BlockSpec(memory_space=pltpu.VMEM),
            pl.BlockSpec(memory_space=pl.ANY),
            pl.BlockSpec(memory_space=pl.ANY),
        ],
        out_specs=pl.BlockSpec(memory_space=pltpu.VMEM),
        scratch_shapes=[
            pltpu.VMEM((4, 2, 2, 2, rows, full), kind),
            pltpu.VMEM((width, 2, model), kind),
            pltpu.VMEM((2, width, model), kind),
            pltpu.VMEM((width, model), kind),
            pltpu.VMEM((8 * rows, width), kind),
            pltpu.VMEM((8 * rows, 1), jnp.float32),
            pltpu.VMEM((4, 2, 2, 2, rows, model), kind),
            pltpu.VMEM((4, 2, 2, rows, model), kind),
            pltpu.VMEM((4, 2, 2, rows, model), kind),
            halves,
            halves,
            line,
            line,
            line,
            line,
            line,
            pltpu.VMEM((3, rows, model), kind),
            pltpu.SemaphoreType.DMA((2,)),
            pltpu.SemaphoreType.DMA((16, 4)),
            pltpu.SemaphoreType.DMA((16, 4)),
            pltpu.SemaphoreType.DMA((12, 4)),
            pltpu.SemaphoreType.DMA((12, 4)),
        ],
        compiler_params=pltpu.CompilerParams(
            collective_id=0, has_side_effects=True, vmem_limit_bytes=58 * 2**20
        ),
    )(sent, w_in, w_down)


def attend_kernel(
    table_ref,
    length_ref,
    nope_ref,
    rope_ref,
    new_ref,
    new_rope_ref,
    pages_ref,
    pages_rope_ref,
    residual_ref,
    gain_ref,
    gates_ref,
    key_up_ref,
    value_up_ref,
    out_weight_ref,
    sent_ref,
    hidden_ref,
    keys,
    keys_rope,
    key_up,
    value_up,
    out_weight,
    residual,
    query_lat,
    query_rope,
    scores,
    heads_out,
    partial,
    arrived,
    loads,
    sends,
    recvs,
):
    x = lax.axis_index("dp")
    other_x = {"dp": 1 - x}
    heads = key_up.shape[0]
    tokens = nope_ref.shape[0]
    held = pages_ref.shape[0]
    rows, model = hidden_ref.shape
    chunks, piece = partial.shape[0], partial.shape[2]
    span = 2 * held
    scale = 1.0 / (HD + RD) ** 0.5
    nt = (((1,), (1,)), ((), ()))

    def remote(src, dst, k):
        return pltpu.make_async_remote_copy(
            src_ref=src,
            dst_ref=dst,
            send_sem=sends.at[k],
            recv_sem=recvs.at[k],
            device_id=other_x,
            device_id_type=pl.DeviceIdType.MESH,
        )

    mine = [
        pltpu.make_async_copy(key_up_ref, key_up, loads.at[0]),
        pltpu.make_async_copy(pages_ref, keys.at[pl.ds(0, held)], loads.at[1]),
        pltpu.make_async_copy(value_up_ref, value_up, loads.at[2]),
        pltpu.make_async_copy(out_weight_ref, out_weight, loads.at[3]),
        pltpu.make_async_copy(residual_ref.at[pl.ds(x * rows, rows)], residual, loads.at[4]),
    ]
    far_keys = remote(pages_ref, keys.at[pl.ds(held + tokens, held)], 0)
    far_rope = remote(pages_rope_ref, keys_rope.at[pl.ds(held, held)], 1)
    barrier = pltpu.get_barrier_semaphore()
    pl.semaphore_signal(barrier, inc=1, device_id=other_x, device_id_type=pl.DeviceIdType.MESH)
    for load in mine:
        load.start()
    pl.semaphore_wait(barrier, 1)
    far_keys.start()
    far_rope.start()
    keys[pl.ds(held, tokens)] = new_ref[...]
    keys_rope[pl.ds(0, held)] = pages_rope_ref[...]

    def bias(start):
        place = lax.broadcasted_iota(jnp.int32, (8, held), 1) + start
        slot, offset = place // PAGE, place % PAGE
        seen = jnp.zeros((8, held), jnp.int32)
        for j in range(span // PAGE):
            seen += jnp.where(
                (slot == table_ref[0, j]) & (offset + j * PAGE < length_ref[0]), 1, 0
            )
        return jnp.where(seen > 0, 0.0, NEG)[0:1]

    mine[0].wait()
    for h in range(heads):
        query_lat[pl.ds(h * tokens, tokens)] = jnp.dot(
            nope_ref[:, pl.ds(h * HD, HD)], key_up[h], preferred_element_type=jnp.float32
        ).astype(query_lat.dtype)
        query_rope[pl.ds(h * tokens, tokens)] = rope_ref[:, pl.ds(h * RD, RD)]
    mine[1].wait()

    def against(lo, n, rope_keys, dims):
        return (
            lax.dot_general(
                query_lat[...], keys[pl.ds(lo, n)], nt, preferred_element_type=jnp.float32
            )
            + lax.dot_general(query_rope[...], rope_keys, dims, preferred_element_type=jnp.float32)
        ) * scale

    scores[:, pl.ds(0, held)] = against(0, held, keys_rope[pl.ds(0, held)], nt) + bias(x * held)
    fresh = against(held, tokens, new_rope_ref[...], (((1,), (0,)), ((), ())))
    seen = lax.broadcasted_iota(jnp.int32, (tokens, tokens), 1) <= lax.broadcasted_iota(
        jnp.int32, (tokens, tokens), 0
    )
    causal = jnp.where(seen, 0.0, NEG)
    scores[:, pl.ds(held, tokens)] = (
        fresh.reshape(heads, tokens, tokens) + causal[None]
    ).reshape(heads * tokens, tokens)
    far_keys.wait_recv()
    far_rope.wait_recv()
    scores[:, pl.ds(held + tokens, held)] = against(
        held + tokens, held, keys_rope[pl.ds(held, held)], nt
    ) + bias((1 - x) * held)
    mine[2].wait()
    for h in range(heads):
        masked = scores[pl.ds(h * tokens, tokens)]
        expo = jnp.exp(masked - jnp.max(masked, axis=1, keepdims=True))
        total = jnp.sum(expo, axis=1, keepdims=True)
        attn = jnp.dot(expo.astype(keys.dtype), keys[...], preferred_element_type=jnp.float32)
        heads_out[:, pl.ds(h * HD, HD)] = jnp.dot(
            (attn / total).astype(keys.dtype), value_up[h], preferred_element_type=jnp.float32
        ).astype(heads_out.dtype)
    mine[3].wait()

    def exchange(n):
        return remote(partial.at[n, pl.ds((1 - x) * rows, rows)], arrived.at[n], 2 + n)

    for n in range(chunks):
        partial[n] = jnp.dot(
            heads_out[...],
            out_weight[:, pl.ds(n * piece, piece)],
            preferred_element_type=jnp.float32,
        ).astype(partial.dtype)
        exchange(n).start()
    mine[4].wait()
    sent_ref[:, pl.ds(model, gates_ref.shape[1])] = gates_ref[...]
    power = jnp.zeros((rows, 1), jnp.float32)
    for n in range(chunks):
        exchange(n).wait_recv()
        at = pl.ds(n * piece, piece)
        hidden = (
            residual[:, at].astype(jnp.float32)
            + partial[n, pl.ds(x * rows, rows)].astype(jnp.float32)
            + arrived[n].astype(jnp.float32)
        )
        hidden_ref[:, at] = hidden
        power += jnp.sum(hidden * hidden, axis=1, keepdims=True)
    factor = lax.rsqrt(power / model + EPS)
    for n in range(chunks):
        at = pl.ds(n * piece, piece)
        sent_ref[:, at] = (hidden_ref[:, at] * factor * gain_ref[:, at]).astype(sent_ref.dtype)
    far_keys.wait_send()
    far_rope.wait_send()
    for n in range(chunks):
        exchange(n).wait_send()


def attend(
    table,
    length,
    nope,
    rope,
    new,
    new_rope,
    pages,
    pages_rope,
    residual,
    gain,
    gates,
    key_up,
    value_up,
    out_weight,
):
    kind = nope.dtype
    heads = key_up.shape[0]
    tokens, model = residual.shape
    rows = tokens // 2
    held = pages.shape[0]
    chunks = 4
    vmem = pl.BlockSpec(memory_space=pltpu.VMEM)
    smem = pl.BlockSpec(memory_space=pltpu.SMEM)
    far = pl.BlockSpec(memory_space=pl.ANY)
    return pl.pallas_call(
        attend_kernel,
        out_shape=(
            jax.ShapeDtypeStruct((rows, model + gates.shape[1]), kind),
            jax.ShapeDtypeStruct((rows, model), jnp.float32),
        ),
        in_specs=[smem, smem, vmem, vmem, vmem, vmem, far, vmem, far, vmem, vmem, far, far, far],
        out_specs=(vmem, vmem),
        scratch_shapes=[
            pltpu.VMEM((2 * held + tokens, LAT), kind),
            pltpu.VMEM((2 * held, RD), kind),
            pltpu.VMEM(key_up.shape, kind),
            pltpu.VMEM(value_up.shape, kind),
            pltpu.VMEM(out_weight.shape, kind),
            pltpu.VMEM((rows, model), kind),
            pltpu.VMEM((heads * tokens, LAT), kind),
            pltpu.VMEM((heads * tokens, RD), kind),
            pltpu.VMEM((heads * tokens, 2 * held + tokens), jnp.float32),
            pltpu.VMEM((tokens, heads * HD), kind),
            pltpu.VMEM((chunks, tokens, model // chunks), kind),
            pltpu.VMEM((chunks, rows, model // chunks), kind),
            pltpu.SemaphoreType.DMA((5,)),
            pltpu.SemaphoreType.DMA((2 + chunks,)),
            pltpu.SemaphoreType.DMA((2 + chunks,)),
        ],
        compiler_params=pltpu.CompilerParams(
            collective_id=1, has_side_effects=True, vmem_limit_bytes=40 * 2**20
        ),
    )(
        table,
        length,
        nope,
        rope,
        new,
        new_rope,
        pages,
        pages_rope,
        residual,
        gain,
        gates,
        key_up,
        value_up,
        out_weight,
    )


def per_device(
    query_nope,
    query_rope,
    latent_new,
    key_rope,
    latent_pages,
    rope_pages,
    page_table,
    prefix_lengths,
    residual,
    key_up,
    value_up,
    out_weight,
    norm_gain,
    expert_in,
    expert_down,
    expert_ids,
    expert_weights,
):
    groups = lax.axis_size("dp")
    experts_all = lax.axis_size("expert") * expert_in.shape[0]
    tokens_col = query_nope.shape[1]
    block_rows = tokens_col // groups
    heads_here = key_up.shape[0]
    fits = groups == 2 and lax.axis_size("expert") == 16
    start = lax.axis_index("dp") * block_rows
    ids_mine = lax.dynamic_slice_in_dim(expert_ids[0], start, block_rows, 0)
    weights_mine = lax.dynamic_slice_in_dim(expert_weights[0], start, block_rows, 0)
    gates = jnp.sum(
        jnp.where(
            ids_mine[:, :, None] == jnp.arange(experts_all)[None, None, :],
            weights_mine[:, :, None],
            0.0,
        ),
        axis=1,
    )
    gates_high = gates.astype(jnp.bfloat16)
    gates_low = (gates - gates_high.astype(jnp.float32)).astype(jnp.bfloat16)
    model = residual.shape[2]
    extra = -(-2 * experts_all // 128) * 128
    fill = jnp.zeros((block_rows, extra - 2 * experts_all), jnp.bfloat16)
    coded = jnp.concatenate([gates_high, gates_low, fill], axis=1)
    if fits:
        sent, hidden_mine = attend(
            page_table,
            prefix_lengths,
            query_nope[0],
            query_rope[0],
            latent_new[0],
            jnp.transpose(key_rope[0]),
            latent_pages[0].reshape(-1, LAT),
            rope_pages[0].reshape(-1, RD),
            residual[0],
            norm_gain[None],
            coded,
            key_up,
            value_up,
            out_weight,
        )
        mixture = mixture_kernel(sent, expert_in[0], expert_down[0])
    else:
        pages_lat, pages_rope = (
            lax.all_gather(latent_pages[0], "dp", axis=0, tiled=True),
            lax.all_gather(rope_pages[0], "dp", axis=0, tiled=True),
        )
        page_count = pages_lat.shape[0]
        table = page_table[0]
        inverse = jnp.sum(
            jnp.where(
                table[:, None] == jnp.arange(page_count)[None, :], jnp.arange(page_count)[:, None], 0
            ),
            axis=0,
        )
        positions = (inverse[:, None] * PAGE + jnp.arange(PAGE)[None, :]).reshape(-1)
        prefix_ok = positions < prefix_lengths[0]
        keys_lat = jnp.concatenate([pages_lat.reshape(-1, LAT), latent_new[0]], axis=0)
        keys_rope = jnp.concatenate([pages_rope.reshape(-1, RD), key_rope[0]], axis=0)
        heads_nope = query_nope[0].reshape(tokens_col, heads_here, HD)
        query_lat = jnp.einsum(
            "thd,hdc->thc", heads_nope, key_up, preferred_element_type=jnp.float32
        ).astype(jnp.bfloat16)
        heads_rope = query_rope[0].reshape(tokens_col, heads_here, RD)
        scale = 1.0 / (HD + RD) ** 0.5
        scores = (
            jnp.einsum("thc,kc->thk", query_lat, keys_lat, preferred_element_type=jnp.float32)
            + jnp.einsum("thr,kr->thk", heads_rope, keys_rope, preferred_element_type=jnp.float32)
        ) * scale
        causal = jnp.arange(tokens_col)[None, :] <= jnp.arange(tokens_col)[:, None]
        allowed = jnp.concatenate(
            [jnp.broadcast_to(prefix_ok[None, :], (tokens_col, prefix_ok.shape[0])), causal], axis=1
        )[:, None, :]
        masked = jnp.where(allowed, scores, NEG)
        peak = jnp.max(masked, axis=-1, keepdims=True)
        expo = jnp.where(allowed, jnp.exp(masked - peak), 0.0)
        total = jnp.sum(expo, axis=-1, keepdims=True)
        probs = expo.astype(jnp.bfloat16)
        attn_latent = (
            jnp.einsum("thk,kc->thc", probs, keys_lat, preferred_element_type=jnp.float32) / total
        ).astype(jnp.bfloat16)
        heads_out = jnp.einsum(
            "thc,hcd->thd", attn_latent, value_up, preferred_element_type=jnp.float32
        ).astype(jnp.bfloat16)
        partial_out = jnp.dot(
            heads_out.reshape(tokens_col, heads_here * HD),
            out_weight,
            preferred_element_type=jnp.float32,
        )
        attended = lax.psum_scatter(
            partial_out.astype(jnp.bfloat16), "dp", scatter_dimension=0, tiled=True
        ).astype(jnp.float32)
        hidden_mine = (
            lax.dynamic_slice_in_dim(residual[0], start, block_rows, 0).astype(jnp.float32) + attended
        )
        normed = norm_rows(hidden_mine, norm_gain)
        sent = jnp.concatenate([normed, coded], axis=1)
        gathered = lax.all_gather(sent, ("expert", "dp"), axis=0, tiled=True)
        everyone = gathered[:, :model]
        mine = lax.axis_index("expert")
        named = (jnp.arange(extra) == mine) | (jnp.arange(extra) == mine + experts_all)
        gate = jnp.sum(
            jnp.where(named[None, :], gathered[:, model:].astype(jnp.float32), 0.0),
            axis=1,
            keepdims=True,
        )
        part = expert_apply(everyone, gate, expert_in, expert_down)
        mixture = lax.psum_scatter(
            part, ("expert", "dp"), scatter_dimension=0, tiled=True
        ).astype(jnp.float32)
    layer_out = (hidden_mine + mixture).astype(jnp.bfloat16)[None]
    return (layer_out, mixture.astype(jnp.bfloat16)[None])


def solution(mesh):
    return jax.shard_map(
        per_device,
        mesh=mesh,
        in_specs=(
            P("expert", None, "dp"),
            P("expert", None, "dp"),
            P("expert", None, None),
            P("expert", None, None),
            P("expert", "dp", None, None),
            P("expert", "dp", None),
            P("expert", None),
            P("expert"),
            P("expert", None, None),
            P("dp", None, None),
            P("dp", None, None),
            P("dp", None),
            P(),
            P("expert", "dp", None, None),
            P("expert", "dp", None),
            P("expert", None, None),
            P("expert", None, None),
        ),
        out_specs=(P("expert", "dp", None), P("expert", "dp", None)),
        check_vma=False,
    )
```

```python
import functools

import jax
import jax.numpy as jnp
from jax import lax
from jax.experimental import pallas as pl
from jax.experimental.pallas import tpu as pltpu
from jax.sharding import PartitionSpec as P

HD = 128
RD = 64
LAT = 512
TOP = 6
PAGE = 64


EPS = 1e-06
NEG = -1e30


def norm_rows(hidden, norm_gain):
    power = jnp.mean(hidden * hidden, axis=-1, keepdims=True)
    return (hidden * lax.rsqrt(power + EPS) * norm_gain).astype(jnp.bfloat16)


def expert_apply(tokens, gate, expert_in, expert_down):
    flat = tokens.reshape(-1, tokens.shape[-1])
    dims = (((1,), (1,)), ((), ()))
    gate_act = lax.dot_general(
        flat, expert_in[0, :, 0, :], dims, preferred_element_type=jnp.float32
    )
    up_act = lax.dot_general(flat, expert_in[0, :, 1, :], dims, preferred_element_type=jnp.float32)
    units = (jax.nn.silu(gate_act) * up_act).astype(jnp.bfloat16)
    part = jnp.dot(units, expert_down[0], preferred_element_type=jnp.float32)
    return (part * gate).astype(jnp.bfloat16)


def moe_kernel(
    sent_ref,
    w_in_ref,
    w_down_ref,
    out_ref,
    tok,
    raw,
    w_in,
    w_down,
    units,
    gate,
    part,
    core_in,
    acc,
    diag_x,
    diag_y,
    from_x,
    from_y,
    z_send,
    z_up,
    z_down,
    relay,
    w_sems,
    g_sends,
    g_recvs,
    sends,
    recvs,
):
    x = lax.axis_index("dp")
    e = lax.axis_index("expert")
    z, y, c = e // 4, (e // 2) % 2, e % 2
    rows, model = out_ref.shape
    half = rows // 2
    width = w_down_ref.shape[0]
    high = z // 2
    low_z = z + high * (3 - 2 * z)
    mid = low_z == 1

    def flip(f):
        return f + high * (3 - 2 * f)

    planes = [z, flip(1 - low_z), flip(3 + 0 * z), flip(2 + 0 * z)]
    other_core = {"expert": e + 1 - 2 * c}
    other_y = {"expert": e + 2 - 4 * y}
    other_x = {"dp": 1 - x}
    above, below = {"expert": e + 4}, {"expert": e - 4}
    pair, middle = {"expert": e + 4 - 8 * (z % 2)}, {"expert": e + 4 * (3 - 2 * z)}
    halves = first, second = pl.ds(0, half), pl.ds(half, half)

    def remote(src, dst, send, recv, to):
        return pltpu.make_async_remote_copy(
            src_ref=src,
            dst_ref=dst,
            send_sem=send,
            recv_sem=recv,
            device_id=to,
            device_id_type=pl.DeviceIdType.MESH,
        )

    def same(ref, kind, p, to):
        return remote(ref, ref, g_sends.at[kind, p], g_recvs.at[kind, p], to)

    def g_up(p, h):
        return same(tok.at[p, y, c, x, halves[h]], h, p, above)

    def g_down(p, h):
        return same(tok.at[p, y, c, x, halves[h]], 2 + h, p, below)

    def g_x(p, i, h):
        return same(tok.at[p, y, c, i, halves[h]], 4 + h, p, other_x)

    def g_y(p, j, h):
        return same(tok.at[p, j, c, x, halves[h]], 6 + h, p, other_y)

    def g_diag_x(p, j):
        return same(tok.at[p, j, c, x, first], 8, p, other_x)

    def g_diag_y(p, i):
        return same(tok.at[p, y, c, i, second], 9, p, other_y)

    def g_core(p, kind, cc):
        j, i = (y, y, 1 - y, 1 - y)[kind], (x, 1 - x, x, 1 - x)[kind]
        return same(tok.at[p, j, cc, i], 10 + kind, p, other_core)

    def own_line(p):
        g_x(p, x, 1).start()
        g_y(p, y, 0).start()
        g_x(p, x, 0).start()
        g_y(p, y, 1).start()
        g_core(p, 0, c).start()

    def along_z(p, h):
        @pl.when(p < z)
        def _():
            g_up(p, h).wait_recv()

            @pl.when(z < 3)
            def _():
                g_up(p, h).start()

        @pl.when(p > z)
        def _():
            g_down(p, h).wait_recv()

            @pl.when(z > 0)
            def _():
                g_down(p, h).start()

    def beside_send(p):
        g_x(p, 1 - x, 1).wait_recv()
        g_diag_y(p, 1 - x).start()
        g_y(p, 1 - y, 0).wait_recv()
        g_diag_x(p, 1 - y).start()

    def beside_rest(p, diag=True):
        if not diag:
            g_x(p, 1 - x, 1).wait_recv()
            g_y(p, 1 - y, 0).wait_recv()
        g_x(p, 1 - x, 0).wait_recv()
        g_core(p, 1, c).start()
        g_y(p, 1 - y, 1).wait_recv()
        g_core(p, 2, c).start()

    def across(p):
        same(tok.at[p, 1 - y, c, 1 - x, first], 8, p, other_x).wait_recv()
        same(tok.at[p, 1 - y, c, 1 - x, second], 9, p, other_y).wait_recv()
        g_core(p, 3, c).start()

    def diag_up(p):
        return same(tok.at[p, 1 - y, c, 1 - x], 14, p, above)

    def diag_down(p):
        return same(tok.at[p, 1 - y, c, 1 - x], 15, p, below)

    def diag_out():
        @pl.when(z < 3)
        def _():
            diag_up(z).start()

        @pl.when(z > 0)
        def _():
            diag_down(z).start()

    def diag_in(p, forward):
        @pl.when(p < z)
        def _():
            diag_up(p).wait_recv()
            if forward:

                @pl.when(mid)
                def _():
                    diag_up(p).start()

        @pl.when(p > z)
        def _():
            diag_down(p).wait_recv()
            if forward:

                @pl.when(mid)
                def _():
                    diag_down(p).start()

        g_core(p, 3, c).start()

    def whole(p):
        for kind in range(4):
            g_core(p, kind, 1 - c).wait_recv()

    def tokens(p):
        return tok[p, :, :, :, :, pl.ds(0, model)].reshape(8 * rows, model)

    def hidden(p, lo, n):
        dims = (((1,), (1,)), ((), ()))
        values = tokens(p)
        gate_act = lax.dot_general(
            values, w_in[0, pl.ds(lo, n)], dims, preferred_element_type=jnp.float32
        )
        up_act = lax.dot_general(
            values, w_in[1, pl.ds(lo, n)], dims, preferred_element_type=jnp.float32
        )
        units[:, pl.ds(lo, n)] = (gate_act / (1.0 + jnp.exp(-gate_act)) * up_act).astype(
            units.dtype
        )

    def gates(p):
        extra = tok.shape[5] - model
        lanes = lax.broadcasted_iota(jnp.int32, (8 * rows, extra), 1)
        named = (lanes == e) | (lanes == e + lax.axis_size("expert"))
        values = tok[p, :, :, :, :, pl.ds(model, extra)].reshape(8 * rows, extra)
        gate[...] = jnp.sum(
            jnp.where(named, values.astype(jnp.float32), 0.0), axis=1, keepdims=True
        )

    def project(p, lo, n):
        value = jnp.dot(units[...], w_down[:, pl.ds(lo, n)], preferred_element_type=jnp.float32)
        part[p, :, :, :, :, pl.ds(lo, n)] = (
            (value * gate[...]).astype(part.dtype).reshape(2, 2, 2, rows, n)
        )

    def compute(p, between):
        steps = [functools.partial(hidden, p, lo, min(256, width - lo)) for lo in range(0, width, 256)]
        steps += [functools.partial(gates, p)]
        steps += [functools.partial(project, p, lo, 256) for lo in range(0, model, 256)]
        for number, step in enumerate(steps):
            step()
            for act in between.get(number, ()):
                act()

    def copy(src, dst, kind, k, to):
        return remote(src, dst, sends.at[kind, k], recvs.at[kind, k], to)

    def core_copy(k):
        return copy(part.at[planes[k], :, 1 - c], core_in.at[k], 0, k, other_core)

    def diag_y_copy(k):
        return copy(acc.at[k, 1 - y, 1 - x, first], diag_y.at[k], 1, k, other_y)

    def diag_x_copy(k):
        return copy(acc.at[k, 1 - y, 1 - x, second], diag_x.at[k], 2, k, other_x)

    def x_copy(k, h):
        return copy(acc.at[k, y, 1 - x, halves[h]], from_x.at[k, halves[h]], 3 + h, k, other_x)

    def y_copy(k, h):
        return copy(acc.at[k, 1 - y, x, halves[h]], from_y.at[k, halves[h]], 5 + h, k, other_y)

    def up_copy(g, h):
        return copy(z_send.at[g, halves[h]], z_up.at[g, halves[h]], 7 + h, g, above)

    def down_copy(g, h):
        return copy(z_send.at[g, halves[h]], z_down.at[g, halves[h]], 9 + h, g, below)

    def wide(value):
        return value.astype(jnp.float32)

    def relay_copy(k, slot, h, to):
        return copy(
            acc.at[k, 1 - y, 1 - x, halves[h]], relay.at[slot, halves[h]], 11 + h, slot, to
        )

    def add_relay(k, slot, h):
        at = halves[h]
        relay_copy(k, slot, h, pair).wait_recv()
        acc[k, 1 - y, 1 - x, at] = (wide(acc[k, 1 - y, 1 - x, at]) + wide(relay[slot, at])).astype(
            acc.dtype
        )

    def add_core(k, j, i):
        acc[k, j, i] = (wide(part[planes[k], j, c, i]) + wide(core_in[k, j, i])).astype(acc.dtype)

    def stage_a(k):
        core_copy(k).wait_recv()
        add_core(k, 1 - y, 1 - x)
        if k == 1:
            relay_copy(1, 0, 0, pair).start()
            relay_copy(1, 0, 1, pair).start()
        if k == 2:
            diag_y_copy(k).start()
            diag_x_copy(k).start()
        if k == 3:

            @pl.when(low_z == 0)
            def _():
                relay_copy(3, 1, 0, pair).start()
                relay_copy(3, 1, 1, pair).start()

        add_core(k, y, 1 - x)
        x_copy(k, 1).start()
        if k % 2 == 1:
            x_copy(k, 0).start()
        add_core(k, 1 - y, x)
        y_copy(k, 0).start()
        if k % 2 == 1:
            y_copy(k, 1).start()
        add_core(k, y, x)
        if k == 3:

            @pl.when(mid)
            def _():
                for h in (0, 1):
                    add_relay(3, 1, h)
                    relay_copy(3, 2, h, middle).start()

    def own_diag():
        for h in (0, 1):
            add_relay(0, 0, h)

            @pl.when(mid)
            def _():
                add_relay(0, 2, h)

            (diag_y_copy, diag_x_copy)[h](0).start()

    def stage_b(k):
        diag_y_copy(k).wait_recv()
        acc[k, y, 1 - x, first] = (wide(acc[k, y, 1 - x, first]) + wide(diag_y[k])).astype(acc.dtype)
        x_copy(k, 0).start()
        diag_x_copy(k).wait_recv()
        acc[k, 1 - y, x, second] = (wide(acc[k, 1 - y, x, second]) + wide(diag_x[k])).astype(
            acc.dtype
        )
        y_copy(k, 1).start()

    def stage_c(k, g, last=False):
        for h in (0, 1):
            at = halves[h]
            x_copy(k, h).wait_recv()
            y_copy(k, h).wait_recv()
            out_ref[at] = wide(acc[k, y, x, at]) + wide(from_x[k, at]) + wide(from_y[k, at])

            @pl.when((g >= z) & (z > 0))
            def _():
                up_copy(g, h).wait_recv()
                out_ref[at] += wide(z_up[g, at])

            @pl.when((g <= z) & (z < 3))
            def _():
                down_copy(g, h).wait_recv()
                out_ref[at] += wide(z_down[g, at])

            if not last:
                z_send[g, at] = out_ref[at].astype(z_send.dtype)

                @pl.when(g > z)
                def _():
                    up_copy(g, h).start()

                @pl.when(g < z)
                def _():
                    down_copy(g, h).start()

    load_in = pltpu.make_async_copy(w_in_ref, raw, w_sems.at[0])

    def untangle(lo, n):
        for at in range(lo, lo + n, 64):
            pairs = raw[pl.ds(at, 64)].reshape(128, model)
            row = lax.broadcasted_iota(jnp.int32, (128, 128), 0)
            column = lax.broadcasted_iota(jnp.int32, (128, 128), 1)
            order = jnp.where(column == 2 * (row % 64) + row // 64, 1.0, 0.0).astype(raw.dtype)
            sorted_rows = jnp.dot(order, pairs, preferred_element_type=jnp.float32).astype(raw.dtype)
            w_in[0, pl.ds(at, 64)] = sorted_rows[:64]
            w_in[1, pl.ds(at, 64)] = sorted_rows[64:]

    load_down = pltpu.make_async_copy(w_down_ref, w_down, w_sems.at[1])
    barrier = pltpu.get_barrier_semaphore()
    for to in (other_core, other_x, other_y):
        pl.semaphore_signal(barrier, inc=1, device_id=to, device_id_type=pl.DeviceIdType.MESH)

    @pl.when(z > 0)
    def _():
        pl.semaphore_signal(barrier, inc=1, device_id=below, device_id_type=pl.DeviceIdType.MESH)

    @pl.when(z < 3)
    def _():
        pl.semaphore_signal(barrier, inc=1, device_id=above, device_id_type=pl.DeviceIdType.MESH)

    load_in.start()
    load_down.start()
    tok[z, y, c, x] = sent_ref[...]
    pl.semaphore_wait(barrier, 4 + ((z + 1) // 2) % 2)

    for h in (0, 1):

        @pl.when(z < 3)
        def _():
            g_up(z, h).start()

        @pl.when(z > 0)
        def _():
            g_down(z, h).start()

    def do(f, *args):
        return functools.partial(f, *args)

    def at_mid(*acts):
        @pl.when(mid)
        def _():
            for act in acts:
                act()

    def at_end(*acts):
        @pl.when(low_z == 0)
        def _():
            for act in acts:
                act()

    def start_core(k):
        core_copy(k).start()

    own_line(z)
    load_in.wait()
    untangle(0, 256)
    along_z(planes[1], 0)
    at_mid(do(along_z, planes[3], 0))
    beside_send(planes[0])
    along_z(planes[1], 1)
    at_mid(do(along_z, planes[3], 1))
    own_line(planes[1])
    beside_rest(planes[0])
    untangle(256, 256)
    at_mid(do(along_z, planes[2], 0), do(along_z, planes[2], 1))
    at_end(do(along_z, planes[3], 0), do(along_z, planes[3], 1))
    across(planes[0])
    diag_out()
    at_mid(do(own_line, planes[2]))
    untangle(512, 192)
    load_down.wait()
    whole(planes[0])
    compute(
        planes[0],
        {
            2: [
                do(at_end, do(along_z, planes[2], 0), do(along_z, planes[2], 1)),
                do(at_end, do(own_line, planes[2])),
            ],
            8: [do(beside_rest, planes[1], False)],
        },
    )
    start_core(0)
    own_line(planes[3])
    at_mid(do(diag_in, planes[3], True))
    beside_send(planes[2])
    diag_in(planes[1], False)
    whole(planes[1])
    compute(planes[1], {4: [do(beside_rest, planes[2])], 9: [do(across, planes[2])]})
    start_core(1)
    whole(planes[2])
    compute(
        planes[2],
        {
            0: [do(stage_a, 0)],
            2: [do(stage_a, 1)],
            5: [do(beside_rest, planes[3], False)],
            8: [do(at_end, do(diag_in, planes[3], False))],
        },
    )
    start_core(2)
    whole(planes[3])
    compute(
        planes[3],
        {
            2: [do(stage_a, 2)],
            7: [do(at_end, do(stage_c, 1, planes[1]))],
            11: [do(stage_b, 2)],
        },
    )
    start_core(3)
    at_end(own_diag)
    stage_a(3)
    stage_c(2, planes[2])
    at_mid(own_diag)
    at_mid(do(stage_c, 1, planes[1]))
    stage_b(0)
    stage_c(3, planes[3])
    stage_c(0, planes[0], True)

    for k in range(4):
        p = planes[k]
        core_copy(k).wait_send()
        if k % 2 == 0:
            diag_y_copy(k).wait_send()
            diag_x_copy(k).wait_send()
            g_diag_y(p, 1 - x).wait_send()
            g_diag_x(p, 1 - y).wait_send()
        for kind in range(4):
            g_core(p, kind, c).wait_send()
        if k == 0:

            @pl.when(z < 3)
            def _():
                diag_up(p).wait_send()

            @pl.when(z > 0)
            def _():
                diag_down(p).wait_send()

        if k == 1:
            relay_copy(1, 0, 0, pair).wait_send()
            relay_copy(1, 0, 1, pair).wait_send()
        if k == 3:

            @pl.when(mid & (p < z))
            def _():
                diag_up(p).wait_send()

            @pl.when(mid & (p > z))
            def _():
                diag_down(p).wait_send()

            @pl.when(mid)
            def _():
                relay_copy(3, 2, 0, middle).wait_send()
                relay_copy(3, 2, 1, middle).wait_send()

            @pl.when(low_z == 0)
            def _():
                relay_copy(3, 1, 0, pair).wait_send()
                relay_copy(3, 1, 1, pair).wait_send()

        for h in (0, 1):
            x_copy(k, h).wait_send()
            y_copy(k, h).wait_send()
            g_x(p, x, h).wait_send()
            g_y(p, y, h).wait_send()

            @pl.when((p <= z) & (z < 3))
            def _():
                g_up(p, h).wait_send()

            @pl.when((p >= z) & (z > 0))
            def _():
                g_down(p, h).wait_send()

            if k > 0:

                @pl.when(p > z)
                def _():
                    up_copy(p, h).wait_send()

                @pl.when(p < z)
                def _():
                    down_copy(p, h).wait_send()


def mixture_kernel(sent, w_in, w_down):
    rows, full = sent.shape
    width, model = w_down.shape
    kind = sent.dtype
    line = pltpu.VMEM((4, rows, model), kind)
    halves = pltpu.VMEM((4, rows // 2, model), kind)
    return pl.pallas_call(
        moe_kernel,
        out_shape=jax.ShapeDtypeStruct((rows, model), jnp.float32),
        in_specs=[
            pl.BlockSpec(memory_space=pltpu.VMEM),
            pl.BlockSpec(memory_space=pl.ANY),
            pl.BlockSpec(memory_space=pl.ANY),
        ],
        out_specs=pl.BlockSpec(memory_space=pltpu.VMEM),
        scratch_shapes=[
            pltpu.VMEM((4, 2, 2, 2, rows, full), kind),
            pltpu.VMEM((width, 2, model), kind),
            pltpu.VMEM((2, width, model), kind),
            pltpu.VMEM((width, model), kind),
            pltpu.VMEM((8 * rows, width), kind),
            pltpu.VMEM((8 * rows, 1), jnp.float32),
            pltpu.VMEM((4, 2, 2, 2, rows, model), kind),
            pltpu.VMEM((4, 2, 2, rows, model), kind),
            pltpu.VMEM((4, 2, 2, rows, model), kind),
            halves,
            halves,
            line,
            line,
            line,
            line,
            line,
            pltpu.VMEM((3, rows, model), kind),
            pltpu.SemaphoreType.DMA((2,)),
            pltpu.SemaphoreType.DMA((16, 4)),
            pltpu.SemaphoreType.DMA((16, 4)),
            pltpu.SemaphoreType.DMA((13, 4)),
            pltpu.SemaphoreType.DMA((13, 4)),
        ],
        compiler_params=pltpu.CompilerParams(
            collective_id=0, has_side_effects=True, vmem_limit_bytes=58 * 2**20
        ),
    )(sent, w_in, w_down)


def attend_kernel(
    table_ref,
    length_ref,
    nope_ref,
    rope_ref,
    new_ref,
    new_rope_ref,
    pages_ref,
    pages_rope_ref,
    residual_ref,
    gain_ref,
    gates_ref,
    key_up_ref,
    value_up_ref,
    out_weight_ref,
    sent_ref,
    hidden_ref,
    keys,
    keys_rope,
    key_up,
    value_up,
    out_weight,
    residual,
    query_lat,
    query_rope,
    scores,
    heads_out,
    partial,
    arrived,
    loads,
    sends,
    recvs,
):
    x = lax.axis_index("dp")
    other_x = {"dp": 1 - x}
    heads = key_up.shape[0]
    tokens = nope_ref.shape[0]
    held = pages_ref.shape[0]
    rows, model = hidden_ref.shape
    chunks, piece = partial.shape[0], partial.shape[2]
    span = 2 * held
    scale = 1.0 / (HD + RD) ** 0.5
    nt = (((1,), (1,)), ((), ()))

    def remote(src, dst, k):
        return pltpu.make_async_remote_copy(
            src_ref=src,
            dst_ref=dst,
            send_sem=sends.at[k],
            recv_sem=recvs.at[k],
            device_id=other_x,
            device_id_type=pl.DeviceIdType.MESH,
        )

    mine = [
        pltpu.make_async_copy(key_up_ref, key_up, loads.at[0]),
        pltpu.make_async_copy(pages_ref, keys.at[pl.ds(0, held)], loads.at[1]),
        pltpu.make_async_copy(value_up_ref, value_up, loads.at[2]),
        pltpu.make_async_copy(out_weight_ref, out_weight, loads.at[3]),
        pltpu.make_async_copy(residual_ref.at[pl.ds(x * rows, rows)], residual, loads.at[4]),
    ]
    far_keys = remote(pages_ref, keys.at[pl.ds(held + tokens, held)], 0)
    far_rope = remote(pages_rope_ref, keys_rope.at[pl.ds(held, held)], 1)
    barrier = pltpu.get_barrier_semaphore()
    pl.semaphore_signal(barrier, inc=1, device_id=other_x, device_id_type=pl.DeviceIdType.MESH)
    for load in mine:
        load.start()
    pl.semaphore_wait(barrier, 1)
    far_keys.start()
    far_rope.start()
    keys[pl.ds(held, tokens)] = new_ref[...]
    keys_rope[pl.ds(0, held)] = pages_rope_ref[...]

    def bias(start):
        place = lax.broadcasted_iota(jnp.int32, (8, held), 1) + start
        slot, offset = place // PAGE, place % PAGE
        seen = jnp.zeros((8, held), jnp.int32)
        for j in range(span // PAGE):
            seen += jnp.where(
                (slot == table_ref[0, j]) & (offset + j * PAGE < length_ref[0]), 1, 0
            )
        return jnp.where(seen > 0, 0.0, NEG)[0:1]

    mine[0].wait()
    for h in range(heads):
        query_lat[pl.ds(h * tokens, tokens)] = jnp.dot(
            nope_ref[:, pl.ds(h * HD, HD)], key_up[h], preferred_element_type=jnp.float32
        ).astype(query_lat.dtype)
        query_rope[pl.ds(h * tokens, tokens)] = rope_ref[:, pl.ds(h * RD, RD)]
    mine[1].wait()

    def against(lo, n, rope_keys, dims):
        return (
            lax.dot_general(
                query_lat[...], keys[pl.ds(lo, n)], nt, preferred_element_type=jnp.float32
            )
            + lax.dot_general(query_rope[...], rope_keys, dims, preferred_element_type=jnp.float32)
        ) * scale

    scores[:, pl.ds(0, held)] = against(0, held, keys_rope[pl.ds(0, held)], nt) + bias(x * held)
    fresh = against(held, tokens, new_rope_ref[...], (((1,), (0,)), ((), ())))
    seen = lax.broadcasted_iota(jnp.int32, (tokens, tokens), 1) <= lax.broadcasted_iota(
        jnp.int32, (tokens, tokens), 0
    )
    causal = jnp.where(seen, 0.0, NEG)
    scores[:, pl.ds(held, tokens)] = (
        fresh.reshape(heads, tokens, tokens) + causal[None]
    ).reshape(heads * tokens, tokens)
    far_keys.wait_recv()
    far_rope.wait_recv()
    scores[:, pl.ds(held + tokens, held)] = against(
        held + tokens, held, keys_rope[pl.ds(held, held)], nt
    ) + bias((1 - x) * held)
    mine[2].wait()
    for h in range(heads):
        masked = scores[pl.ds(h * tokens, tokens)]
        expo = jnp.exp(masked - jnp.max(masked, axis=1, keepdims=True))
        total = jnp.sum(expo, axis=1, keepdims=True)
        attn = jnp.dot(expo.astype(keys.dtype), keys[...], preferred_element_type=jnp.float32)
        heads_out[:, pl.ds(h * HD, HD)] = jnp.dot(
            (attn / total).astype(keys.dtype), value_up[h], preferred_element_type=jnp.float32
        ).astype(heads_out.dtype)
    mine[3].wait()

    def exchange(n):
        return remote(partial.at[n, pl.ds((1 - x) * rows, rows)], arrived.at[n], 2 + n)

    for n in range(chunks):
        partial[n] = jnp.dot(
            heads_out[...],
            out_weight[:, pl.ds(n * piece, piece)],
            preferred_element_type=jnp.float32,
        ).astype(partial.dtype)
        exchange(n).start()
    mine[4].wait()
    sent_ref[:, pl.ds(model, gates_ref.shape[1])] = gates_ref[...]
    power = jnp.zeros((rows, 1), jnp.float32)
    for n in range(chunks):
        exchange(n).wait_recv()
        at = pl.ds(n * piece, piece)
        hidden = (
            residual[:, at].astype(jnp.float32)
            + partial[n, pl.ds(x * rows, rows)].astype(jnp.float32)
            + arrived[n].astype(jnp.float32)
        )
        hidden_ref[:, at] = hidden
        power += jnp.sum(hidden * hidden, axis=1, keepdims=True)
    factor = lax.rsqrt(power / model + EPS)
    for n in range(chunks):
        at = pl.ds(n * piece, piece)
        sent_ref[:, at] = (hidden_ref[:, at] * factor * gain_ref[:, at]).astype(sent_ref.dtype)
    far_keys.wait_send()
    far_rope.wait_send()
    for n in range(chunks):
        exchange(n).wait_send()


def attend(
    table,
    length,
    nope,
    rope,
    new,
    new_rope,
    pages,
    pages_rope,
    residual,
    gain,
    gates,
    key_up,
    value_up,
    out_weight,
):
    kind = nope.dtype
    heads = key_up.shape[0]
    tokens, model = residual.shape
    rows = tokens // 2
    held = pages.shape[0]
    chunks = 4
    vmem = pl.BlockSpec(memory_space=pltpu.VMEM)
    smem = pl.BlockSpec(memory_space=pltpu.SMEM)
    far = pl.BlockSpec(memory_space=pl.ANY)
    return pl.pallas_call(
        attend_kernel,
        out_shape=(
            jax.ShapeDtypeStruct((rows, model + gates.shape[1]), kind),
            jax.ShapeDtypeStruct((rows, model), jnp.float32),
        ),
        in_specs=[smem, smem, vmem, vmem, vmem, vmem, far, vmem, far, vmem, vmem, far, far, far],
        out_specs=(vmem, vmem),
        scratch_shapes=[
            pltpu.VMEM((2 * held + tokens, LAT), kind),
            pltpu.VMEM((2 * held, RD), kind),
            pltpu.VMEM(key_up.shape, kind),
            pltpu.VMEM(value_up.shape, kind),
            pltpu.VMEM(out_weight.shape, kind),
            pltpu.VMEM((rows, model), kind),
            pltpu.VMEM((heads * tokens, LAT), kind),
            pltpu.VMEM((heads * tokens, RD), kind),
            pltpu.VMEM((heads * tokens, 2 * held + tokens), jnp.float32),
            pltpu.VMEM((tokens, heads * HD), kind),
            pltpu.VMEM((chunks, tokens, model // chunks), kind),
            pltpu.VMEM((chunks, rows, model // chunks), kind),
            pltpu.SemaphoreType.DMA((5,)),
            pltpu.SemaphoreType.DMA((2 + chunks,)),
            pltpu.SemaphoreType.DMA((2 + chunks,)),
        ],
        compiler_params=pltpu.CompilerParams(
            collective_id=1, has_side_effects=True, vmem_limit_bytes=62 * 2**20
        ),
    )(
        table,
        length,
        nope,
        rope,
        new,
        new_rope,
        pages,
        pages_rope,
        residual,
        gain,
        gates,
        key_up,
        value_up,
        out_weight,
    )


def per_device(
    query_nope,
    query_rope,
    latent_new,
    key_rope,
    latent_pages,
    rope_pages,
    page_table,
    prefix_lengths,
    residual,
    key_up,
    value_up,
    out_weight,
    norm_gain,
    expert_in,
    expert_down,
    expert_ids,
    expert_weights,
):
    groups = lax.axis_size("dp")
    experts_all = lax.axis_size("expert") * expert_in.shape[0]
    tokens_col = query_nope.shape[1]
    block_rows = tokens_col // groups
    heads_here = key_up.shape[0]
    fits = groups == 2 and lax.axis_size("expert") == 16
    start = lax.axis_index("dp") * block_rows
    ids_mine = lax.dynamic_slice_in_dim(expert_ids[0], start, block_rows, 0)
    weights_mine = lax.dynamic_slice_in_dim(expert_weights[0], start, block_rows, 0)
    gates = jnp.sum(
        jnp.where(
            ids_mine[:, :, None] == jnp.arange(experts_all)[None, None, :],
            weights_mine[:, :, None],
            0.0,
        ),
        axis=1,
    )
    gates_high = gates.astype(jnp.bfloat16)
    gates_low = (gates - gates_high.astype(jnp.float32)).astype(jnp.bfloat16)
    model = residual.shape[2]
    extra = -(-2 * experts_all // 128) * 128
    fill = jnp.zeros((block_rows, extra - 2 * experts_all), jnp.bfloat16)
    coded = jnp.concatenate([gates_high, gates_low, fill], axis=1)
    if fits:
        sent, hidden_mine = attend(
            page_table,
            prefix_lengths,
            query_nope[0],
            query_rope[0],
            latent_new[0],
            jnp.transpose(key_rope[0]),
            latent_pages[0].reshape(-1, LAT),
            rope_pages[0].reshape(-1, RD),
            residual[0],
            norm_gain[None],
            coded,
            key_up,
            value_up,
            out_weight,
        )
        mixture = mixture_kernel(sent, expert_in[0], expert_down[0])
    else:
        pages_lat, pages_rope = (
            lax.all_gather(latent_pages[0], "dp", axis=0, tiled=True),
            lax.all_gather(rope_pages[0], "dp", axis=0, tiled=True),
        )
        page_count = pages_lat.shape[0]
        table = page_table[0]
        inverse = jnp.sum(
            jnp.where(
                table[:, None] == jnp.arange(page_count)[None, :], jnp.arange(page_count)[:, None], 0
            ),
            axis=0,
        )
        positions = (inverse[:, None] * PAGE + jnp.arange(PAGE)[None, :]).reshape(-1)
        prefix_ok = positions < prefix_lengths[0]
        keys_lat = jnp.concatenate([pages_lat.reshape(-1, LAT), latent_new[0]], axis=0)
        keys_rope = jnp.concatenate([pages_rope.reshape(-1, RD), key_rope[0]], axis=0)
        heads_nope = query_nope[0].reshape(tokens_col, heads_here, HD)
        query_lat = jnp.einsum(
            "thd,hdc->thc", heads_nope, key_up, preferred_element_type=jnp.float32
        ).astype(jnp.bfloat16)
        heads_rope = query_rope[0].reshape(tokens_col, heads_here, RD)
        scale = 1.0 / (HD + RD) ** 0.5
        scores = (
            jnp.einsum("thc,kc->thk", query_lat, keys_lat, preferred_element_type=jnp.float32)
            + jnp.einsum("thr,kr->thk", heads_rope, keys_rope, preferred_element_type=jnp.float32)
        ) * scale
        causal = jnp.arange(tokens_col)[None, :] <= jnp.arange(tokens_col)[:, None]
        allowed = jnp.concatenate(
            [jnp.broadcast_to(prefix_ok[None, :], (tokens_col, prefix_ok.shape[0])), causal], axis=1
        )[:, None, :]
        masked = jnp.where(allowed, scores, NEG)
        peak = jnp.max(masked, axis=-1, keepdims=True)
        expo = jnp.where(allowed, jnp.exp(masked - peak), 0.0)
        total = jnp.sum(expo, axis=-1, keepdims=True)
        probs = expo.astype(jnp.bfloat16)
        attn_latent = (
            jnp.einsum("thk,kc->thc", probs, keys_lat, preferred_element_type=jnp.float32) / total
        ).astype(jnp.bfloat16)
        heads_out = jnp.einsum(
            "thc,hcd->thd", attn_latent, value_up, preferred_element_type=jnp.float32
        ).astype(jnp.bfloat16)
        partial_out = jnp.dot(
            heads_out.reshape(tokens_col, heads_here * HD),
            out_weight,
            preferred_element_type=jnp.float32,
        )
        attended = lax.psum_scatter(
            partial_out.astype(jnp.bfloat16), "dp", scatter_dimension=0, tiled=True
        ).astype(jnp.float32)
        hidden_mine = (
            lax.dynamic_slice_in_dim(residual[0], start, block_rows, 0).astype(jnp.float32) + attended
        )
        normed = norm_rows(hidden_mine, norm_gain)
        sent = jnp.concatenate([normed, coded], axis=1)
        gathered = lax.all_gather(sent, ("expert", "dp"), axis=0, tiled=True)
        everyone = gathered[:, :model]
        mine = lax.axis_index("expert")
        named = (jnp.arange(extra) == mine) | (jnp.arange(extra) == mine + experts_all)
        gate = jnp.sum(
            jnp.where(named[None, :], gathered[:, model:].astype(jnp.float32), 0.0),
            axis=1,
            keepdims=True,
        )
        part = expert_apply(everyone, gate, expert_in, expert_down)
        mixture = lax.psum_scatter(
            part, ("expert", "dp"), scatter_dimension=0, tiled=True
        ).astype(jnp.float32)
    layer_out = (hidden_mine + mixture).astype(jnp.bfloat16)[None]
    return (layer_out, mixture.astype(jnp.bfloat16)[None])


def solution(mesh):
    return jax.shard_map(
        per_device,
        mesh=mesh,
        in_specs=(
            P("expert", None, "dp"),
            P("expert", None, "dp"),
            P("expert", None, None),
            P("expert", None, None),
            P("expert", "dp", None, None),
            P("expert", "dp", None),
            P("expert", None),
            P("expert"),
            P("expert", None, None),
            P("dp", None, None),
            P("dp", None, None),
            P("dp", None),
            P(),
            P("expert", "dp", None, None),
            P("expert", "dp", None),
            P("expert", None, None),
            P("expert", None, None),
        ),
        out_specs=(P("expert", "dp", None), P("expert", "dp", None)),
        check_vma=False,
    )
```

```python
import functools

import jax
import jax.numpy as jnp
from jax import lax
from jax.experimental import pallas as pl
from jax.experimental.pallas import tpu as pltpu
from jax.sharding import PartitionSpec as P

HD = 128
RD = 64
LAT = 512
TOP = 6
PAGE = 64


EPS = 1e-06
NEG = -1e30


def norm_rows(hidden, norm_gain):
    power = jnp.mean(hidden * hidden, axis=-1, keepdims=True)
    return (hidden * lax.rsqrt(power + EPS) * norm_gain).astype(jnp.bfloat16)


def expert_apply(tokens, gate, expert_in, expert_down):
    flat = tokens.reshape(-1, tokens.shape[-1])
    dims = (((1,), (1,)), ((), ()))
    gate_act = lax.dot_general(
        flat, expert_in[0, :, 0, :], dims, preferred_element_type=jnp.float32
    )
    up_act = lax.dot_general(flat, expert_in[0, :, 1, :], dims, preferred_element_type=jnp.float32)
    units = (jax.nn.silu(gate_act) * up_act).astype(jnp.bfloat16)
    part = jnp.dot(units, expert_down[0], preferred_element_type=jnp.float32)
    return (part * gate).astype(jnp.bfloat16)


def moe_kernel(
    sent_ref,
    w_in_ref,
    w_down_ref,
    out_ref,
    tok,
    raw,
    w_in,
    w_down,
    units,
    gate,
    part,
    core_in,
    acc,
    diag_x,
    diag_y,
    from_x,
    from_y,
    z_send,
    z_up,
    z_down,
    relay,
    w_sems,
    g_sends,
    g_recvs,
    sends,
    recvs,
):
    x = lax.axis_index("dp")
    e = lax.axis_index("expert")
    z, y, c = e // 4, (e // 2) % 2, e % 2
    rows, model = out_ref.shape
    half = rows // 2
    width = w_down_ref.shape[0]
    high = z // 2
    low_z = z + high * (3 - 2 * z)
    mid = low_z == 1

    def flip(f):
        return f + high * (3 - 2 * f)

    planes = [z, flip(1 - low_z), flip(3 + 0 * z), flip(2 + 0 * z)]
    other_core = {"expert": e + 1 - 2 * c}
    other_y = {"expert": e + 2 - 4 * y}
    other_x = {"dp": 1 - x}
    above, below = {"expert": e + 4}, {"expert": e - 4}
    pair, middle = {"expert": e + 4 - 8 * (z % 2)}, {"expert": e + 4 * (3 - 2 * z)}
    halves = first, second = pl.ds(0, half), pl.ds(half, half)

    def remote(src, dst, send, recv, to):
        return pltpu.make_async_remote_copy(
            src_ref=src,
            dst_ref=dst,
            send_sem=send,
            recv_sem=recv,
            device_id=to,
            device_id_type=pl.DeviceIdType.MESH,
        )

    def same(ref, kind, p, to):
        return remote(ref, ref, g_sends.at[kind, p], g_recvs.at[kind, p], to)

    def g_up(p, h):
        return same(tok.at[p, y, c, x, halves[h]], h, p, above)

    def g_down(p, h):
        return same(tok.at[p, y, c, x, halves[h]], 2 + h, p, below)

    def g_x(p, i, h):
        return same(tok.at[p, y, c, i, halves[h]], 4 + h, p, other_x)

    def g_y(p, j, h):
        return same(tok.at[p, j, c, x, halves[h]], 6 + h, p, other_y)

    def g_diag_x(p, j):
        return same(tok.at[p, j, c, x, first], 8, p, other_x)

    def g_diag_y(p, i):
        return same(tok.at[p, y, c, i, second], 9, p, other_y)

    def g_core(p, kind, cc):
        j, i = (y, y, 1 - y, 1 - y)[kind], (x, 1 - x, x, 1 - x)[kind]
        return same(tok.at[p, j, cc, i], 10 + kind, p, other_core)

    def own_line(p):
        g_x(p, x, 1).start()
        g_y(p, y, 0).start()
        g_x(p, x, 0).start()
        g_y(p, y, 1).start()
        g_core(p, 0, c).start()

    def along_z(p, h):
        @pl.when(p < z)
        def _():
            g_up(p, h).wait_recv()

            @pl.when(z < 3)
            def _():
                g_up(p, h).start()

        @pl.when(p > z)
        def _():
            g_down(p, h).wait_recv()

            @pl.when(z > 0)
            def _():
                g_down(p, h).start()

    def beside_send(p):
        g_x(p, 1 - x, 1).wait_recv()
        g_diag_y(p, 1 - x).start()
        g_y(p, 1 - y, 0).wait_recv()
        g_diag_x(p, 1 - y).start()

    def beside_rest(p, diag=True):
        if not diag:
            g_x(p, 1 - x, 1).wait_recv()
            g_y(p, 1 - y, 0).wait_recv()
        g_x(p, 1 - x, 0).wait_recv()
        g_core(p, 1, c).start()
        g_y(p, 1 - y, 1).wait_recv()
        g_core(p, 2, c).start()

    def across(p):
        same(tok.at[p, 1 - y, c, 1 - x, first], 8, p, other_x).wait_recv()
        same(tok.at[p, 1 - y, c, 1 - x, second], 9, p, other_y).wait_recv()
        g_core(p, 3, c).start()

    def diag_up(p):
        return same(tok.at[p, 1 - y, c, 1 - x], 14, p, above)

    def diag_down(p):
        return same(tok.at[p, 1 - y, c, 1 - x], 15, p, below)

    def diag_out():
        @pl.when(z == 1)
        def _():
            diag_up(z).start()

        @pl.when(z == 2)
        def _():
            diag_down(z).start()

    def diag_in(p, forward):
        @pl.when(p < z)
        def _():
            diag_up(p).wait_recv()
            if forward:

                @pl.when(mid)
                def _():
                    diag_up(p).start()

        @pl.when(p > z)
        def _():
            diag_down(p).wait_recv()
            if forward:

                @pl.when(mid)
                def _():
                    diag_down(p).start()

        g_core(p, 3, c).start()

    def whole(p):
        for kind in range(4):
            g_core(p, kind, 1 - c).wait_recv()

    def tokens(p):
        return tok[p, :, :, :, :, pl.ds(0, model)].reshape(8 * rows, model)

    def hidden(p, lo, n):
        dims = (((1,), (1,)), ((), ()))
        values = tokens(p)
        gate_act = lax.dot_general(
            values, w_in[0, pl.ds(lo, n)], dims, preferred_element_type=jnp.float32
        )
        up_act = lax.dot_general(
            values, w_in[1, pl.ds(lo, n)], dims, preferred_element_type=jnp.float32
        )
        units[:, pl.ds(lo, n)] = (gate_act / (1.0 + jnp.exp(-gate_act)) * up_act).astype(
            units.dtype
        )

    def gates(p):
        extra = tok.shape[5] - model
        lanes = lax.broadcasted_iota(jnp.int32, (8 * rows, extra), 1)
        named = (lanes == e) | (lanes == e + lax.axis_size("expert"))
        values = tok[p, :, :, :, :, pl.ds(model, extra)].reshape(8 * rows, extra)
        gate[...] = jnp.sum(
            jnp.where(named, values.astype(jnp.float32), 0.0), axis=1, keepdims=True
        )

    def project(p, lo, n):
        value = jnp.dot(units[...], w_down[:, pl.ds(lo, n)], preferred_element_type=jnp.float32)
        part[p, :, :, :, :, pl.ds(lo, n)] = (
            (value * gate[...]).astype(part.dtype).reshape(2, 2, 2, rows, n)
        )

    def compute(p, between):
        steps = [functools.partial(hidden, p, lo, min(256, width - lo)) for lo in range(0, width, 256)]
        steps += [functools.partial(gates, p)]
        steps += [functools.partial(project, p, lo, 256) for lo in range(0, model, 256)]
        for number, step in enumerate(steps):
            step()
            for act in between.get(number, ()):
                act()

    def copy(src, dst, kind, k, to):
        return remote(src, dst, sends.at[kind, k], recvs.at[kind, k], to)

    def core_copy(k):
        return copy(part.at[planes[k], :, 1 - c], core_in.at[k], 0, k, other_core)

    def diag_y_copy(k):
        return copy(acc.at[k, 1 - y, 1 - x, first], diag_y.at[k], 1, k, other_y)

    def diag_x_copy(k):
        return copy(acc.at[k, 1 - y, 1 - x, second], diag_x.at[k], 2, k, other_x)

    def x_copy(k, h):
        return copy(acc.at[k, y, 1 - x, halves[h]], from_x.at[k, halves[h]], 3 + h, k, other_x)

    def y_copy(k, h):
        return copy(acc.at[k, 1 - y, x, halves[h]], from_y.at[k, halves[h]], 5 + h, k, other_y)

    def up_copy(g, h):
        return copy(z_send.at[g, halves[h]], z_up.at[g, halves[h]], 7 + h, g, above)

    def down_copy(g, h):
        return copy(z_send.at[g, halves[h]], z_down.at[g, halves[h]], 9 + h, g, below)

    def wide(value):
        return value.astype(jnp.float32)

    def relay_copy(k, slot, h, to):
        return copy(
            acc.at[k, 1 - y, 1 - x, halves[h]], relay.at[slot, halves[h]], 11 + h, slot, to
        )

    def add_relay(k, slot, h):
        at = halves[h]
        relay_copy(k, slot, h, pair).wait_recv()
        acc[k, 1 - y, 1 - x, at] = (wide(acc[k, 1 - y, 1 - x, at]) + wide(relay[slot, at])).astype(
            acc.dtype
        )

    def add_core(k, j, i):
        acc[k, j, i] = (wide(part[planes[k], j, c, i]) + wide(core_in[k, j, i])).astype(acc.dtype)

    def stage_a(k):
        core_copy(k).wait_recv()
        add_core(k, 1 - y, 1 - x)
        if k == 1:
            relay_copy(1, 0, 0, pair).start()
            relay_copy(1, 0, 1, pair).start()
        if k == 2:
            diag_y_copy(k).start()
            diag_x_copy(k).start()
        if k == 3:

            @pl.when(low_z == 0)
            def _():
                relay_copy(3, 1, 0, pair).start()
                relay_copy(3, 1, 1, pair).start()

        add_core(k, y, 1 - x)
        x_copy(k, 1).start()
        if k % 2 == 1:
            x_copy(k, 0).start()
        add_core(k, 1 - y, x)
        y_copy(k, 0).start()
        if k % 2 == 1:
            y_copy(k, 1).start()
        add_core(k, y, x)
        if k == 3:

            @pl.when(mid)
            def _():
                for h in (0, 1):
                    add_relay(3, 1, h)
                    relay_copy(3, 2, h, middle).start()

    def own_diag():
        for h in (0, 1):
            add_relay(0, 0, h)

            @pl.when(mid)
            def _():
                add_relay(0, 2, h)

            (diag_y_copy, diag_x_copy)[h](0).start()

    def stage_b(k):
        diag_y_copy(k).wait_recv()
        acc[k, y, 1 - x, first] = (wide(acc[k, y, 1 - x, first]) + wide(diag_y[k])).astype(acc.dtype)
        x_copy(k, 0).start()
        diag_x_copy(k).wait_recv()
        acc[k, 1 - y, x, second] = (wide(acc[k, 1 - y, x, second]) + wide(diag_x[k])).astype(
            acc.dtype
        )
        y_copy(k, 1).start()

    def stage_c(k, g, last=False):
        for h in (0, 1):
            at = halves[h]
            x_copy(k, h).wait_recv()
            y_copy(k, h).wait_recv()
            out_ref[at] = wide(acc[k, y, x, at]) + wide(from_x[k, at]) + wide(from_y[k, at])

            @pl.when((g >= z) & (z > 0))
            def _():
                up_copy(g, h).wait_recv()
                out_ref[at] += wide(z_up[g, at])

            @pl.when((g <= z) & (z < 3))
            def _():
                down_copy(g, h).wait_recv()
                out_ref[at] += wide(z_down[g, at])

            if not last:
                z_send[g, at] = out_ref[at].astype(z_send.dtype)

                @pl.when(g > z)
                def _():
                    up_copy(g, h).start()

                @pl.when(g < z)
                def _():
                    down_copy(g, h).start()

    load_in = pltpu.make_async_copy(w_in_ref, raw, w_sems.at[0])

    def untangle(lo, n):
        for at in range(lo, lo + n, 64):
            pairs = raw[pl.ds(at, 64)].reshape(128, model)
            row = lax.broadcasted_iota(jnp.int32, (128, 128), 0)
            column = lax.broadcasted_iota(jnp.int32, (128, 128), 1)
            order = jnp.where(column == 2 * (row % 64) + row // 64, 1.0, 0.0).astype(raw.dtype)
            sorted_rows = jnp.dot(order, pairs, preferred_element_type=jnp.float32).astype(raw.dtype)
            w_in[0, pl.ds(at, 64)] = sorted_rows[:64]
            w_in[1, pl.ds(at, 64)] = sorted_rows[64:]

    load_down = pltpu.make_async_copy(w_down_ref, w_down, w_sems.at[1])
    barrier = pltpu.get_barrier_semaphore()
    for to in (other_core, other_x, other_y):
        pl.semaphore_signal(barrier, inc=1, device_id=to, device_id_type=pl.DeviceIdType.MESH)

    @pl.when(z > 0)
    def _():
        pl.semaphore_signal(barrier, inc=1, device_id=below, device_id_type=pl.DeviceIdType.MESH)

    @pl.when(z < 3)
    def _():
        pl.semaphore_signal(barrier, inc=1, device_id=above, device_id_type=pl.DeviceIdType.MESH)

    load_in.start()
    load_down.start()
    tok[z, y, c, x] = sent_ref[...]
    pl.semaphore_wait(barrier, 4 + ((z + 1) // 2) % 2)

    for h in (0, 1):

        @pl.when(z < 3)
        def _():
            g_up(z, h).start()

        @pl.when(z > 0)
        def _():
            g_down(z, h).start()

    def do(f, *args):
        return functools.partial(f, *args)

    def at_mid(*acts):
        @pl.when(mid)
        def _():
            for act in acts:
                act()

    def at_end(*acts):
        @pl.when(low_z == 0)
        def _():
            for act in acts:
                act()

    def start_core(k):
        core_copy(k).start()

    own_line(z)
    load_in.wait()
    untangle(0, 256)
    along_z(planes[1], 0)
    at_mid(do(along_z, planes[3], 0))
    beside_send(planes[0])
    along_z(planes[1], 1)
    at_mid(do(along_z, planes[3], 1))
    own_line(planes[1])
    beside_rest(planes[0])
    untangle(256, 256)
    across(planes[0])
    at_mid(do(along_z, planes[2], 0), do(diag_out), do(along_z, planes[2], 1))
    beside_send(planes[1])
    at_mid(do(own_line, planes[2]))
    untangle(512, 192)
    load_down.wait()
    whole(planes[0])
    compute(
        planes[0],
        {
            2: [do(at_end, do(along_z, planes[3], 0), do(along_z, planes[3], 1))],
            5: [do(beside_rest, planes[1])],
            9: [
                do(at_end, do(along_z, planes[2], 0), do(along_z, planes[2], 1)),
                do(at_end, do(own_line, planes[2])),
            ],
        },
    )
    start_core(0)
    across(planes[1])
    at_mid(do(diag_in, planes[3], True))
    whole(planes[1])
    compute(
        planes[1],
        {
            2: [do(beside_send, planes[2]), do(own_line, planes[3])],
            7: [do(beside_rest, planes[2])],
        },
    )
    start_core(1)
    across(planes[2])
    stage_a(0)
    whole(planes[2])
    compute(
        planes[2],
        {
            2: [do(stage_a, 1)],
            6: [do(at_end, do(diag_in, planes[3], False))],
            9: [do(beside_rest, planes[3], False)],
        },
    )
    start_core(2)
    whole(planes[3])
    compute(
        planes[3],
        {
            2: [do(stage_a, 2)],
            7: [do(at_end, do(stage_c, 1, planes[1]))],
            11: [do(stage_b, 2)],
        },
    )
    start_core(3)
    at_end(own_diag)
    stage_a(3)
    stage_c(2, planes[2])
    at_mid(own_diag)
    at_mid(do(stage_c, 1, planes[1]))
    stage_b(0)
    stage_c(3, planes[3])
    stage_c(0, planes[0], True)

    for k in range(4):
        p = planes[k]
        core_copy(k).wait_send()
        if k % 2 == 0:
            diag_y_copy(k).wait_send()
            diag_x_copy(k).wait_send()
        if k < 3:
            g_diag_y(p, 1 - x).wait_send()
            g_diag_x(p, 1 - y).wait_send()
        for kind in range(4):
            g_core(p, kind, c).wait_send()
        if k == 0:

            @pl.when(z == 1)
            def _():
                diag_up(p).wait_send()

            @pl.when(z == 2)
            def _():
                diag_down(p).wait_send()

        if k == 1:
            relay_copy(1, 0, 0, pair).wait_send()
            relay_copy(1, 0, 1, pair).wait_send()
        if k == 3:

            @pl.when(mid & (p < z))
            def _():
                diag_up(p).wait_send()

            @pl.when(mid & (p > z))
            def _():
                diag_down(p).wait_send()

            @pl.when(mid)
            def _():
                relay_copy(3, 2, 0, middle).wait_send()
                relay_copy(3, 2, 1, middle).wait_send()

            @pl.when(low_z == 0)
            def _():
                relay_copy(3, 1, 0, pair).wait_send()
                relay_copy(3, 1, 1, pair).wait_send()

        for h in (0, 1):
            x_copy(k, h).wait_send()
            y_copy(k, h).wait_send()
            g_x(p, x, h).wait_send()
            g_y(p, y, h).wait_send()

            @pl.when((p <= z) & (z < 3))
            def _():
                g_up(p, h).wait_send()

            @pl.when((p >= z) & (z > 0))
            def _():
                g_down(p, h).wait_send()

            if k > 0:

                @pl.when(p > z)
                def _():
                    up_copy(p, h).wait_send()

                @pl.when(p < z)
                def _():
                    down_copy(p, h).wait_send()


def mixture_kernel(sent, w_in, w_down):
    rows, full = sent.shape
    width, model = w_down.shape
    kind = sent.dtype
    line = pltpu.VMEM((4, rows, model), kind)
    halves = pltpu.VMEM((4, rows // 2, model), kind)
    return pl.pallas_call(
        moe_kernel,
        out_shape=jax.ShapeDtypeStruct((rows, model), jnp.float32),
        in_specs=[
            pl.BlockSpec(memory_space=pltpu.VMEM),
            pl.BlockSpec(memory_space=pl.ANY),
            pl.BlockSpec(memory_space=pl.ANY),
        ],
        out_specs=pl.BlockSpec(memory_space=pltpu.VMEM),
        scratch_shapes=[
            pltpu.VMEM((4, 2, 2, 2, rows, full), kind),
            pltpu.VMEM((width, 2, model), kind),
            pltpu.VMEM((2, width, model), kind),
            pltpu.VMEM((width, model), kind),
            pltpu.VMEM((8 * rows, width), kind),
            pltpu.VMEM((8 * rows, 1), jnp.float32),
            pltpu.VMEM((4, 2, 2, 2, rows, model), kind),
            pltpu.VMEM((4, 2, 2, rows, model), kind),
            pltpu.VMEM((4, 2, 2, rows, model), kind),
            halves,
            halves,
            line,
            line,
            line,
            line,
            line,
            pltpu.VMEM((3, rows, model), kind),
            pltpu.SemaphoreType.DMA((2,)),
            pltpu.SemaphoreType.DMA((16, 4)),
            pltpu.SemaphoreType.DMA((16, 4)),
            pltpu.SemaphoreType.DMA((13, 4)),
            pltpu.SemaphoreType.DMA((13, 4)),
        ],
        compiler_params=pltpu.CompilerParams(
            collective_id=0, has_side_effects=True, vmem_limit_bytes=58 * 2**20
        ),
    )(sent, w_in, w_down)


def attend_kernel(
    table_ref,
    length_ref,
    nope_in,
    rope_in,
    new_in,
    new_rope_ref,
    pages_ref,
    pages_rope_ref,
    residual_ref,
    gain_ref,
    ids_ref,
    weights_ref,
    key_up_ref,
    value_up_ref,
    out_weight_ref,
    sent_ref,
    hidden_ref,
    keys,
    keys_rope,
    key_up,
    value_up,
    out_weight,
    residual,
    query_lat,
    query_rope,
    scores,
    far_scores,
    near,
    near_peak,
    near_total,
    coded,
    nope_ref,
    rope_ref,
    heads_out,
    partial,
    arrived,
    loads,
    sends,
    recvs,
):
    x = lax.axis_index("dp")
    other_x = {"dp": 1 - x}
    heads = key_up.shape[0]
    tokens = nope_in.shape[0]
    held = pages_ref.shape[0]
    rows, model = hidden_ref.shape
    chunks, piece = partial.shape[0], partial.shape[2]
    span = 2 * held
    scale = 1.0 / (HD + RD) ** 0.5
    nt = (((1,), (1,)), ((), ()))

    def remote(src, dst, k):
        return pltpu.make_async_remote_copy(
            src_ref=src,
            dst_ref=dst,
            send_sem=sends.at[k],
            recv_sem=recvs.at[k],
            device_id=other_x,
            device_id_type=pl.DeviceIdType.MESH,
        )

    mine = [
        pltpu.make_async_copy(key_up_ref, key_up, loads.at[0]),
        pltpu.make_async_copy(pages_ref, keys.at[pl.ds(0, held)], loads.at[1]),
        pltpu.make_async_copy(value_up_ref, value_up, loads.at[2]),
        pltpu.make_async_copy(out_weight_ref, out_weight, loads.at[3]),
        pltpu.make_async_copy(residual_ref.at[pl.ds(x * rows, rows)], residual, loads.at[4]),
        pltpu.make_async_copy(nope_in, nope_ref, loads.at[5]),
        pltpu.make_async_copy(rope_in, rope_ref, loads.at[6]),
        pltpu.make_async_copy(new_in, keys.at[pl.ds(held, tokens)], loads.at[7]),
    ]
    far_keys = remote(pages_ref, keys.at[pl.ds(held + tokens, held)], 0)
    far_rope = remote(pages_rope_ref, keys_rope.at[pl.ds(held, held)], 1)
    barrier = pltpu.get_barrier_semaphore()
    pl.semaphore_signal(barrier, inc=1, device_id=other_x, device_id_type=pl.DeviceIdType.MESH)
    for k in (5, 0, 6, 1, 7, 2, 3, 4):
        mine[k].start()
    pl.semaphore_wait(barrier, 1)
    far_keys.start()
    far_rope.start()
    keys_rope[pl.ds(0, held)] = pages_rope_ref[...]

    def bias(start):
        place = lax.broadcasted_iota(jnp.int32, (8, held), 1) + start
        slot, offset = place // PAGE, place % PAGE
        seen = jnp.zeros((8, held), jnp.int32)
        for j in range(span // PAGE):
            seen += jnp.where(
                (slot == table_ref[0, j]) & (offset + j * PAGE < length_ref[0]), 1, 0
            )
        return jnp.where(seen > 0, 0.0, NEG)[0:1]

    mine[0].wait()
    mine[5].wait()
    mine[6].wait()
    for h in range(heads):
        query_lat[pl.ds(h * tokens, tokens)] = jnp.dot(
            nope_ref[:, pl.ds(h * HD, HD)], key_up[h], preferred_element_type=jnp.float32
        ).astype(query_lat.dtype)
        query_rope[pl.ds(h * tokens, tokens)] = rope_ref[:, pl.ds(h * RD, RD)]
    mine[1].wait()
    mine[7].wait()

    def against(lo, n, rope_keys, dims):
        return (
            lax.dot_general(
                query_lat[...], keys[pl.ds(lo, n)], nt, preferred_element_type=jnp.float32
            )
            + lax.dot_general(query_rope[...], rope_keys, dims, preferred_element_type=jnp.float32)
        ) * scale

    scores[:, pl.ds(0, held)] = against(0, held, keys_rope[pl.ds(0, held)], nt) + bias(x * held)
    fresh = against(held, tokens, new_rope_ref[...], (((1,), (0,)), ((), ())))
    seen = lax.broadcasted_iota(jnp.int32, (tokens, tokens), 1) <= lax.broadcasted_iota(
        jnp.int32, (tokens, tokens), 0
    )
    causal = jnp.where(seen, 0.0, NEG)
    scores[:, pl.ds(held, tokens)] = (
        fresh.reshape(heads, tokens, tokens) + causal[None]
    ).reshape(heads * tokens, tokens)
    for h in range(heads):
        at = pl.ds(h * tokens, tokens)
        masked = scores[at]
        peak = jnp.max(masked, axis=1, keepdims=True)
        expo = jnp.exp(masked - peak)
        near_peak[at] = peak
        near_total[at] = jnp.sum(expo, axis=1, keepdims=True)
        near[at] = jnp.dot(
            expo.astype(keys.dtype),
            keys[pl.ds(0, held + tokens)],
            preferred_element_type=jnp.float32,
        )
    experts = lax.axis_size("expert")
    number = lax.broadcasted_iota(jnp.int32, (experts, tokens), 0)
    picked = jnp.zeros((experts, tokens), jnp.float32)
    for k in range(TOP):
        picked += jnp.where(ids_ref[k] == number, weights_ref[k], 0.0)
    high = picked.astype(sent_ref.dtype).astype(jnp.float32)
    fill = jnp.zeros((coded.shape[1] - 2 * experts, tokens), jnp.float32)
    coded[...] = jnp.concatenate([high, picked - high, fill], axis=0).T
    sent_ref[:, pl.ds(model, coded.shape[1])] = coded[pl.ds(x * rows, rows)].astype(sent_ref.dtype)
    mine[2].wait()
    far_keys.wait_recv()
    far_rope.wait_recv()
    far_scores[...] = against(
        held + tokens, held, keys_rope[pl.ds(held, held)], nt
    ) + bias((1 - x) * held)
    for h in range(heads):
        at = pl.ds(h * tokens, tokens)
        masked = far_scores[at]
        peak = jnp.maximum(near_peak[at], jnp.max(masked, axis=1, keepdims=True))
        expo = jnp.exp(masked - peak)
        shrink = jnp.exp(near_peak[at] - peak)
        total = near_total[at] * shrink + jnp.sum(expo, axis=1, keepdims=True)
        attn = near[at] * shrink + jnp.dot(
            expo.astype(keys.dtype),
            keys[pl.ds(held + tokens, held)],
            preferred_element_type=jnp.float32,
        )
        heads_out[:, pl.ds(h * HD, HD)] = jnp.dot(
            (attn / total).astype(keys.dtype), value_up[h], preferred_element_type=jnp.float32
        ).astype(heads_out.dtype)
    mine[3].wait()

    def exchange(n):
        return remote(partial.at[n, pl.ds((1 - x) * rows, rows)], arrived.at[n], 2 + n)

    for n in range(chunks):
        partial[n] = jnp.dot(
            heads_out[...],
            out_weight[:, pl.ds(n * piece, piece)],
            preferred_element_type=jnp.float32,
        ).astype(partial.dtype)
        exchange(n).start()
    mine[4].wait()
    power = jnp.zeros((rows, 1), jnp.float32)
    for n in range(chunks):
        exchange(n).wait_recv()
        at = pl.ds(n * piece, piece)
        hidden = (
            residual[:, at].astype(jnp.float32)
            + partial[n, pl.ds(x * rows, rows)].astype(jnp.float32)
            + arrived[n].astype(jnp.float32)
        )
        hidden_ref[:, at] = hidden
        power += jnp.sum(hidden * hidden, axis=1, keepdims=True)
    factor = lax.rsqrt(power / model + EPS)
    for n in range(chunks):
        at = pl.ds(n * piece, piece)
        sent_ref[:, at] = (hidden_ref[:, at] * factor * gain_ref[:, at]).astype(sent_ref.dtype)
    far_keys.wait_send()
    far_rope.wait_send()
    for n in range(chunks):
        exchange(n).wait_send()


def attend(
    table,
    length,
    nope,
    rope,
    new,
    new_rope,
    pages,
    pages_rope,
    residual,
    gain,
    ids,
    weights,
    key_up,
    value_up,
    out_weight,
):
    kind = nope.dtype
    heads = key_up.shape[0]
    tokens, model = residual.shape
    rows = tokens // 2
    held = pages.shape[0]
    chunks = 4
    vmem = pl.BlockSpec(memory_space=pltpu.VMEM)
    smem = pl.BlockSpec(memory_space=pltpu.SMEM)
    far = pl.BlockSpec(memory_space=pl.ANY)
    return pl.pallas_call(
        attend_kernel,
        out_shape=(
            jax.ShapeDtypeStruct((rows, model + 128), kind),
            jax.ShapeDtypeStruct((rows, model), jnp.float32),
        ),
        in_specs=[smem, smem, far, far, far, vmem, far, vmem, far, vmem, vmem, vmem, far, far, far],
        out_specs=(vmem, vmem),
        scratch_shapes=[
            pltpu.VMEM((2 * held + tokens, LAT), kind),
            pltpu.VMEM((2 * held, RD), kind),
            pltpu.VMEM(key_up.shape, kind),
            pltpu.VMEM(value_up.shape, kind),
            pltpu.VMEM(out_weight.shape, kind),
            pltpu.VMEM((rows, model), kind),
            pltpu.VMEM((heads * tokens, LAT), kind),
            pltpu.VMEM((heads * tokens, RD), kind),
            pltpu.VMEM((heads * tokens, held + tokens), jnp.float32),
            pltpu.VMEM((heads * tokens, held), jnp.float32),
            pltpu.VMEM((heads * tokens, LAT), jnp.float32),
            pltpu.VMEM((heads * tokens, 1), jnp.float32),
            pltpu.VMEM((heads * tokens, 1), jnp.float32),
            pltpu.VMEM((tokens, 128), jnp.float32),
            pltpu.VMEM(nope.shape, kind),
            pltpu.VMEM(rope.shape, kind),
            pltpu.VMEM((tokens, heads * HD), kind),
            pltpu.VMEM((chunks, tokens, model // chunks), kind),
            pltpu.VMEM((chunks, rows, model // chunks), kind),
            pltpu.SemaphoreType.DMA((8,)),
            pltpu.SemaphoreType.DMA((2 + chunks,)),
            pltpu.SemaphoreType.DMA((2 + chunks,)),
        ],
        compiler_params=pltpu.CompilerParams(
            collective_id=1, has_side_effects=True, vmem_limit_bytes=62 * 2**20
        ),
    )(
        table,
        length,
        nope,
        rope,
        new,
        new_rope,
        pages,
        pages_rope,
        residual,
        gain,
        ids,
        weights,
        key_up,
        value_up,
        out_weight,
    )


def per_device(
    query_nope,
    query_rope,
    latent_new,
    key_rope,
    latent_pages,
    rope_pages,
    page_table,
    prefix_lengths,
    residual,
    key_up,
    value_up,
    out_weight,
    norm_gain,
    expert_in,
    expert_down,
    expert_ids,
    expert_weights,
):
    groups = lax.axis_size("dp")
    experts_all = lax.axis_size("expert") * expert_in.shape[0]
    tokens_col = query_nope.shape[1]
    block_rows = tokens_col // groups
    heads_here = key_up.shape[0]
    fits = groups == 2 and lax.axis_size("expert") == 16
    start = lax.axis_index("dp") * block_rows
    model = residual.shape[2]
    if fits:
        sent, hidden_mine = attend(
            page_table,
            prefix_lengths,
            query_nope[0],
            query_rope[0],
            latent_new[0],
            jnp.transpose(key_rope[0]),
            latent_pages[0].reshape(-1, LAT),
            rope_pages[0].reshape(-1, RD),
            residual[0],
            norm_gain[None],
            jnp.transpose(expert_ids, (2, 0, 1)),
            jnp.transpose(expert_weights, (2, 0, 1)),
            key_up,
            value_up,
            out_weight,
        )
        mixture = mixture_kernel(sent, expert_in[0], expert_down[0])
    else:
        ids_mine = lax.dynamic_slice_in_dim(expert_ids[0], start, block_rows, 0)
        weights_mine = lax.dynamic_slice_in_dim(expert_weights[0], start, block_rows, 0)
        gates = jnp.sum(
            jnp.where(
                ids_mine[:, :, None] == jnp.arange(experts_all)[None, None, :],
                weights_mine[:, :, None],
                0.0,
            ),
            axis=1,
        )
        gates_high = gates.astype(jnp.bfloat16)
        gates_low = (gates - gates_high.astype(jnp.float32)).astype(jnp.bfloat16)
        extra = -(-2 * experts_all // 128) * 128
        fill = jnp.zeros((block_rows, extra - 2 * experts_all), jnp.bfloat16)
        coded = jnp.concatenate([gates_high, gates_low, fill], axis=1)
        pages_lat, pages_rope = (
            lax.all_gather(latent_pages[0], "dp", axis=0, tiled=True),
            lax.all_gather(rope_pages[0], "dp", axis=0, tiled=True),
        )
        page_count = pages_lat.shape[0]
        table = page_table[0]
        inverse = jnp.sum(
            jnp.where(
                table[:, None] == jnp.arange(page_count)[None, :], jnp.arange(page_count)[:, None], 0
            ),
            axis=0,
        )
        positions = (inverse[:, None] * PAGE + jnp.arange(PAGE)[None, :]).reshape(-1)
        prefix_ok = positions < prefix_lengths[0]
        keys_lat = jnp.concatenate([pages_lat.reshape(-1, LAT), latent_new[0]], axis=0)
        keys_rope = jnp.concatenate([pages_rope.reshape(-1, RD), key_rope[0]], axis=0)
        heads_nope = query_nope[0].reshape(tokens_col, heads_here, HD)
        query_lat = jnp.einsum(
            "thd,hdc->thc", heads_nope, key_up, preferred_element_type=jnp.float32
        ).astype(jnp.bfloat16)
        heads_rope = query_rope[0].reshape(tokens_col, heads_here, RD)
        scale = 1.0 / (HD + RD) ** 0.5
        scores = (
            jnp.einsum("thc,kc->thk", query_lat, keys_lat, preferred_element_type=jnp.float32)
            + jnp.einsum("thr,kr->thk", heads_rope, keys_rope, preferred_element_type=jnp.float32)
        ) * scale
        causal = jnp.arange(tokens_col)[None, :] <= jnp.arange(tokens_col)[:, None]
        allowed = jnp.concatenate(
            [jnp.broadcast_to(prefix_ok[None, :], (tokens_col, prefix_ok.shape[0])), causal], axis=1
        )[:, None, :]
        masked = jnp.where(allowed, scores, NEG)
        peak = jnp.max(masked, axis=-1, keepdims=True)
        expo = jnp.where(allowed, jnp.exp(masked - peak), 0.0)
        total = jnp.sum(expo, axis=-1, keepdims=True)
        probs = expo.astype(jnp.bfloat16)
        attn_latent = (
            jnp.einsum("thk,kc->thc", probs, keys_lat, preferred_element_type=jnp.float32) / total
        ).astype(jnp.bfloat16)
        heads_out = jnp.einsum(
            "thc,hcd->thd", attn_latent, value_up, preferred_element_type=jnp.float32
        ).astype(jnp.bfloat16)
        partial_out = jnp.dot(
            heads_out.reshape(tokens_col, heads_here * HD),
            out_weight,
            preferred_element_type=jnp.float32,
        )
        attended = lax.psum_scatter(
            partial_out.astype(jnp.bfloat16), "dp", scatter_dimension=0, tiled=True
        ).astype(jnp.float32)
        hidden_mine = (
            lax.dynamic_slice_in_dim(residual[0], start, block_rows, 0).astype(jnp.float32) + attended
        )
        normed = norm_rows(hidden_mine, norm_gain)
        sent = jnp.concatenate([normed, coded], axis=1)
        gathered = lax.all_gather(sent, ("expert", "dp"), axis=0, tiled=True)
        everyone = gathered[:, :model]
        mine = lax.axis_index("expert")
        named = (jnp.arange(extra) == mine) | (jnp.arange(extra) == mine + experts_all)
        gate = jnp.sum(
            jnp.where(named[None, :], gathered[:, model:].astype(jnp.float32), 0.0),
            axis=1,
            keepdims=True,
        )
        part = expert_apply(everyone, gate, expert_in, expert_down)
        mixture = lax.psum_scatter(
            part, ("expert", "dp"), scatter_dimension=0, tiled=True
        ).astype(jnp.float32)
    layer_out = (hidden_mine + mixture).astype(jnp.bfloat16)[None]
    return (layer_out, mixture.astype(jnp.bfloat16)[None])


def solution(mesh):
    return jax.shard_map(
        per_device,
        mesh=mesh,
        in_specs=(
            P("expert", None, "dp"),
            P("expert", None, "dp"),
            P("expert", None, None),
            P("expert", None, None),
            P("expert", "dp", None, None),
            P("expert", "dp", None),
            P("expert", None),
            P("expert"),
            P("expert", None, None),
            P("dp", None, None),
            P("dp", None, None),
            P("dp", None),
            P(),
            P("expert", "dp", None, None),
            P("expert", "dp", None),
            P("expert", None, None),
            P("expert", None, None),
        ),
        out_specs=(P("expert", "dp", None), P("expert", "dp", None)),
        check_vma=False,
    )
```

```python
import functools

import jax
import jax.numpy as jnp
from jax import lax
from jax.experimental import pallas as pl
from jax.experimental.pallas import tpu as pltpu
from jax.sharding import PartitionSpec as P

HD = 128
RD = 64
LAT = 512
TOP = 6
PAGE = 64


EPS = 1e-06
NEG = -1e30


def norm_rows(hidden, norm_gain):
    power = jnp.mean(hidden * hidden, axis=-1, keepdims=True)
    return (hidden * lax.rsqrt(power + EPS) * norm_gain).astype(jnp.bfloat16)


def expert_apply(tokens, gate, expert_in, expert_down):
    flat = tokens.reshape(-1, tokens.shape[-1])
    dims = (((1,), (1,)), ((), ()))
    gate_act = lax.dot_general(
        flat, expert_in[0, :, 0, :], dims, preferred_element_type=jnp.float32
    )
    up_act = lax.dot_general(flat, expert_in[0, :, 1, :], dims, preferred_element_type=jnp.float32)
    units = (jax.nn.silu(gate_act) * up_act).astype(jnp.bfloat16)
    part = jnp.dot(units, expert_down[0], preferred_element_type=jnp.float32)
    return (part * gate).astype(jnp.bfloat16)


def moe_kernel(
    sent_ref,
    w_in_ref,
    w_down_ref,
    out_ref,
    tok,
    raw,
    w_in,
    w_down,
    units,
    gate,
    part,
    core_in,
    acc,
    diag_x,
    diag_y,
    from_x,
    from_y,
    z_send,
    z_up,
    z_down,
    relay,
    w_sems,
    g_sends,
    g_recvs,
    sends,
    recvs,
):
    x = lax.axis_index("dp")
    e = lax.axis_index("expert")
    z, y, c = e // 4, (e // 2) % 2, e % 2
    rows, model = out_ref.shape
    half = rows // 2
    width = w_down_ref.shape[0]
    high = z // 2
    low_z = z + high * (3 - 2 * z)
    mid = low_z == 1

    def flip(f):
        return f + high * (3 - 2 * f)

    planes = [z, flip(1 - low_z), flip(3 + 0 * z), flip(2 + 0 * z)]
    other_core = {"expert": e + 1 - 2 * c}
    other_y = {"expert": e + 2 - 4 * y}
    other_x = {"dp": 1 - x}
    above, below = {"expert": e + 4}, {"expert": e - 4}
    pair, middle = {"expert": e + 4 - 8 * (z % 2)}, {"expert": e + 4 * (3 - 2 * z)}
    halves = first, second = pl.ds(0, half), pl.ds(half, half)

    def remote(src, dst, send, recv, to):
        return pltpu.make_async_remote_copy(
            src_ref=src,
            dst_ref=dst,
            send_sem=send,
            recv_sem=recv,
            device_id=to,
            device_id_type=pl.DeviceIdType.MESH,
        )

    def same(ref, kind, p, to):
        return remote(ref, ref, g_sends.at[kind, p], g_recvs.at[kind, p], to)

    def g_up(p, h):
        return same(tok.at[p, y, c, x, halves[h]], h, p, above)

    def g_down(p, h):
        return same(tok.at[p, y, c, x, halves[h]], 2 + h, p, below)

    def g_x(p, i, h):
        return same(tok.at[p, y, c, i, halves[h]], 4 + h, p, other_x)

    def g_y(p, j, h):
        return same(tok.at[p, j, c, x, halves[h]], 6 + h, p, other_y)

    def g_diag_x(p, j):
        return same(tok.at[p, j, c, x, first], 8, p, other_x)

    def g_diag_y(p, i):
        return same(tok.at[p, y, c, i, second], 9, p, other_y)

    def g_core(p, kind, cc):
        j, i = (y, y, 1 - y, 1 - y)[kind], (x, 1 - x, x, 1 - x)[kind]
        return same(tok.at[p, j, cc, i], 10 + kind, p, other_core)

    def own_line(p):
        g_x(p, x, 1).start()
        g_y(p, y, 0).start()
        g_x(p, x, 0).start()
        g_y(p, y, 1).start()
        g_core(p, 0, c).start()

    def along_z(p, h):
        @pl.when(p < z)
        def _():
            g_up(p, h).wait_recv()

            @pl.when(z < 3)
            def _():
                g_up(p, h).start()

        @pl.when(p > z)
        def _():
            g_down(p, h).wait_recv()

            @pl.when(z > 0)
            def _():
                g_down(p, h).start()

    def beside_send(p):
        g_x(p, 1 - x, 1).wait_recv()
        g_diag_y(p, 1 - x).start()
        g_y(p, 1 - y, 0).wait_recv()
        g_diag_x(p, 1 - y).start()

    def beside_rest(p, diag=True):
        if not diag:
            g_x(p, 1 - x, 1).wait_recv()
            g_y(p, 1 - y, 0).wait_recv()
        g_x(p, 1 - x, 0).wait_recv()
        g_core(p, 1, c).start()
        g_y(p, 1 - y, 1).wait_recv()
        g_core(p, 2, c).start()

    def across(p):
        same(tok.at[p, 1 - y, c, 1 - x, first], 8, p, other_x).wait_recv()
        same(tok.at[p, 1 - y, c, 1 - x, second], 9, p, other_y).wait_recv()
        g_core(p, 3, c).start()

    def diag_up(p):
        return same(tok.at[p, 1 - y, c, 1 - x], 14, p, above)

    def diag_down(p):
        return same(tok.at[p, 1 - y, c, 1 - x], 15, p, below)

    def diag_out():
        @pl.when(z == 1)
        def _():
            diag_up(z).start()

        @pl.when(z == 2)
        def _():
            diag_down(z).start()

    def diag_in(p, forward):
        @pl.when(p < z)
        def _():
            diag_up(p).wait_recv()
            if forward:

                @pl.when(mid)
                def _():
                    diag_up(p).start()

        @pl.when(p > z)
        def _():
            diag_down(p).wait_recv()
            if forward:

                @pl.when(mid)
                def _():
                    diag_down(p).start()

        g_core(p, 3, c).start()

    def whole(p):
        for kind in range(4):
            g_core(p, kind, 1 - c).wait_recv()

    def tokens(p):
        return tok[p, :, :, :, :, pl.ds(0, model)].reshape(8 * rows, model)

    def hidden(p, lo, n):
        dims = (((1,), (1,)), ((), ()))
        values = tokens(p)
        gate_act = lax.dot_general(
            values, w_in[0, pl.ds(lo, n)], dims, preferred_element_type=jnp.float32
        )
        up_act = lax.dot_general(
            values, w_in[1, pl.ds(lo, n)], dims, preferred_element_type=jnp.float32
        )
        units[:, pl.ds(lo, n)] = (gate_act / (1.0 + jnp.exp(-gate_act)) * up_act).astype(
            units.dtype
        )

    def gates(p):
        extra = tok.shape[5] - model
        lanes = lax.broadcasted_iota(jnp.int32, (8 * rows, extra), 1)
        named = (lanes == e) | (lanes == e + lax.axis_size("expert"))
        values = tok[p, :, :, :, :, pl.ds(model, extra)].reshape(8 * rows, extra)
        gate[...] = jnp.sum(
            jnp.where(named, values.astype(jnp.float32), 0.0), axis=1, keepdims=True
        )

    def project(p, lo, n):
        value = jnp.dot(units[...], w_down[:, pl.ds(lo, n)], preferred_element_type=jnp.float32)
        part[p, :, :, :, :, pl.ds(lo, n)] = (
            (value * gate[...]).astype(part.dtype).reshape(2, 2, 2, rows, n)
        )

    def compute(p, between):
        steps = [functools.partial(hidden, p, lo, min(256, width - lo)) for lo in range(0, width, 256)]
        steps += [functools.partial(gates, p)]
        steps += [functools.partial(project, p, lo, 256) for lo in range(0, model, 256)]
        for number, step in enumerate(steps):
            step()
            for act in between.get(number, ()):
                act()

    def copy(src, dst, kind, k, to):
        return remote(src, dst, sends.at[kind, k], recvs.at[kind, k], to)

    def core_copy(k):
        return copy(part.at[planes[k], :, 1 - c], core_in.at[k], 0, k, other_core)

    def diag_y_copy(k):
        return copy(acc.at[k, 1 - y, 1 - x, first], diag_y.at[k], 1, k, other_y)

    def diag_x_copy(k):
        return copy(acc.at[k, 1 - y, 1 - x, second], diag_x.at[k], 2, k, other_x)

    def x_copy(k, h):
        return copy(acc.at[k, y, 1 - x, halves[h]], from_x.at[k, halves[h]], 3 + h, k, other_x)

    def y_copy(k, h):
        return copy(acc.at[k, 1 - y, x, halves[h]], from_y.at[k, halves[h]], 5 + h, k, other_y)

    def up_copy(g, h):
        return copy(z_send.at[g, halves[h]], z_up.at[g, halves[h]], 7 + h, g, above)

    def down_copy(g, h):
        return copy(z_send.at[g, halves[h]], z_down.at[g, halves[h]], 9 + h, g, below)

    def wide(value):
        return value.astype(jnp.float32)

    def relay_copy(k, slot, h, to):
        return copy(
            acc.at[k, 1 - y, 1 - x, halves[h]], relay.at[slot, halves[h]], 11 + h, slot, to
        )

    def add_relay(k, slot, h):
        at = halves[h]
        relay_copy(k, slot, h, pair).wait_recv()
        acc[k, 1 - y, 1 - x, at] = (wide(acc[k, 1 - y, 1 - x, at]) + wide(relay[slot, at])).astype(
            acc.dtype
        )

    def add_core(k, j, i):
        acc[k, j, i] = (wide(part[planes[k], j, c, i]) + wide(core_in[k, j, i])).astype(acc.dtype)

    def stage_a(k):
        core_copy(k).wait_recv()
        add_core(k, 1 - y, 1 - x)
        if k == 1:
            relay_copy(1, 0, 0, pair).start()
            relay_copy(1, 0, 1, pair).start()
        if k == 2:
            diag_y_copy(k).start()
            diag_x_copy(k).start()
        if k == 3:

            @pl.when(low_z == 0)
            def _():
                relay_copy(3, 1, 0, pair).start()
                relay_copy(3, 1, 1, pair).start()

        add_core(k, y, 1 - x)
        x_copy(k, 1).start()
        if k % 2 == 1:
            x_copy(k, 0).start()
        add_core(k, 1 - y, x)
        y_copy(k, 0).start()
        if k % 2 == 1:
            y_copy(k, 1).start()
        add_core(k, y, x)
        if k == 3:

            @pl.when(mid)
            def _():
                for h in (0, 1):
                    add_relay(3, 1, h)
                    relay_copy(3, 2, h, middle).start()

    def own_diag():
        for h in (0, 1):
            add_relay(0, 0, h)

            @pl.when(mid)
            def _():
                add_relay(0, 2, h)

            (diag_y_copy, diag_x_copy)[h](0).start()

    def stage_b(k):
        diag_y_copy(k).wait_recv()
        acc[k, y, 1 - x, first] = (wide(acc[k, y, 1 - x, first]) + wide(diag_y[k])).astype(acc.dtype)
        x_copy(k, 0).start()
        diag_x_copy(k).wait_recv()
        acc[k, 1 - y, x, second] = (wide(acc[k, 1 - y, x, second]) + wide(diag_x[k])).astype(
            acc.dtype
        )
        y_copy(k, 1).start()

    def stage_c(k, g, last=False):
        for h in (0, 1):
            at = halves[h]
            x_copy(k, h).wait_recv()
            y_copy(k, h).wait_recv()
            out_ref[at] = wide(acc[k, y, x, at]) + wide(from_x[k, at]) + wide(from_y[k, at])

            @pl.when((g >= z) & (z > 0))
            def _():
                up_copy(g, h).wait_recv()
                out_ref[at] += wide(z_up[g, at])

            @pl.when((g <= z) & (z < 3))
            def _():
                down_copy(g, h).wait_recv()
                out_ref[at] += wide(z_down[g, at])

            if not last:
                z_send[g, at] = out_ref[at].astype(z_send.dtype)

                @pl.when(g > z)
                def _():
                    up_copy(g, h).start()

                @pl.when(g < z)
                def _():
                    down_copy(g, h).start()

    load_in = pltpu.make_async_copy(w_in_ref, raw, w_sems.at[0])

    def untangle(lo, n):
        for at in range(lo, lo + n, 64):
            pairs = raw[pl.ds(at, 64)].reshape(128, model)
            row = lax.broadcasted_iota(jnp.int32, (128, 128), 0)
            column = lax.broadcasted_iota(jnp.int32, (128, 128), 1)
            order = jnp.where(column == 2 * (row % 64) + row // 64, 1.0, 0.0).astype(raw.dtype)
            sorted_rows = jnp.dot(order, pairs, preferred_element_type=jnp.float32).astype(raw.dtype)
            w_in[0, pl.ds(at, 64)] = sorted_rows[:64]
            w_in[1, pl.ds(at, 64)] = sorted_rows[64:]

    load_down = pltpu.make_async_copy(w_down_ref, w_down, w_sems.at[1])
    barrier = pltpu.get_barrier_semaphore()
    for to in (other_core, other_x, other_y):
        pl.semaphore_signal(barrier, inc=1, device_id=to, device_id_type=pl.DeviceIdType.MESH)

    @pl.when(z > 0)
    def _():
        pl.semaphore_signal(barrier, inc=1, device_id=below, device_id_type=pl.DeviceIdType.MESH)

    @pl.when(z < 3)
    def _():
        pl.semaphore_signal(barrier, inc=1, device_id=above, device_id_type=pl.DeviceIdType.MESH)

    load_in.start()
    load_down.start()
    tok[z, y, c, x] = sent_ref[...]
    pl.semaphore_wait(barrier, 4 + ((z + 1) // 2) % 2)

    for h in (0, 1):

        @pl.when(z < 3)
        def _():
            g_up(z, h).start()

        @pl.when(z > 0)
        def _():
            g_down(z, h).start()

    def do(f, *args):
        return functools.partial(f, *args)

    def at_mid(*acts):
        @pl.when(mid)
        def _():
            for act in acts:
                act()

    def at_end(*acts):
        @pl.when(low_z == 0)
        def _():
            for act in acts:
                act()

    def start_core(k):
        core_copy(k).start()

    own_line(z)
    load_in.wait()
    untangle(0, 256)
    along_z(planes[1], 0)
    at_mid(do(along_z, planes[3], 0))
    beside_send(planes[0])
    along_z(planes[1], 1)
    at_mid(do(along_z, planes[3], 1))
    own_line(planes[1])
    beside_rest(planes[0])
    untangle(256, 256)
    across(planes[0])
    at_mid(do(along_z, planes[2], 0), do(diag_out), do(along_z, planes[2], 1))
    beside_send(planes[1])
    at_mid(do(own_line, planes[2]))
    untangle(512, 192)
    load_down.wait()
    whole(planes[0])
    compute(
        planes[0],
        {
            2: [do(at_end, do(along_z, planes[3], 0), do(along_z, planes[3], 1))],
            5: [do(beside_rest, planes[1])],
            9: [
                do(at_end, do(along_z, planes[2], 0), do(along_z, planes[2], 1)),
                do(at_end, do(own_line, planes[2])),
            ],
        },
    )
    start_core(0)
    across(planes[1])
    at_mid(do(diag_in, planes[3], True))
    whole(planes[1])
    compute(
        planes[1],
        {
            2: [do(beside_send, planes[2]), do(own_line, planes[3])],
            7: [do(beside_rest, planes[2])],
        },
    )
    start_core(1)
    across(planes[2])
    stage_a(0)
    whole(planes[2])
    compute(
        planes[2],
        {
            2: [do(stage_a, 1)],
            6: [do(at_end, do(diag_in, planes[3], False))],
            9: [do(beside_rest, planes[3], False)],
        },
    )
    start_core(2)
    whole(planes[3])
    compute(
        planes[3],
        {
            2: [do(stage_a, 2)],
            7: [do(at_end, do(stage_c, 1, planes[1]))],
            11: [do(stage_b, 2)],
        },
    )
    start_core(3)
    at_end(own_diag)
    stage_a(3)
    stage_c(2, planes[2])
    at_mid(own_diag, do(stage_c, 1, planes[1]), do(stage_c, 3, planes[3]))
    stage_b(0)
    at_end(do(stage_c, 3, planes[3]))
    stage_c(0, planes[0], True)

    for k in range(4):
        p = planes[k]
        core_copy(k).wait_send()
        if k % 2 == 0:
            diag_y_copy(k).wait_send()
            diag_x_copy(k).wait_send()
        if k < 3:
            g_diag_y(p, 1 - x).wait_send()
            g_diag_x(p, 1 - y).wait_send()
        for kind in range(4):
            g_core(p, kind, c).wait_send()
        if k == 0:

            @pl.when(z == 1)
            def _():
                diag_up(p).wait_send()

            @pl.when(z == 2)
            def _():
                diag_down(p).wait_send()

        if k == 1:
            relay_copy(1, 0, 0, pair).wait_send()
            relay_copy(1, 0, 1, pair).wait_send()
        if k == 3:

            @pl.when(mid & (p < z))
            def _():
                diag_up(p).wait_send()

            @pl.when(mid & (p > z))
            def _():
                diag_down(p).wait_send()

            @pl.when(mid)
            def _():
                relay_copy(3, 2, 0, middle).wait_send()
                relay_copy(3, 2, 1, middle).wait_send()

            @pl.when(low_z == 0)
            def _():
                relay_copy(3, 1, 0, pair).wait_send()
                relay_copy(3, 1, 1, pair).wait_send()

        for h in (0, 1):
            x_copy(k, h).wait_send()
            y_copy(k, h).wait_send()
            g_x(p, x, h).wait_send()
            g_y(p, y, h).wait_send()

            @pl.when((p <= z) & (z < 3))
            def _():
                g_up(p, h).wait_send()

            @pl.when((p >= z) & (z > 0))
            def _():
                g_down(p, h).wait_send()

            if k > 0:

                @pl.when(p > z)
                def _():
                    up_copy(p, h).wait_send()

                @pl.when(p < z)
                def _():
                    down_copy(p, h).wait_send()


def mixture_kernel(sent, w_in, w_down):
    rows, full = sent.shape
    width, model = w_down.shape
    kind = sent.dtype
    line = pltpu.VMEM((4, rows, model), kind)
    halves = pltpu.VMEM((4, rows // 2, model), kind)
    return pl.pallas_call(
        moe_kernel,
        out_shape=jax.ShapeDtypeStruct((rows, model), jnp.float32),
        in_specs=[
            pl.BlockSpec(memory_space=pltpu.VMEM),
            pl.BlockSpec(memory_space=pl.ANY),
            pl.BlockSpec(memory_space=pl.ANY),
        ],
        out_specs=pl.BlockSpec(memory_space=pltpu.VMEM),
        scratch_shapes=[
            pltpu.VMEM((4, 2, 2, 2, rows, full), kind),
            pltpu.VMEM((width, 2, model), kind),
            pltpu.VMEM((2, width, model), kind),
            pltpu.VMEM((width, model), kind),
            pltpu.VMEM((8 * rows, width), kind),
            pltpu.VMEM((8 * rows, 1), jnp.float32),
            pltpu.VMEM((4, 2, 2, 2, rows, model), kind),
            pltpu.VMEM((4, 2, 2, rows, model), kind),
            pltpu.VMEM((4, 2, 2, rows, model), kind),
            halves,
            halves,
            line,
            line,
            line,
            line,
            line,
            pltpu.VMEM((3, rows, model), kind),
            pltpu.SemaphoreType.DMA((2,)),
            pltpu.SemaphoreType.DMA((16, 4)),
            pltpu.SemaphoreType.DMA((16, 4)),
            pltpu.SemaphoreType.DMA((13, 4)),
            pltpu.SemaphoreType.DMA((13, 4)),
        ],
        compiler_params=pltpu.CompilerParams(
            collective_id=0, has_side_effects=True, vmem_limit_bytes=52 * 2**20
        ),
    )(sent, w_in, w_down)


def attend_kernel(
    table_ref,
    length_ref,
    nope_in,
    rope_in,
    new_in,
    new_rope_ref,
    pages_ref,
    pages_rope_ref,
    residual_ref,
    gain_ref,
    ids_ref,
    weights_ref,
    key_up_ref,
    value_up_ref,
    out_weight_ref,
    sent_ref,
    hidden_ref,
    keys,
    keys_rope,
    key_up,
    value_up,
    out_weight,
    residual,
    query_lat,
    query_rope,
    scores,
    far_scores,
    near,
    near_peak,
    near_total,
    coded,
    nope_ref,
    rope_ref,
    heads_out,
    partial,
    arrived,
    loads,
    sends,
    recvs,
):
    x = lax.axis_index("dp")
    other_x = {"dp": 1 - x}
    heads = key_up.shape[0]
    tokens = nope_in.shape[0]
    held = pages_ref.shape[0]
    rows, model = hidden_ref.shape
    chunks, piece = partial.shape[0], partial.shape[2]
    span = 2 * held
    scale = 1.0 / (HD + RD) ** 0.5
    nt = (((1,), (1,)), ((), ()))

    def remote(src, dst, k):
        return pltpu.make_async_remote_copy(
            src_ref=src,
            dst_ref=dst,
            send_sem=sends.at[k],
            recv_sem=recvs.at[k],
            device_id=other_x,
            device_id_type=pl.DeviceIdType.MESH,
        )

    mine = [
        pltpu.make_async_copy(key_up_ref, key_up, loads.at[0]),
        pltpu.make_async_copy(pages_ref, keys.at[pl.ds(0, held)], loads.at[1]),
        pltpu.make_async_copy(value_up_ref, value_up, loads.at[2]),
        pltpu.make_async_copy(out_weight_ref, out_weight, loads.at[3]),
        pltpu.make_async_copy(residual_ref.at[pl.ds(x * rows, rows)], residual, loads.at[4]),
        pltpu.make_async_copy(nope_in, nope_ref, loads.at[5]),
        pltpu.make_async_copy(rope_in, rope_ref, loads.at[6]),
        pltpu.make_async_copy(new_in, keys.at[pl.ds(held, tokens)], loads.at[7]),
    ]
    far_keys = remote(pages_ref, keys.at[pl.ds(held + tokens, held)], 0)
    far_rope = remote(pages_rope_ref, keys_rope.at[pl.ds(held, held)], 1)
    barrier = pltpu.get_barrier_semaphore()
    pl.semaphore_signal(barrier, inc=1, device_id=other_x, device_id_type=pl.DeviceIdType.MESH)
    for k in (5, 0, 6, 1, 7, 2, 3, 4):
        mine[k].start()
    pl.semaphore_wait(barrier, 1)
    far_keys.start()
    far_rope.start()
    keys_rope[pl.ds(0, held)] = pages_rope_ref[...]

    def bias(start):
        place = lax.broadcasted_iota(jnp.int32, (8, held), 1) + start
        slot, offset = place // PAGE, place % PAGE
        seen = jnp.zeros((8, held), jnp.int32)
        for j in range(span // PAGE):
            seen += jnp.where(
                (slot == table_ref[0, j]) & (offset + j * PAGE < length_ref[0]), 1, 0
            )
        return jnp.where(seen > 0, 0.0, NEG)[0:1]

    mine[0].wait()
    mine[5].wait()
    mine[6].wait()
    for h in range(heads):
        query_lat[pl.ds(h * tokens, tokens)] = jnp.dot(
            nope_ref[:, pl.ds(h * HD, HD)], key_up[h], preferred_element_type=jnp.float32
        ).astype(query_lat.dtype)
        query_rope[pl.ds(h * tokens, tokens)] = rope_ref[:, pl.ds(h * RD, RD)]
    mine[1].wait()
    mine[7].wait()

    def against(lo, n, rope_keys, dims):
        return (
            lax.dot_general(
                query_lat[...], keys[pl.ds(lo, n)], nt, preferred_element_type=jnp.float32
            )
            + lax.dot_general(query_rope[...], rope_keys, dims, preferred_element_type=jnp.float32)
        ) * scale

    scores[:, pl.ds(0, held)] = against(0, held, keys_rope[pl.ds(0, held)], nt) + bias(x * held)
    fresh = against(held, tokens, new_rope_ref[...], (((1,), (0,)), ((), ())))
    seen = lax.broadcasted_iota(jnp.int32, (tokens, tokens), 1) <= lax.broadcasted_iota(
        jnp.int32, (tokens, tokens), 0
    )
    causal = jnp.where(seen, 0.0, NEG)
    scores[:, pl.ds(held, tokens)] = (
        fresh.reshape(heads, tokens, tokens) + causal[None]
    ).reshape(heads * tokens, tokens)
    for h in range(heads):
        at = pl.ds(h * tokens, tokens)
        masked = scores[at]
        peak = jnp.max(masked, axis=1, keepdims=True)
        expo = jnp.exp(masked - peak)
        near_peak[at] = peak
        near_total[at] = jnp.sum(expo, axis=1, keepdims=True)
        near[at] = jnp.dot(
            expo.astype(keys.dtype),
            keys[pl.ds(0, held + tokens)],
            preferred_element_type=jnp.float32,
        )
    experts = lax.axis_size("expert")
    number = lax.broadcasted_iota(jnp.int32, (experts, tokens), 0)
    picked = jnp.zeros((experts, tokens), jnp.float32)
    for k in range(TOP):
        picked += jnp.where(ids_ref[k] == number, weights_ref[k], 0.0)
    high = picked.astype(sent_ref.dtype).astype(jnp.float32)
    fill = jnp.zeros((coded.shape[1] - 2 * experts, tokens), jnp.float32)
    coded[...] = jnp.concatenate([high, picked - high, fill], axis=0).T
    sent_ref[:, pl.ds(model, coded.shape[1])] = coded[pl.ds(x * rows, rows)].astype(sent_ref.dtype)
    mine[2].wait()
    far_keys.wait_recv()
    far_rope.wait_recv()
    far_scores[...] = against(
        held + tokens, held, keys_rope[pl.ds(held, held)], nt
    ) + bias((1 - x) * held)
    for h in range(heads):
        at = pl.ds(h * tokens, tokens)
        masked = far_scores[at]
        peak = jnp.maximum(near_peak[at], jnp.max(masked, axis=1, keepdims=True))
        expo = jnp.exp(masked - peak)
        shrink = jnp.exp(near_peak[at] - peak)
        total = near_total[at] * shrink + jnp.sum(expo, axis=1, keepdims=True)
        attn = near[at] * shrink + jnp.dot(
            expo.astype(keys.dtype),
            keys[pl.ds(held + tokens, held)],
            preferred_element_type=jnp.float32,
        )
        heads_out[:, pl.ds(h * HD, HD)] = jnp.dot(
            (attn / total).astype(keys.dtype), value_up[h], preferred_element_type=jnp.float32
        ).astype(heads_out.dtype)
    mine[3].wait()

    def exchange(n):
        return remote(partial.at[n, pl.ds((1 - x) * rows, rows)], arrived.at[n], 2 + n)

    for n in range(chunks):
        partial[n] = jnp.dot(
            heads_out[...],
            out_weight[:, pl.ds(n * piece, piece)],
            preferred_element_type=jnp.float32,
        ).astype(partial.dtype)
        exchange(n).start()
    mine[4].wait()
    power = jnp.zeros((rows, 1), jnp.float32)
    for n in range(chunks):
        exchange(n).wait_recv()
        at = pl.ds(n * piece, piece)
        hidden = (
            residual[:, at].astype(jnp.float32)
            + partial[n, pl.ds(x * rows, rows)].astype(jnp.float32)
            + arrived[n].astype(jnp.float32)
        )
        hidden_ref[:, at] = hidden
        power += jnp.sum(hidden * hidden, axis=1, keepdims=True)
    factor = lax.rsqrt(power / model + EPS)
    for n in range(chunks):
        at = pl.ds(n * piece, piece)
        sent_ref[:, at] = (hidden_ref[:, at] * factor * gain_ref[:, at]).astype(sent_ref.dtype)
    far_keys.wait_send()
    far_rope.wait_send()
    for n in range(chunks):
        exchange(n).wait_send()


def attend(
    table,
    length,
    nope,
    rope,
    new,
    new_rope,
    pages,
    pages_rope,
    residual,
    gain,
    ids,
    weights,
    key_up,
    value_up,
    out_weight,
):
    kind = nope.dtype
    heads = key_up.shape[0]
    tokens, model = residual.shape
    rows = tokens // 2
    held = pages.shape[0]
    chunks = 4
    vmem = pl.BlockSpec(memory_space=pltpu.VMEM)
    smem = pl.BlockSpec(memory_space=pltpu.SMEM)
    far = pl.BlockSpec(memory_space=pl.ANY)
    return pl.pallas_call(
        attend_kernel,
        out_shape=(
            jax.ShapeDtypeStruct((rows, model + 128), kind),
            jax.ShapeDtypeStruct((rows, model), jnp.float32),
        ),
        in_specs=[smem, smem, far, far, far, vmem, far, vmem, far, vmem, vmem, vmem, far, far, far],
        out_specs=(vmem, vmem),
        scratch_shapes=[
            pltpu.VMEM((2 * held + tokens, LAT), kind),
            pltpu.VMEM((2 * held, RD), kind),
            pltpu.VMEM(key_up.shape, kind),
            pltpu.VMEM(value_up.shape, kind),
            pltpu.VMEM(out_weight.shape, kind),
            pltpu.VMEM((rows, model), kind),
            pltpu.VMEM((heads * tokens, LAT), kind),
            pltpu.VMEM((heads * tokens, RD), kind),
            pltpu.VMEM((heads * tokens, held + tokens), jnp.float32),
            pltpu.VMEM((heads * tokens, held), jnp.float32),
            pltpu.VMEM((heads * tokens, LAT), jnp.float32),
            pltpu.VMEM((heads * tokens, 1), jnp.float32),
            pltpu.VMEM((heads * tokens, 1), jnp.float32),
            pltpu.VMEM((tokens, 128), jnp.float32),
            pltpu.VMEM(nope.shape, kind),
            pltpu.VMEM(rope.shape, kind),
            pltpu.VMEM((tokens, heads * HD), kind),
            pltpu.VMEM((chunks, tokens, model // chunks), kind),
            pltpu.VMEM((chunks, rows, model // chunks), kind),
            pltpu.SemaphoreType.DMA((8,)),
            pltpu.SemaphoreType.DMA((2 + chunks,)),
            pltpu.SemaphoreType.DMA((2 + chunks,)),
        ],
        compiler_params=pltpu.CompilerParams(
            collective_id=1, has_side_effects=True, vmem_limit_bytes=62 * 2**20
        ),
    )(
        table,
        length,
        nope,
        rope,
        new,
        new_rope,
        pages,
        pages_rope,
        residual,
        gain,
        ids,
        weights,
        key_up,
        value_up,
        out_weight,
    )


def per_device(
    query_nope,
    query_rope,
    latent_new,
    key_rope,
    latent_pages,
    rope_pages,
    page_table,
    prefix_lengths,
    residual,
    key_up,
    value_up,
    out_weight,
    norm_gain,
    expert_in,
    expert_down,
    expert_ids,
    expert_weights,
):
    groups = lax.axis_size("dp")
    experts_all = lax.axis_size("expert") * expert_in.shape[0]
    tokens_col = query_nope.shape[1]
    block_rows = tokens_col // groups
    heads_here = key_up.shape[0]
    fits = groups == 2 and lax.axis_size("expert") == 16
    start = lax.axis_index("dp") * block_rows
    model = residual.shape[2]
    if fits:
        sent, hidden_mine = attend(
            page_table,
            prefix_lengths,
            query_nope[0],
            query_rope[0],
            latent_new[0],
            jnp.transpose(key_rope[0]),
            latent_pages[0].reshape(-1, LAT),
            rope_pages[0].reshape(-1, RD),
            residual[0],
            norm_gain[None],
            jnp.transpose(expert_ids, (2, 0, 1)),
            jnp.transpose(expert_weights, (2, 0, 1)),
            key_up,
            value_up,
            out_weight,
        )
        mixture = mixture_kernel(sent, expert_in[0], expert_down[0])
    else:
        ids_mine = lax.dynamic_slice_in_dim(expert_ids[0], start, block_rows, 0)
        weights_mine = lax.dynamic_slice_in_dim(expert_weights[0], start, block_rows, 0)
        gates = jnp.sum(
            jnp.where(
                ids_mine[:, :, None] == jnp.arange(experts_all)[None, None, :],
                weights_mine[:, :, None],
                0.0,
            ),
            axis=1,
        )
        gates_high = gates.astype(jnp.bfloat16)
        gates_low = (gates - gates_high.astype(jnp.float32)).astype(jnp.bfloat16)
        extra = -(-2 * experts_all // 128) * 128
        fill = jnp.zeros((block_rows, extra - 2 * experts_all), jnp.bfloat16)
        coded = jnp.concatenate([gates_high, gates_low, fill], axis=1)
        pages_lat, pages_rope = (
            lax.all_gather(latent_pages[0], "dp", axis=0, tiled=True),
            lax.all_gather(rope_pages[0], "dp", axis=0, tiled=True),
        )
        page_count = pages_lat.shape[0]
        table = page_table[0]
        inverse = jnp.sum(
            jnp.where(
                table[:, None] == jnp.arange(page_count)[None, :], jnp.arange(page_count)[:, None], 0
            ),
            axis=0,
        )
        positions = (inverse[:, None] * PAGE + jnp.arange(PAGE)[None, :]).reshape(-1)
        prefix_ok = positions < prefix_lengths[0]
        keys_lat = jnp.concatenate([pages_lat.reshape(-1, LAT), latent_new[0]], axis=0)
        keys_rope = jnp.concatenate([pages_rope.reshape(-1, RD), key_rope[0]], axis=0)
        heads_nope = query_nope[0].reshape(tokens_col, heads_here, HD)
        query_lat = jnp.einsum(
            "thd,hdc->thc", heads_nope, key_up, preferred_element_type=jnp.float32
        ).astype(jnp.bfloat16)
        heads_rope = query_rope[0].reshape(tokens_col, heads_here, RD)
        scale = 1.0 / (HD + RD) ** 0.5
        scores = (
            jnp.einsum("thc,kc->thk", query_lat, keys_lat, preferred_element_type=jnp.float32)
            + jnp.einsum("thr,kr->thk", heads_rope, keys_rope, preferred_element_type=jnp.float32)
        ) * scale
        causal = jnp.arange(tokens_col)[None, :] <= jnp.arange(tokens_col)[:, None]
        allowed = jnp.concatenate(
            [jnp.broadcast_to(prefix_ok[None, :], (tokens_col, prefix_ok.shape[0])), causal], axis=1
        )[:, None, :]
        masked = jnp.where(allowed, scores, NEG)
        peak = jnp.max(masked, axis=-1, keepdims=True)
        expo = jnp.where(allowed, jnp.exp(masked - peak), 0.0)
        total = jnp.sum(expo, axis=-1, keepdims=True)
        probs = expo.astype(jnp.bfloat16)
        attn_latent = (
            jnp.einsum("thk,kc->thc", probs, keys_lat, preferred_element_type=jnp.float32) / total
        ).astype(jnp.bfloat16)
        heads_out = jnp.einsum(
            "thc,hcd->thd", attn_latent, value_up, preferred_element_type=jnp.float32
        ).astype(jnp.bfloat16)
        partial_out = jnp.dot(
            heads_out.reshape(tokens_col, heads_here * HD),
            out_weight,
            preferred_element_type=jnp.float32,
        )
        attended = lax.psum_scatter(
            partial_out.astype(jnp.bfloat16), "dp", scatter_dimension=0, tiled=True
        ).astype(jnp.float32)
        hidden_mine = (
            lax.dynamic_slice_in_dim(residual[0], start, block_rows, 0).astype(jnp.float32) + attended
        )
        normed = norm_rows(hidden_mine, norm_gain)
        sent = jnp.concatenate([normed, coded], axis=1)
        gathered = lax.all_gather(sent, ("expert", "dp"), axis=0, tiled=True)
        everyone = gathered[:, :model]
        mine = lax.axis_index("expert")
        named = (jnp.arange(extra) == mine) | (jnp.arange(extra) == mine + experts_all)
        gate = jnp.sum(
            jnp.where(named[None, :], gathered[:, model:].astype(jnp.float32), 0.0),
            axis=1,
            keepdims=True,
        )
        part = expert_apply(everyone, gate, expert_in, expert_down)
        mixture = lax.psum_scatter(
            part, ("expert", "dp"), scatter_dimension=0, tiled=True
        ).astype(jnp.float32)
    layer_out = (hidden_mine + mixture).astype(jnp.bfloat16)[None]
    return (layer_out, mixture.astype(jnp.bfloat16)[None])


def solution(mesh):
    return jax.shard_map(
        per_device,
        mesh=mesh,
        in_specs=(
            P("expert", None, "dp"),
            P("expert", None, "dp"),
            P("expert", None, None),
            P("expert", None, None),
            P("expert", "dp", None, None),
            P("expert", "dp", None),
            P("expert", None),
            P("expert"),
            P("expert", None, None),
            P("dp", None, None),
            P("dp", None, None),
            P("dp", None),
            P(),
            P("expert", "dp", None, None),
            P("expert", "dp", None),
            P("expert", None, None),
            P("expert", None, None),
        ),
        out_specs=(P("expert", "dp", None), P("expert", "dp", None)),
        check_vma=False,
    )
```

```python
import functools

import jax
import jax.numpy as jnp
from jax import lax
from jax.experimental import pallas as pl
from jax.experimental.pallas import tpu as pltpu
from jax.sharding import PartitionSpec as P

HD = 128
RD = 64
LAT = 512
TOP = 6
PAGE = 64


EPS = 1e-06
NEG = -1e30


def norm_rows(hidden, norm_gain):
    power = jnp.mean(hidden * hidden, axis=-1, keepdims=True)
    return (hidden * lax.rsqrt(power + EPS) * norm_gain).astype(jnp.bfloat16)


def expert_apply(tokens, gate, expert_in, expert_down):
    flat = tokens.reshape(-1, tokens.shape[-1])
    dims = (((1,), (1,)), ((), ()))
    gate_act = lax.dot_general(
        flat, expert_in[0, :, 0, :], dims, preferred_element_type=jnp.float32
    )
    up_act = lax.dot_general(flat, expert_in[0, :, 1, :], dims, preferred_element_type=jnp.float32)
    units = (jax.nn.silu(gate_act) * up_act).astype(jnp.bfloat16)
    part = jnp.dot(units, expert_down[0], preferred_element_type=jnp.float32)
    return (part * gate).astype(jnp.bfloat16)


def moe_kernel(
    sent_ref,
    w_in_ref,
    w_down_ref,
    out_ref,
    tok,
    raw,
    w_in,
    w_down,
    units,
    gate,
    part,
    core_in,
    acc,
    diag_x,
    diag_y,
    from_x,
    from_y,
    z_send,
    z_up,
    z_down,
    relay,
    w_sems,
    g_sends,
    g_recvs,
    sends,
    recvs,
):
    x = lax.axis_index("dp")
    e = lax.axis_index("expert")
    z, y, c = e // 4, (e // 2) % 2, e % 2
    rows, model = out_ref.shape
    half = rows // 2
    width = w_down_ref.shape[0]
    high = z // 2
    low_z = z + high * (3 - 2 * z)
    mid = low_z == 1

    def flip(f):
        return f + high * (3 - 2 * f)

    planes = [z, flip(1 - low_z), flip(3 + 0 * z), flip(2 + 0 * z)]
    other_core = {"expert": e + 1 - 2 * c}
    other_y = {"expert": e + 2 - 4 * y}
    other_x = {"dp": 1 - x}
    above, below = {"expert": e + 4}, {"expert": e - 4}
    pair, middle = {"expert": e + 4 - 8 * (z % 2)}, {"expert": e + 4 * (3 - 2 * z)}
    halves = first, second = pl.ds(0, half), pl.ds(half, half)

    def remote(src, dst, send, recv, to):
        return pltpu.make_async_remote_copy(
            src_ref=src,
            dst_ref=dst,
            send_sem=send,
            recv_sem=recv,
            device_id=to,
            device_id_type=pl.DeviceIdType.MESH,
        )

    def same(ref, kind, p, to):
        return remote(ref, ref, g_sends.at[kind, p], g_recvs.at[kind, p], to)

    def g_up(p, h):
        return same(tok.at[p, y, c, x, halves[h]], h, p, above)

    def g_down(p, h):
        return same(tok.at[p, y, c, x, halves[h]], 2 + h, p, below)

    def g_x(p, i, h):
        return same(tok.at[p, y, c, i, halves[h]], 4 + h, p, other_x)

    def g_y(p, j, h):
        return same(tok.at[p, j, c, x, halves[h]], 6 + h, p, other_y)

    def g_diag_x(p, j):
        return same(tok.at[p, j, c, x, first], 8, p, other_x)

    def g_diag_y(p, i):
        return same(tok.at[p, y, c, i, second], 9, p, other_y)

    def g_core(p, kind, cc):
        j, i = (y, y, 1 - y, 1 - y)[kind], (x, 1 - x, x, 1 - x)[kind]
        return same(tok.at[p, j, cc, i], 10 + kind, p, other_core)

    def own_line(p):
        g_x(p, x, 1).start()
        g_y(p, y, 0).start()
        g_x(p, x, 0).start()
        g_y(p, y, 1).start()
        g_core(p, 0, c).start()

    def along_z(p, h):
        @pl.when(p < z)
        def _():
            g_up(p, h).wait_recv()

            @pl.when(z < 3)
            def _():
                g_up(p, h).start()

        @pl.when(p > z)
        def _():
            g_down(p, h).wait_recv()

            @pl.when(z > 0)
            def _():
                g_down(p, h).start()

    def beside_send(p):
        g_x(p, 1 - x, 1).wait_recv()
        g_diag_y(p, 1 - x).start()
        g_y(p, 1 - y, 0).wait_recv()
        g_diag_x(p, 1 - y).start()

    def beside_rest(p, diag=True):
        if not diag:
            g_x(p, 1 - x, 1).wait_recv()
            g_y(p, 1 - y, 0).wait_recv()
        g_x(p, 1 - x, 0).wait_recv()
        g_core(p, 1, c).start()
        g_y(p, 1 - y, 1).wait_recv()
        g_core(p, 2, c).start()

    def across(p):
        same(tok.at[p, 1 - y, c, 1 - x, first], 8, p, other_x).wait_recv()
        same(tok.at[p, 1 - y, c, 1 - x, second], 9, p, other_y).wait_recv()
        g_core(p, 3, c).start()

    def diag_up(p):
        return same(tok.at[p, 1 - y, c, 1 - x], 14, p, above)

    def diag_down(p):
        return same(tok.at[p, 1 - y, c, 1 - x], 15, p, below)

    def diag_out():
        @pl.when(z == 1)
        def _():
            diag_up(z).start()

        @pl.when(z == 2)
        def _():
            diag_down(z).start()

    def diag_in(p, forward):
        @pl.when(p < z)
        def _():
            diag_up(p).wait_recv()
            if forward:

                @pl.when(mid)
                def _():
                    diag_up(p).start()

        @pl.when(p > z)
        def _():
            diag_down(p).wait_recv()
            if forward:

                @pl.when(mid)
                def _():
                    diag_down(p).start()

        g_core(p, 3, c).start()

    def whole(p):
        for kind in range(4):
            g_core(p, kind, 1 - c).wait_recv()

    def tokens(p):
        return tok[p, :, :, :, :, pl.ds(0, model)].reshape(8 * rows, model)

    def hidden(p, lo, n):
        dims = (((1,), (1,)), ((), ()))
        values = tokens(p)
        gate_act = lax.dot_general(
            values, w_in[0, pl.ds(lo, n)], dims, preferred_element_type=jnp.float32
        )
        up_act = lax.dot_general(
            values, w_in[1, pl.ds(lo, n)], dims, preferred_element_type=jnp.float32
        )
        units[:, pl.ds(lo, n)] = (gate_act / (1.0 + jnp.exp(-gate_act)) * up_act).astype(
            units.dtype
        )

    def gates(p):
        extra = tok.shape[5] - model
        lanes = lax.broadcasted_iota(jnp.int32, (8 * rows, extra), 1)
        named = (lanes == e) | (lanes == e + lax.axis_size("expert"))
        values = tok[p, :, :, :, :, pl.ds(model, extra)].reshape(8 * rows, extra)
        gate[...] = jnp.sum(
            jnp.where(named, values.astype(jnp.float32), 0.0), axis=1, keepdims=True
        )

    def project(p, lo, n):
        value = jnp.dot(units[...], w_down[:, pl.ds(lo, n)], preferred_element_type=jnp.float32)
        part[p, :, :, :, :, pl.ds(lo, n)] = (
            (value * gate[...]).astype(part.dtype).reshape(2, 2, 2, rows, n)
        )

    def compute(p, between):
        steps = [functools.partial(hidden, p, lo, min(256, width - lo)) for lo in range(0, width, 256)]
        steps += [functools.partial(gates, p)]
        steps += [functools.partial(project, p, lo, 256) for lo in range(0, model, 256)]
        for number, step in enumerate(steps):
            step()
            for act in between.get(number, ()):
                act()

    def copy(src, dst, kind, k, to):
        return remote(src, dst, sends.at[kind, k], recvs.at[kind, k], to)

    def core_copy(k):
        return copy(part.at[planes[k], :, 1 - c], core_in.at[k], 0, k, other_core)

    def diag_y_copy(k):
        return copy(acc.at[k, 1 - y, 1 - x, first], diag_y.at[k], 1, k, other_y)

    def diag_x_copy(k):
        return copy(acc.at[k, 1 - y, 1 - x, second], diag_x.at[k], 2, k, other_x)

    def x_copy(k, h):
        return copy(acc.at[k, y, 1 - x, halves[h]], from_x.at[k, halves[h]], 3 + h, k, other_x)

    def y_copy(k, h):
        return copy(acc.at[k, 1 - y, x, halves[h]], from_y.at[k, halves[h]], 5 + h, k, other_y)

    def up_copy(g, h):
        return copy(z_send.at[g, halves[h]], z_up.at[g, halves[h]], 7 + h, g, above)

    def down_copy(g, h):
        return copy(z_send.at[g, halves[h]], z_down.at[g, halves[h]], 9 + h, g, below)

    def wide(value):
        return value.astype(jnp.float32)

    def relay_copy(k, slot, h, to):
        return copy(
            acc.at[k, 1 - y, 1 - x, halves[h]], relay.at[slot, halves[h]], 11 + h, slot, to
        )

    def add_relay(k, slot, h):
        at = halves[h]
        relay_copy(k, slot, h, pair).wait_recv()
        acc[k, 1 - y, 1 - x, at] = (wide(acc[k, 1 - y, 1 - x, at]) + wide(relay[slot, at])).astype(
            acc.dtype
        )

    def add_core(k, j, i):
        acc[k, j, i] = (wide(part[planes[k], j, c, i]) + wide(core_in[k, j, i])).astype(acc.dtype)

    def stage_a(k):
        core_copy(k).wait_recv()
        add_core(k, 1 - y, 1 - x)
        if k == 1:
            relay_copy(1, 0, 0, pair).start()
            relay_copy(1, 0, 1, pair).start()
        if k == 2:
            diag_y_copy(k).start()
            diag_x_copy(k).start()
        if k == 3:

            @pl.when(low_z == 0)
            def _():
                relay_copy(3, 1, 0, pair).start()
                relay_copy(3, 1, 1, pair).start()

        add_core(k, y, 1 - x)
        x_copy(k, 1).start()
        if k % 2 == 1:
            x_copy(k, 0).start()
        add_core(k, 1 - y, x)
        y_copy(k, 0).start()
        if k % 2 == 1:
            y_copy(k, 1).start()
        add_core(k, y, x)
        if k == 3:

            @pl.when(mid)
            def _():
                for h in (0, 1):
                    add_relay(3, 1, h)
                    relay_copy(3, 2, h, middle).start()

    def own_diag():
        for h in (0, 1):
            add_relay(0, 0, h)

            @pl.when(mid)
            def _():
                add_relay(0, 2, h)

            (diag_y_copy, diag_x_copy)[h](0).start()

    def stage_b(k):
        diag_y_copy(k).wait_recv()
        acc[k, y, 1 - x, first] = (wide(acc[k, y, 1 - x, first]) + wide(diag_y[k])).astype(acc.dtype)
        x_copy(k, 0).start()
        diag_x_copy(k).wait_recv()
        acc[k, 1 - y, x, second] = (wide(acc[k, 1 - y, x, second]) + wide(diag_x[k])).astype(
            acc.dtype
        )
        y_copy(k, 1).start()

    def stage_c(k, g, last=False):
        for h in (0, 1):
            at = halves[h]
            x_copy(k, h).wait_recv()
            y_copy(k, h).wait_recv()
            out_ref[at] = wide(acc[k, y, x, at]) + wide(from_x[k, at]) + wide(from_y[k, at])

            @pl.when((g >= z) & (z > 0))
            def _():
                up_copy(g, h).wait_recv()
                out_ref[at] += wide(z_up[g, at])

            @pl.when((g <= z) & (z < 3))
            def _():
                down_copy(g, h).wait_recv()
                out_ref[at] += wide(z_down[g, at])

            if not last:
                z_send[g, at] = out_ref[at].astype(z_send.dtype)

                @pl.when(g > z)
                def _():
                    up_copy(g, h).start()

                @pl.when(g < z)
                def _():
                    down_copy(g, h).start()

    load_in = pltpu.make_async_copy(w_in_ref, raw, w_sems.at[0])

    def untangle(lo, n):
        for at in range(lo, lo + n, 64):
            pairs = raw[pl.ds(at, 64)].reshape(128, model)
            row = lax.broadcasted_iota(jnp.int32, (128, 128), 0)
            column = lax.broadcasted_iota(jnp.int32, (128, 128), 1)
            order = jnp.where(column == 2 * (row % 64) + row // 64, 1.0, 0.0).astype(raw.dtype)
            sorted_rows = jnp.dot(order, pairs, preferred_element_type=jnp.float32).astype(raw.dtype)
            w_in[0, pl.ds(at, 64)] = sorted_rows[:64]
            w_in[1, pl.ds(at, 64)] = sorted_rows[64:]

    load_down = pltpu.make_async_copy(w_down_ref, w_down, w_sems.at[1])
    barrier = pltpu.get_barrier_semaphore()
    for to in (other_core, other_x, other_y):
        pl.semaphore_signal(barrier, inc=1, device_id=to, device_id_type=pl.DeviceIdType.MESH)

    @pl.when(z > 0)
    def _():
        pl.semaphore_signal(barrier, inc=1, device_id=below, device_id_type=pl.DeviceIdType.MESH)

    @pl.when(z < 3)
    def _():
        pl.semaphore_signal(barrier, inc=1, device_id=above, device_id_type=pl.DeviceIdType.MESH)

    load_own = pltpu.make_async_copy(sent_ref, tok.at[z, y, c, x], w_sems.at[2])
    load_own.start()
    load_in.start()
    load_down.start()
    load_own.wait()
    pl.semaphore_wait(barrier, 4 + ((z + 1) // 2) % 2)

    for h in (0, 1):

        @pl.when(z < 3)
        def _():
            g_up(z, h).start()

        @pl.when(z > 0)
        def _():
            g_down(z, h).start()

    def do(f, *args):
        return functools.partial(f, *args)

    def at_mid(*acts):
        @pl.when(mid)
        def _():
            for act in acts:
                act()

    def at_end(*acts):
        @pl.when(low_z == 0)
        def _():
            for act in acts:
                act()

    def start_core(k):
        core_copy(k).start()

    own_line(z)
    load_in.wait()
    untangle(0, 256)
    along_z(planes[1], 0)
    at_mid(do(along_z, planes[3], 0))
    beside_send(planes[0])
    along_z(planes[1], 1)
    at_mid(do(along_z, planes[3], 1))
    own_line(planes[1])
    beside_rest(planes[0])
    untangle(256, 256)
    across(planes[0])
    at_mid(do(along_z, planes[2], 0), do(diag_out), do(along_z, planes[2], 1))
    beside_send(planes[1])
    at_mid(do(own_line, planes[2]))
    untangle(512, 192)
    load_down.wait()
    whole(planes[0])
    compute(
        planes[0],
        {
            2: [do(at_end, do(along_z, planes[3], 0), do(along_z, planes[3], 1))],
            5: [do(beside_rest, planes[1])],
            9: [
                do(at_end, do(along_z, planes[2], 0), do(along_z, planes[2], 1)),
                do(at_end, do(own_line, planes[2])),
            ],
        },
    )
    start_core(0)
    across(planes[1])
    at_mid(do(diag_in, planes[3], True))
    whole(planes[1])
    compute(
        planes[1],
        {
            2: [do(beside_send, planes[2]), do(own_line, planes[3])],
            7: [do(beside_rest, planes[2])],
        },
    )
    start_core(1)
    across(planes[2])
    stage_a(0)
    whole(planes[2])
    compute(
        planes[2],
        {
            2: [do(stage_a, 1)],
            6: [do(at_end, do(diag_in, planes[3], False))],
            9: [do(beside_rest, planes[3], False)],
        },
    )
    start_core(2)
    whole(planes[3])
    compute(
        planes[3],
        {
            2: [do(stage_a, 2)],
            7: [do(at_end, do(stage_c, 1, planes[1]))],
            11: [do(stage_b, 2)],
        },
    )
    start_core(3)
    at_end(own_diag)
    stage_a(3)
    stage_c(2, planes[2])
    at_mid(own_diag, do(stage_c, 1, planes[1]), do(stage_c, 3, planes[3]))
    stage_b(0)
    at_end(do(stage_c, 3, planes[3]))
    stage_c(0, planes[0], True)

    for k in range(4):
        p = planes[k]
        core_copy(k).wait_send()
        if k % 2 == 0:
            diag_y_copy(k).wait_send()
            diag_x_copy(k).wait_send()
        if k < 3:
            g_diag_y(p, 1 - x).wait_send()
            g_diag_x(p, 1 - y).wait_send()
        for kind in range(4):
            g_core(p, kind, c).wait_send()
        if k == 0:

            @pl.when(z == 1)
            def _():
                diag_up(p).wait_send()

            @pl.when(z == 2)
            def _():
                diag_down(p).wait_send()

        if k == 1:
            relay_copy(1, 0, 0, pair).wait_send()
            relay_copy(1, 0, 1, pair).wait_send()
        if k == 3:

            @pl.when(mid & (p < z))
            def _():
                diag_up(p).wait_send()

            @pl.when(mid & (p > z))
            def _():
                diag_down(p).wait_send()

            @pl.when(mid)
            def _():
                relay_copy(3, 2, 0, middle).wait_send()
                relay_copy(3, 2, 1, middle).wait_send()

            @pl.when(low_z == 0)
            def _():
                relay_copy(3, 1, 0, pair).wait_send()
                relay_copy(3, 1, 1, pair).wait_send()

        for h in (0, 1):
            x_copy(k, h).wait_send()
            y_copy(k, h).wait_send()
            g_x(p, x, h).wait_send()
            g_y(p, y, h).wait_send()

            @pl.when((p <= z) & (z < 3))
            def _():
                g_up(p, h).wait_send()

            @pl.when((p >= z) & (z > 0))
            def _():
                g_down(p, h).wait_send()

            if k > 0:

                @pl.when(p > z)
                def _():
                    up_copy(p, h).wait_send()

                @pl.when(p < z)
                def _():
                    down_copy(p, h).wait_send()


def mixture_kernel(sent, w_in, w_down):
    rows, full = sent.shape
    width, model = w_down.shape
    kind = sent.dtype
    line = pltpu.VMEM((4, rows, model), kind)
    halves = pltpu.VMEM((4, rows // 2, model), kind)
    return pl.pallas_call(
        moe_kernel,
        out_shape=jax.ShapeDtypeStruct((rows, model), jnp.float32),
        in_specs=[
            pl.BlockSpec(memory_space=pl.ANY),
            pl.BlockSpec(memory_space=pl.ANY),
            pl.BlockSpec(memory_space=pl.ANY),
        ],
        out_specs=pl.BlockSpec(memory_space=pltpu.VMEM),
        scratch_shapes=[
            pltpu.VMEM((4, 2, 2, 2, rows, full), kind),
            pltpu.VMEM((width, 2, model), kind),
            pltpu.VMEM((2, width, model), kind),
            pltpu.VMEM((width, model), kind),
            pltpu.VMEM((8 * rows, width), kind),
            pltpu.VMEM((8 * rows, 1), jnp.float32),
            pltpu.VMEM((4, 2, 2, 2, rows, model), kind),
            pltpu.VMEM((4, 2, 2, rows, model), kind),
            pltpu.VMEM((4, 2, 2, rows, model), kind),
            halves,
            halves,
            line,
            line,
            line,
            line,
            line,
            pltpu.VMEM((3, rows, model), kind),
            pltpu.SemaphoreType.DMA((3,)),
            pltpu.SemaphoreType.DMA((16, 4)),
            pltpu.SemaphoreType.DMA((16, 4)),
            pltpu.SemaphoreType.DMA((13, 4)),
            pltpu.SemaphoreType.DMA((13, 4)),
        ],
        compiler_params=pltpu.CompilerParams(
            collective_id=0, has_side_effects=True, vmem_limit_bytes=52 * 2**20
        ),
    )(sent, w_in, w_down)


def attend_kernel(
    table_ref,
    length_ref,
    nope_in,
    rope_in,
    new_in,
    new_rope_ref,
    pages_ref,
    pages_rope_ref,
    residual_ref,
    gain_ref,
    ids_ref,
    weights_ref,
    key_up_ref,
    value_up_ref,
    out_weight_ref,
    sent_ref,
    hidden_ref,
    keys,
    keys_rope,
    key_up,
    value_up,
    out_weight,
    residual,
    query_lat,
    query_rope,
    scores,
    far_scores,
    near,
    near_peak,
    near_total,
    coded,
    nope_ref,
    rope_ref,
    heads_out,
    partial,
    arrived,
    loads,
    sends,
    recvs,
):
    x = lax.axis_index("dp")
    other_x = {"dp": 1 - x}
    heads = key_up.shape[0]
    tokens = nope_in.shape[0]
    held = pages_ref.shape[0]
    rows, model = hidden_ref.shape
    chunks, piece = partial.shape[0], partial.shape[2]
    span = 2 * held
    scale = 1.0 / (HD + RD) ** 0.5
    nt = (((1,), (1,)), ((), ()))

    def remote(src, dst, k):
        return pltpu.make_async_remote_copy(
            src_ref=src,
            dst_ref=dst,
            send_sem=sends.at[k],
            recv_sem=recvs.at[k],
            device_id=other_x,
            device_id_type=pl.DeviceIdType.MESH,
        )

    mine = [
        pltpu.make_async_copy(key_up_ref, key_up, loads.at[0]),
        pltpu.make_async_copy(pages_ref, keys.at[pl.ds(0, held)], loads.at[1]),
        pltpu.make_async_copy(value_up_ref, value_up, loads.at[2]),
        pltpu.make_async_copy(out_weight_ref, out_weight, loads.at[3]),
        pltpu.make_async_copy(residual_ref.at[pl.ds(x * rows, rows)], residual, loads.at[4]),
        pltpu.make_async_copy(nope_in, nope_ref, loads.at[5]),
        pltpu.make_async_copy(rope_in, rope_ref, loads.at[6]),
        pltpu.make_async_copy(new_in, keys.at[pl.ds(held, tokens)], loads.at[7]),
    ]
    far_keys = remote(pages_ref, keys.at[pl.ds(held + tokens, held)], 0)
    far_rope = remote(pages_rope_ref, keys_rope.at[pl.ds(held, held)], 1)
    barrier = pltpu.get_barrier_semaphore()
    pl.semaphore_signal(barrier, inc=1, device_id=other_x, device_id_type=pl.DeviceIdType.MESH)
    for k in (5, 0, 6, 1, 7, 2, 3, 4):
        mine[k].start()
    pl.semaphore_wait(barrier, 1)
    far_keys.start()
    far_rope.start()
    keys_rope[pl.ds(0, held)] = pages_rope_ref[...]

    def bias(start):
        place = lax.broadcasted_iota(jnp.int32, (8, held), 1) + start
        slot, offset = place // PAGE, place % PAGE
        seen = jnp.zeros((8, held), jnp.int32)
        for j in range(span // PAGE):
            seen += jnp.where(
                (slot == table_ref[0, j]) & (offset + j * PAGE < length_ref[0]), 1, 0
            )
        return jnp.where(seen > 0, 0.0, NEG)[0:1]

    mine[0].wait()
    mine[5].wait()
    mine[6].wait()
    for h in range(heads):
        query_lat[pl.ds(h * tokens, tokens)] = jnp.dot(
            nope_ref[:, pl.ds(h * HD, HD)], key_up[h], preferred_element_type=jnp.float32
        ).astype(query_lat.dtype)
        query_rope[pl.ds(h * tokens, tokens)] = rope_ref[:, pl.ds(h * RD, RD)]
    mine[1].wait()
    mine[7].wait()

    def against(lo, n, rope_keys, dims):
        return (
            lax.dot_general(
                query_lat[...], keys[pl.ds(lo, n)], nt, preferred_element_type=jnp.float32
            )
            + lax.dot_general(query_rope[...], rope_keys, dims, preferred_element_type=jnp.float32)
        ) * scale

    scores[:, pl.ds(0, held)] = against(0, held, keys_rope[pl.ds(0, held)], nt) + bias(x * held)
    fresh = against(held, tokens, new_rope_ref[...], (((1,), (0,)), ((), ())))
    seen = lax.broadcasted_iota(jnp.int32, (tokens, tokens), 1) <= lax.broadcasted_iota(
        jnp.int32, (tokens, tokens), 0
    )
    causal = jnp.where(seen, 0.0, NEG)
    scores[:, pl.ds(held, tokens)] = (
        fresh.reshape(heads, tokens, tokens) + causal[None]
    ).reshape(heads * tokens, tokens)
    for h in range(heads):
        at = pl.ds(h * tokens, tokens)
        masked = scores[at]
        peak = jnp.max(masked, axis=1, keepdims=True)
        expo = jnp.exp(masked - peak)
        near_peak[at] = peak
        near_total[at] = jnp.sum(expo, axis=1, keepdims=True)
        near[at] = jnp.dot(
            expo.astype(keys.dtype),
            keys[pl.ds(0, held + tokens)],
            preferred_element_type=jnp.float32,
        )
    experts = lax.axis_size("expert")
    number = lax.broadcasted_iota(jnp.int32, (experts, tokens), 0)
    picked = jnp.zeros((experts, tokens), jnp.float32)
    for k in range(TOP):
        picked += jnp.where(ids_ref[k] == number, weights_ref[k], 0.0)
    high = picked.astype(sent_ref.dtype).astype(jnp.float32)
    fill = jnp.zeros((coded.shape[1] - 2 * experts, tokens), jnp.float32)
    coded[...] = jnp.concatenate([high, picked - high, fill], axis=0).T
    sent_ref[:, pl.ds(model, coded.shape[1])] = coded[pl.ds(x * rows, rows)].astype(sent_ref.dtype)
    mine[2].wait()
    far_keys.wait_recv()
    far_rope.wait_recv()
    far_scores[...] = against(
        held + tokens, held, keys_rope[pl.ds(held, held)], nt
    ) + bias((1 - x) * held)
    for h in range(heads):
        at = pl.ds(h * tokens, tokens)
        masked = far_scores[at]
        peak = jnp.maximum(near_peak[at], jnp.max(masked, axis=1, keepdims=True))
        expo = jnp.exp(masked - peak)
        shrink = jnp.exp(near_peak[at] - peak)
        total = near_total[at] * shrink + jnp.sum(expo, axis=1, keepdims=True)
        attn = near[at] * shrink + jnp.dot(
            expo.astype(keys.dtype),
            keys[pl.ds(held + tokens, held)],
            preferred_element_type=jnp.float32,
        )
        heads_out[:, pl.ds(h * HD, HD)] = jnp.dot(
            (attn / total).astype(keys.dtype), value_up[h], preferred_element_type=jnp.float32
        ).astype(heads_out.dtype)
    mine[3].wait()

    def exchange(n):
        return remote(partial.at[n, pl.ds((1 - x) * rows, rows)], arrived.at[n], 2 + n)

    for n in range(chunks):
        partial[n] = jnp.dot(
            heads_out[...],
            out_weight[:, pl.ds(n * piece, piece)],
            preferred_element_type=jnp.float32,
        ).astype(partial.dtype)
        exchange(n).start()
    mine[4].wait()
    power = jnp.zeros((rows, 1), jnp.float32)
    for n in range(chunks):
        exchange(n).wait_recv()
        at = pl.ds(n * piece, piece)
        hidden = (
            residual[:, at].astype(jnp.float32)
            + partial[n, pl.ds(x * rows, rows)].astype(jnp.float32)
            + arrived[n].astype(jnp.float32)
        )
        hidden_ref[:, at] = hidden
        power += jnp.sum(hidden * hidden, axis=1, keepdims=True)
    factor = lax.rsqrt(power / model + EPS)
    for n in range(chunks):
        at = pl.ds(n * piece, piece)
        sent_ref[:, at] = (hidden_ref[:, at] * factor * gain_ref[:, at]).astype(sent_ref.dtype)
    far_keys.wait_send()
    far_rope.wait_send()
    for n in range(chunks):
        exchange(n).wait_send()


def attend(
    table,
    length,
    nope,
    rope,
    new,
    new_rope,
    pages,
    pages_rope,
    residual,
    gain,
    ids,
    weights,
    key_up,
    value_up,
    out_weight,
):
    kind = nope.dtype
    heads = key_up.shape[0]
    tokens, model = residual.shape
    rows = tokens // 2
    held = pages.shape[0]
    chunks = 4
    vmem = pl.BlockSpec(memory_space=pltpu.VMEM)
    smem = pl.BlockSpec(memory_space=pltpu.SMEM)
    far = pl.BlockSpec(memory_space=pl.ANY)
    return pl.pallas_call(
        attend_kernel,
        out_shape=(
            jax.ShapeDtypeStruct((rows, model + 128), kind),
            jax.ShapeDtypeStruct((rows, model), jnp.float32),
        ),
        in_specs=[smem, smem, far, far, far, vmem, far, vmem, far, vmem, vmem, vmem, far, far, far],
        out_specs=(vmem, vmem),
        scratch_shapes=[
            pltpu.VMEM((2 * held + tokens, LAT), kind),
            pltpu.VMEM((2 * held, RD), kind),
            pltpu.VMEM(key_up.shape, kind),
            pltpu.VMEM(value_up.shape, kind),
            pltpu.VMEM(out_weight.shape, kind),
            pltpu.VMEM((rows, model), kind),
            pltpu.VMEM((heads * tokens, LAT), kind),
            pltpu.VMEM((heads * tokens, RD), kind),
            pltpu.VMEM((heads * tokens, held + tokens), jnp.float32),
            pltpu.VMEM((heads * tokens, held), jnp.float32),
            pltpu.VMEM((heads * tokens, LAT), jnp.float32),
            pltpu.VMEM((heads * tokens, 1), jnp.float32),
            pltpu.VMEM((heads * tokens, 1), jnp.float32),
            pltpu.VMEM((tokens, 128), jnp.float32),
            pltpu.VMEM(nope.shape, kind),
            pltpu.VMEM(rope.shape, kind),
            pltpu.VMEM((tokens, heads * HD), kind),
            pltpu.VMEM((chunks, tokens, model // chunks), kind),
            pltpu.VMEM((chunks, rows, model // chunks), kind),
            pltpu.SemaphoreType.DMA((8,)),
            pltpu.SemaphoreType.DMA((2 + chunks,)),
            pltpu.SemaphoreType.DMA((2 + chunks,)),
        ],
        compiler_params=pltpu.CompilerParams(
            collective_id=1, has_side_effects=True, vmem_limit_bytes=62 * 2**20
        ),
    )(
        table,
        length,
        nope,
        rope,
        new,
        new_rope,
        pages,
        pages_rope,
        residual,
        gain,
        ids,
        weights,
        key_up,
        value_up,
        out_weight,
    )


def per_device(
    query_nope,
    query_rope,
    latent_new,
    key_rope,
    latent_pages,
    rope_pages,
    page_table,
    prefix_lengths,
    residual,
    key_up,
    value_up,
    out_weight,
    norm_gain,
    expert_in,
    expert_down,
    expert_ids,
    expert_weights,
):
    groups = lax.axis_size("dp")
    experts_all = lax.axis_size("expert") * expert_in.shape[0]
    tokens_col = query_nope.shape[1]
    block_rows = tokens_col // groups
    heads_here = key_up.shape[0]
    fits = groups == 2 and lax.axis_size("expert") == 16
    start = lax.axis_index("dp") * block_rows
    model = residual.shape[2]
    if fits:
        sent, hidden_mine = attend(
            page_table,
            prefix_lengths,
            query_nope[0],
            query_rope[0],
            latent_new[0],
            jnp.transpose(key_rope[0]),
            latent_pages[0].reshape(-1, LAT),
            rope_pages[0].reshape(-1, RD),
            residual[0],
            norm_gain[None],
            jnp.transpose(expert_ids, (2, 0, 1)),
            jnp.transpose(expert_weights, (2, 0, 1)),
            key_up,
            value_up,
            out_weight,
        )
        mixture = mixture_kernel(sent, expert_in[0], expert_down[0])
    else:
        ids_mine = lax.dynamic_slice_in_dim(expert_ids[0], start, block_rows, 0)
        weights_mine = lax.dynamic_slice_in_dim(expert_weights[0], start, block_rows, 0)
        gates = jnp.sum(
            jnp.where(
                ids_mine[:, :, None] == jnp.arange(experts_all)[None, None, :],
                weights_mine[:, :, None],
                0.0,
            ),
            axis=1,
        )
        gates_high = gates.astype(jnp.bfloat16)
        gates_low = (gates - gates_high.astype(jnp.float32)).astype(jnp.bfloat16)
        extra = -(-2 * experts_all // 128) * 128
        fill = jnp.zeros((block_rows, extra - 2 * experts_all), jnp.bfloat16)
        coded = jnp.concatenate([gates_high, gates_low, fill], axis=1)
        pages_lat, pages_rope = (
            lax.all_gather(latent_pages[0], "dp", axis=0, tiled=True),
            lax.all_gather(rope_pages[0], "dp", axis=0, tiled=True),
        )
        page_count = pages_lat.shape[0]
        table = page_table[0]
        inverse = jnp.sum(
            jnp.where(
                table[:, None] == jnp.arange(page_count)[None, :], jnp.arange(page_count)[:, None], 0
            ),
            axis=0,
        )
        positions = (inverse[:, None] * PAGE + jnp.arange(PAGE)[None, :]).reshape(-1)
        prefix_ok = positions < prefix_lengths[0]
        keys_lat = jnp.concatenate([pages_lat.reshape(-1, LAT), latent_new[0]], axis=0)
        keys_rope = jnp.concatenate([pages_rope.reshape(-1, RD), key_rope[0]], axis=0)
        heads_nope = query_nope[0].reshape(tokens_col, heads_here, HD)
        query_lat = jnp.einsum(
            "thd,hdc->thc", heads_nope, key_up, preferred_element_type=jnp.float32
        ).astype(jnp.bfloat16)
        heads_rope = query_rope[0].reshape(tokens_col, heads_here, RD)
        scale = 1.0 / (HD + RD) ** 0.5
        scores = (
            jnp.einsum("thc,kc->thk", query_lat, keys_lat, preferred_element_type=jnp.float32)
            + jnp.einsum("thr,kr->thk", heads_rope, keys_rope, preferred_element_type=jnp.float32)
        ) * scale
        causal = jnp.arange(tokens_col)[None, :] <= jnp.arange(tokens_col)[:, None]
        allowed = jnp.concatenate(
            [jnp.broadcast_to(prefix_ok[None, :], (tokens_col, prefix_ok.shape[0])), causal], axis=1
        )[:, None, :]
        masked = jnp.where(allowed, scores, NEG)
        peak = jnp.max(masked, axis=-1, keepdims=True)
        expo = jnp.where(allowed, jnp.exp(masked - peak), 0.0)
        total = jnp.sum(expo, axis=-1, keepdims=True)
        probs = expo.astype(jnp.bfloat16)
        attn_latent = (
            jnp.einsum("thk,kc->thc", probs, keys_lat, preferred_element_type=jnp.float32) / total
        ).astype(jnp.bfloat16)
        heads_out = jnp.einsum(
            "thc,hcd->thd", attn_latent, value_up, preferred_element_type=jnp.float32
        ).astype(jnp.bfloat16)
        partial_out = jnp.dot(
            heads_out.reshape(tokens_col, heads_here * HD),
            out_weight,
            preferred_element_type=jnp.float32,
        )
        attended = lax.psum_scatter(
            partial_out.astype(jnp.bfloat16), "dp", scatter_dimension=0, tiled=True
        ).astype(jnp.float32)
        hidden_mine = (
            lax.dynamic_slice_in_dim(residual[0], start, block_rows, 0).astype(jnp.float32) + attended
        )
        normed = norm_rows(hidden_mine, norm_gain)
        sent = jnp.concatenate([normed, coded], axis=1)
        gathered = lax.all_gather(sent, ("expert", "dp"), axis=0, tiled=True)
        everyone = gathered[:, :model]
        mine = lax.axis_index("expert")
        named = (jnp.arange(extra) == mine) | (jnp.arange(extra) == mine + experts_all)
        gate = jnp.sum(
            jnp.where(named[None, :], gathered[:, model:].astype(jnp.float32), 0.0),
            axis=1,
            keepdims=True,
        )
        part = expert_apply(everyone, gate, expert_in, expert_down)
        mixture = lax.psum_scatter(
            part, ("expert", "dp"), scatter_dimension=0, tiled=True
        ).astype(jnp.float32)
    layer_out = (hidden_mine + mixture).astype(jnp.bfloat16)[None]
    return (layer_out, mixture.astype(jnp.bfloat16)[None])


def solution(mesh):
    return jax.shard_map(
        per_device,
        mesh=mesh,
        in_specs=(
            P("expert", None, "dp"),
            P("expert", None, "dp"),
            P("expert", None, None),
            P("expert", None, None),
            P("expert", "dp", None, None),
            P("expert", "dp", None),
            P("expert", None),
            P("expert"),
            P("expert", None, None),
            P("dp", None, None),
            P("dp", None, None),
            P("dp", None),
            P(),
            P("expert", "dp", None, None),
            P("expert", "dp", None),
            P("expert", None, None),
            P("expert", None, None),
        ),
        out_specs=(P("expert", "dp", None), P("expert", "dp", None)),
        check_vma=False,
    )
```
